32 devices in a mesh: seq: 16 (over z, y, core), dp: 2 (over x).
Axes of the slice: x: 2, y: 2, z: 4, core: 2. Of those that a mesh axis runs over, the one named last changes fastest.
Arguments:
- layer_input: bfloat16 [2, 2048, 4096], P('dp', 'seq'), may hold values from -0.3125 to 0.3125
- scan_input: bfloat16 [2, 2048, 2048], P('dp', 'seq'), may hold values from -6 to 6
- readout: bfloat16 [2, 2048, 64], P('dp', 'seq'), may hold values from -6 to 6
- log_decay: float32 [2, 2048, 32], P('dp', 'seq'), may hold values from -1 to 0
- output_cotangent: bfloat16 [2, 2048, 2048], P('dp', 'seq'), may hold values from -0.0078125 to 0.0078125
- write_weight: float32 [4096, 64], P('dp'), may hold values from -6 to 6
- first_moment: float32 [4096, 64], P('dp'), may hold values from -6 to 6
- second_moment: float32 [4096, 64], P('dp'), may hold values from 1 to 25
Outputs:
- decay_gradient: float32 [2, 2048, 32], P('dp', 'seq')
- new_weight: float32 [4096, 64], P('dp')
- new_first: float32 [4096, 64], P('dp')
- new_second: float32 [4096, 64], P('dp')
The draws below stay inside these ranges and needn't reach their ends.
All inputs are finite; a program needn't handle non-finite values.
Results may differ from the reference program's by a relative error of at most 0.0039.
Values may be sent and summed in bfloat16 or wider, within the bound.
A program may use at most 64 MiB of HBM per device.

```python
import math
import jax
import jax.numpy as jnp
from jax import lax

D = 4096
HALF_HEAD_COUNT = 32
HEAD_DIM = 64
STATE = 64
TOK_DEV = 128
SEQUENCE_LENGTH = 2048
BATCH_SEQUENCES = 2


def draw_log_decay(key, part):
    random_keys = jax.random.split(key, 7)
    fast_share = 0.5
    fast_heads = jax.random.uniform(random_keys[0], (HALF_HEAD_COUNT,)) < fast_share
    fast_rate = jnp.exp(jax.random.uniform(random_keys[1], (HALF_HEAD_COUNT,), minval=jnp.log(1.0 / 50.0), maxval=jnp.log(1.0 / 30.0)))
    slow_rate = jnp.exp(jax.random.uniform(random_keys[2], (HALF_HEAD_COUNT,), minval=jnp.log(0.05), maxval=jnp.log(0.5))) / SEQUENCE_LENGTH
    decay_rate = jnp.where(fast_heads, fast_rate, slow_rate)
    roughness = jnp.exp(jax.random.uniform(random_keys[3], (BATCH_SEQUENCES, SEQUENCE_LENGTH, HALF_HEAD_COUNT), minval=-0.7, maxval=0.7))
    block_factor = jnp.exp(jax.random.uniform(random_keys[4], (BATCH_SEQUENCES, SEQUENCE_LENGTH // TOK_DEV, 1, HALF_HEAD_COUNT), minval=-0.7, maxval=0.7))
    block_factor = jnp.broadcast_to(block_factor, (BATCH_SEQUENCES, SEQUENCE_LENGTH // TOK_DEV, TOK_DEV, HALF_HEAD_COUNT)).reshape(BATCH_SEQUENCES, SEQUENCE_LENGTH, HALF_HEAD_COUNT)
    stable_result = -decay_rate[None, None, :] * roughness * block_factor
    spike_location = jax.random.randint(random_keys[5], (BATCH_SEQUENCES, 2, 1), 0, SEQUENCE_LENGTH)
    token_positions = lax.broadcasted_iota(jnp.int32, (BATCH_SEQUENCES, 2, SEQUENCE_LENGTH), 2)
    spike_found = jnp.any(token_positions == spike_location, axis=1)
    spike_loss = jax.random.uniform(random_keys[6], (BATCH_SEQUENCES, SEQUENCE_LENGTH, HALF_HEAD_COUNT), minval=0.2, maxval=0.5)
    final_output = stable_result + jnp.where(spike_found[:, :, None], jnp.log(1.0 - spike_loss), 0.0)
    return final_output.astype(jnp.float32)


def with_spikes(result, own_key, source, target, shards_of, factor):
    owner, partner = [(jnp.arange(result.shape[position]) // (result.shape[position] // shards_of)).reshape([-1 if axis == position else 1 for axis in range(result.ndim)]) for position in (source, target)]
    chosen = jax.random.permutation(own_key, shards_of)[partner]
    strong = (owner == chosen) | (owner == (partner + shards_of // 2) % shards_of)
    return jnp.where(strong, factor * result, result)


def levels(key, extent, cuts, least, largest):
    def one(dim, shards_of):
        heights = jax.random.uniform(jax.random.fold_in(jax.random.fold_in(key, 6), dim), (shards_of,), jnp.float32, least / len(cuts), largest / len(cuts))
        return jnp.repeat(jnp.exp(heights), extent[dim] // shards_of).reshape((-1,) + (1,) * (len(extent) - dim - 1))

    gain = one(*cuts[0])
    for cut in cuts[1:]:
        gain = gain * one(*cut)
    return gain


def centred(rng, extent, deviation, reach, pieces=(), kind=jnp.bfloat16):
    values = deviation * jax.random.normal(rng, extent, jnp.float32)
    if pieces:
        values = values * levels(rng, extent, pieces, -0.22, 0.18)
    return jnp.clip(values, -reach, reach).astype(kind)


def bell_draw_with(own_key, dims, scale, most, cuts, heavy, dtype=jnp.bfloat16):
    values = scale * jax.random.normal(own_key, dims, jnp.float32)
    if cuts:
        values = values * levels(own_key, dims, cuts, -0.22, 0.18)
    return jnp.clip(with_spikes(values, jax.random.fold_in(own_key, 3), *heavy), -most, most).astype(dtype)


def setup_inputs(seed: int = 0) -> dict:
    keys = jax.random.split(jax.random.key(seed), 9)
    layer_input = bell_draw_with(keys[0], (BATCH_SEQUENCES, SEQUENCE_LENGTH, D), 0.015625, 0.3125, ((0, 2), (1, 16)), (0, 2, 2, 2.0))
    scan_input = centred(keys[1], (BATCH_SEQUENCES, SEQUENCE_LENGTH, HALF_HEAD_COUNT * HEAD_DIM), 1.0, 6.0, ((0, 2), (1, 16)))
    readout = centred(keys[2], (BATCH_SEQUENCES, SEQUENCE_LENGTH, STATE), 1.0, 6.0, ((0, 2), (1, 16)))
    log_decay = draw_log_decay(jax.random.fold_in(keys[8], 71), 0)
    output_cotangent = centred(keys[4], (BATCH_SEQUENCES, SEQUENCE_LENGTH, HALF_HEAD_COUNT * HEAD_DIM), (1.0 / SEQUENCE_LENGTH), 0.0078125, ((0, 2), (1, 16)))
    write_weight = centred(keys[5], (D, STATE), 1.0, 6.0, ((0, 2),), jnp.float32)
    first_moment = centred(keys[6], (D, STATE), 1.0, 6.0, ((0, 2),), jnp.float32)
    second_moment = jnp.clip(jnp.exp(math.log(25.0) - 3.218876 * jax.random.uniform(keys[7], (D, STATE), jnp.float32) ** levels(keys[7], (D, STATE), ((0, 2),), -0.2, 0.2)), 1.0, 25.0)
    return {"layer_input": layer_input, "scan_input": scan_input, "readout": readout, "log_decay": log_decay, "output_cotangent": output_cotangent, "write_weight": write_weight, "first_moment": first_moment, "second_moment": second_moment}


beta_one = 0.9
beta_two = 0.999
adam_count = 10.0
learn_rate = 0.01
weight_decay = 0.1
epsilon = 1e-08
highest = lax.Precision.HIGHEST

def block_setup(input_rows, scan_rows, read_rows, decay_rows, back_rows, weight_half):
    length = input_rows.shape[0]
    write_half = jnp.dot(input_rows, weight_half, preferred_element_type=jnp.float32).astype(jnp.bfloat16)
    write_float = lax.optimization_barrier(write_half).astype(jnp.float32)
    running = jnp.cumsum(decay_rows, axis=0)
    overall = running[-1]
    to_end = jnp.exp(overall[None, :] - running)
    from_start = jnp.exp(running)
    scan_heads = scan_rows.astype(jnp.float32).reshape(length, HALF_HEAD_COUNT, HEAD_DIM)
    back_heads = back_rows.astype(jnp.float32).reshape(length, HALF_HEAD_COUNT, HEAD_DIM)
    read_float = read_rows.astype(jnp.float32)
    return (running, overall, to_end, from_start, scan_heads, back_heads, write_float, read_float)

def block_states(input_rows, scan_rows, read_rows, decay_rows, back_rows, weight_half):
    running, overall, to_end, from_start, scan_heads, back_heads, write_float, read_float = block_setup(input_rows, scan_rows, read_rows, decay_rows, back_rows, weight_half)
    state_local = jnp.einsum('shp,sn->hpn', scan_heads * to_end[:, :, None], write_float, precision=highest)
    reverse_local = jnp.einsum('shp,sn->hpn', back_heads * from_start[:, :, None], read_float, precision=highest)
    return (jnp.exp(overall), state_local, reverse_local)

def block_gradients(input_rows, scan_rows, read_rows, decay_rows, back_rows, weight_half, state_before, grad_after):
    length = input_rows.shape[0]
    running, overall, to_end, from_start, scan_heads, back_heads, write_float, read_float = block_setup(input_rows, scan_rows, read_rows, decay_rows, back_rows, weight_half)
    term_one = jnp.exp(overall) * lax.optimization_barrier(jnp.sum(grad_after * state_before, axis=(1, 2)))
    grad_write = jnp.einsum('hpn,sn->shp', grad_after, write_float, precision=highest)
    second_rows = to_end * lax.optimization_barrier(jnp.sum(scan_heads * grad_write, axis=2))
    term_two = jnp.cumsum(second_rows, axis=0) - second_rows
    state_read = jnp.einsum('hpn,sn->shp', state_before, read_float, precision=highest)
    third_rows = from_start * lax.optimization_barrier(jnp.sum(back_heads * state_read, axis=2))
    term_three = jnp.flip(jnp.cumsum(jnp.flip(third_rows, 0), axis=0), 0)
    crossed = jnp.einsum('thp,shp->hts', scan_heads, back_heads, precision=highest)
    heads_running = running.T
    spread = heads_running[:, None, :] - heads_running[:, :, None]
    row_index = lax.broadcasted_iota(jnp.int32, (length, length), 0)
    col_index = lax.broadcasted_iota(jnp.int32, (length, length), 1)
    kernel_mat = jnp.where((row_index <= col_index)[None], jnp.exp(jnp.minimum(spread, 0.0)), 0.0) * crossed
    write_read = jnp.dot(write_float, read_float.T, precision=highest)
    pairing = jnp.where((row_index < col_index)[None], kernel_mat * write_read[None], 0.0)
    balance = (lax.optimization_barrier(jnp.sum(pairing, axis=2)) - lax.optimization_barrier(jnp.sum(pairing, axis=1))).T
    term_four = jnp.cumsum(balance, axis=0) - balance
    decay_grad = term_one[None, :] + term_two + term_three + term_four
    scaled_scan = (scan_heads * to_end[:, :, None]).reshape(length, HALF_HEAD_COUNT * HEAD_DIM)
    write_grad = jnp.dot(scaled_scan, grad_after.reshape(HALF_HEAD_COUNT * HEAD_DIM, STATE), precision=highest)
    write_grad = write_grad + jnp.dot(lax.optimization_barrier(jnp.sum(kernel_mat, axis=0)), read_float, precision=highest)
    write_half = write_grad.astype(jnp.bfloat16)
    partial_grad = jnp.dot(input_rows.T, write_half, preferred_element_type=jnp.float32)
    return (decay_grad, partial_grad)

def one_sequence(weight_half, inputs):
    block_count = SEQUENCE_LENGTH // TOK_DEV

    def to_blocks(array):
        return array.reshape((block_count, TOK_DEV) + array.shape[1:])
    blocked = tuple((to_blocks(array) for array in inputs))

    def states_of(item):
        return block_states(item[0], item[1], item[2], item[3], item[4], weight_half)
    decays, state_local, reverse_local = lax.map(states_of, blocked)
    zero_state = jnp.zeros((HALF_HEAD_COUNT, HEAD_DIM, STATE), jnp.float32)

    def forward_step(running_state, item):
        return (item[0][:, None, None] * running_state + item[1], running_state)
    unused_end, state_before = lax.scan(forward_step, zero_state, (decays, state_local))

    def reverse_step(running_state, item):
        return (item[1] + item[0][:, None, None] * running_state, running_state)
    unused_start, grad_after = lax.scan(reverse_step, zero_state, (decays, reverse_local), reverse=True)

    def grads_of(item):
        return block_gradients(item[0], item[1], item[2], item[3], item[4], weight_half, item[5], item[6])
    decay_grad, partials = lax.map(grads_of, blocked + (state_before, grad_after))
    return (decay_grad.reshape(SEQUENCE_LENGTH, HALF_HEAD_COUNT), lax.optimization_barrier(jnp.sum(partials, axis=0)))

def reference(layer_input, scan_input, readout, log_decay, output_cotangent, write_weight, first_moment, second_moment):
    weight_half = write_weight.astype(jnp.bfloat16)

    def sequence_step(grad_sum, inputs):
        decay_grad, partial_sum = one_sequence(weight_half, inputs)
        return (grad_sum + partial_sum, decay_grad)
    grad_total, decay_gradient = lax.scan(sequence_step, jnp.zeros((D, STATE), jnp.float32), (layer_input, scan_input, readout, log_decay, output_cotangent))
    new_first = beta_one * first_moment + (1.0 - beta_one) * grad_total
    new_second = beta_two * second_moment + (1.0 - beta_two) * grad_total * grad_total
    first_hat = new_first / (1.0 - beta_one ** adam_count)
    second_hat = new_second / (1.0 - beta_two ** adam_count)
    new_weight = write_weight - learn_rate * (first_hat / (jnp.sqrt(second_hat) + epsilon) + weight_decay * write_weight)
    return (decay_gradient, new_weight, new_first, new_second)
```

```python
import functools

import jax
import jax.numpy as jnp
from jax import lax
from jax.experimental import pallas as pl
from jax.experimental.pallas import tpu as pltpu
from jax.sharding import PartitionSpec as P

HEAD_DIM = 64

beta_one = 0.9
beta_two = 0.999
adam_count = 10.0
learn_rate = 0.01
weight_decay = 0.1
epsilon = 1e-08
highest = lax.Precision.HIGHEST
f32 = jnp.float32
bf16 = jnp.bfloat16
MESH = pl.DeviceIdType.MESH
VMEM = pl.BlockSpec(memory_space=pltpu.VMEM)


def remote(src, dst, send_sem, recv_sem, where):
    return pltpu.make_async_remote_copy(
        src_ref=src, dst_ref=dst, send_sem=send_sem, recv_sem=recv_sem, device_id=where,
        device_id_type=MESH,
    )


def loop(low, high, body):
    lax.fori_loop(low, high, lambda i, carry: (body(i), carry)[1], 0)


class Scan:
    def __init__(self, count, me, local, decay, gathered, sent, result, sems):
        self.count, self.me = count, me
        self.local, self.decay, self.gathered, self.sent, self.result = (
            local, decay, gathered, sent, result)
        self.width = local.shape[1] // count
        self.out_send, self.out_recv, self.back_send, self.back_recv = sems

    def columns(self, place):
        return pl.ds(pl.multiple_of(place * self.width, self.width), self.width)

    def outward(self, j, source):
        return remote(self.local.at[:, self.columns(j)], self.gathered.at[source],
                      self.out_send.at[j], self.out_recv.at[source], {"seq": j})

    def homeward(self, i, owner):
        return remote(self.sent.at[i], self.result.at[:, self.columns(owner)],
                      self.back_send.at[i], self.back_recv.at[owner], {"seq": i})

    def start(self):
        loop(1, self.count,
             lambda k: self.outward(lax.rem(self.me + k, self.count), self.me).start())
        self.gathered[self.me] = self.local[:, self.columns(self.me)]

    def combine(self, reverse):
        count, me = self.count, self.me

        def one(k, running):
            i = count - 1 - k if reverse else k

            @pl.when(i != me)
            def _():
                self.outward(i, i).wait_recv()

            self.sent[i] = running.astype(bf16)
            new = self.decay[i] * running + self.gathered[i].astype(f32)

            @pl.when(i != me)
            def _():
                self.homeward(i, me).start()

            return new

        lax.fori_loop(0, count, one, jnp.zeros(self.gathered.shape[1:], f32))
        self.result[:, self.columns(me)] = self.sent[me]

    def arrive(self):
        def one(k):
            j = lax.rem(self.me + k, self.count)
            self.homeward(j, j).wait_recv()

        loop(1, self.count, one)

    def drain(self):
        def one(k):
            j = lax.rem(self.me + k, self.count)
            self.outward(j, j).wait_send()
            self.homeward(j, j).wait_send()

        loop(1, self.count, one)

    def finish(self):
        self.arrive()
        self.drain()


def greet(seq_count, dp_count, same_core):
    seq_me, dp_me = lax.axis_index("seq"), lax.axis_index("dp")
    barrier = pltpu.get_barrier_semaphore()
    loop(1, seq_count, lambda k: pl.semaphore_signal(
        barrier, inc=1, device_id={"seq": lax.rem(seq_me + k, seq_count)}, device_id_type=MESH))
    total = seq_count - 1
    places = seq_count // 2 if same_core else 1

    def over(k):
        d = lax.rem(dp_me + 1 + k // places, dp_count)
        s = lax.rem(seq_me + 2 * (k % places), seq_count)
        pl.semaphore_signal(barrier, inc=1, device_id={"seq": s, "dp": d}, device_id_type=MESH)

    loop(0, (dp_count - 1) * places, over)
    return lambda: pl.semaphore_wait(barrier, total + (dp_count - 1) * places)


def first_kernel(seq_count, dp_count, weight, local, decay, weights, decays, result,
                 gathered, sent, w_send, w_recv, p_send, p_recv, d_send, d_recv,
                 a_send, a_recv, b_send, b_recv):
    seq_me, dp_me = lax.axis_index("seq"), lax.axis_index("dp")
    core = lax.rem(seq_me, 2)
    partner = seq_me + 1 - 2 * core
    greet(seq_count, dp_count, False)()

    def across(d, source):
        return remote(weight.at[core], weights.at[source, core], w_send.at[d], w_recv.at[source],
                      {"dp": d})

    def beside(d, half):
        return remote(weights.at[d, half], weights.at[d, half], p_send.at[d], p_recv.at[d],
                      {"seq": partner})

    def tell(j, source):
        return remote(decay.at[j], decays.at[source], d_send.at[j], d_recv.at[source], {"seq": j})

    loop(1, dp_count, lambda k: across(lax.rem(dp_me + k, dp_count), dp_me).start())
    loop(1, seq_count, lambda k: tell(lax.rem(seq_me + k, seq_count), seq_me).start())
    scan = Scan(seq_count, seq_me, local, decays, gathered, sent, result,
                (a_send, a_recv, b_send, b_recv))
    scan.start()
    decays[seq_me] = decay[seq_me]
    weights[dp_me] = weight[...]

    def told(k):
        j = lax.rem(seq_me + k, seq_count)
        tell(j, j).wait_recv()

    loop(1, seq_count, told)

    def pass_on(k):
        d = lax.rem(dp_me + k, dp_count)
        across(d, d).wait_recv()
        beside(d, core).start()

    loop(1, dp_count, pass_on)
    scan.combine(True)

    def end(k):
        d = lax.rem(dp_me + k, dp_count)
        across(d, d).wait_send()
        beside(d, core).wait_send()
        beside(d, 1 - core).wait_recv()

    loop(1, dp_count, end)
    loop(1, seq_count, lambda k: tell(lax.rem(seq_me + k, seq_count), 0).wait_send())
    scan.finish()


def second_kernel(seq_count, local, decays, result, gathered, sent, a_send, a_recv, b_send, b_recv):
    greet(seq_count, 1, False)()
    scan = Scan(seq_count, lax.axis_index("seq"), local, decays, gathered, sent, result,
                (a_send, a_recv, b_send, b_recv))
    scan.start()
    scan.combine(False)
    scan.finish()


def third_kernel(seq_count, dp_count, part, total, halves, summed, pieces,
                 h_send, h_recv, s_send, s_recv, g_send, g_recv):
    seq_me, dp_me = lax.axis_index("seq"), lax.axis_index("dp")
    core = lax.rem(seq_me, 2)
    chip = seq_me // 2
    partner = seq_me + 1 - 2 * core
    group = (seq_count // 2) * dp_count
    mine = chip * dp_count + dp_me
    greet(seq_count, dp_count, True)()

    def half(g):
        return remote(part.at[1 - core, g], halves.at[g], h_send.at[g], h_recv.at[g],
                      {"seq": partner})

    def scatter(g, source):
        return remote(summed.at[g], pieces.at[source], s_send.at[g], s_recv.at[source],
                      {"seq": 2 * (g // dp_count) + core, "dp": g % dp_count})

    def share(j, source):
        return remote(total.at[seq_me], total.at[source], g_send.at[j], g_recv.at[source],
                      {"seq": j})

    loop(1, group + 1, lambda k: half(lax.rem(mine + k, group)).start())

    def pair(k):
        g = lax.rem(mine + k, group)
        half(g).wait_recv()
        summed[g] = (part[core, g].astype(f32) + halves[g].astype(f32)).astype(bf16)

        @pl.when(g != mine)
        def _():
            scatter(g, mine).start()

    loop(1, group + 1, pair)

    def collect(k, running):
        g = lax.rem(mine + group - k, group)
        scatter(g, g).wait_recv()
        return running + pieces[g].astype(f32)

    own = part[core, mine].astype(f32) + halves[mine].astype(f32)
    total[seq_me] = lax.fori_loop(1, group, collect, own).astype(bf16)
    loop(1, seq_count, lambda k: share(lax.rem(seq_me + k, seq_count), seq_me).start())

    def end(k):
        j = lax.rem(seq_me + seq_count - k, seq_count)
        share(j, j).wait_recv()
        share(j, j).wait_send()

    loop(1, group + 1, lambda k: half(lax.rem(mine + k, group)).wait_send())
    loop(1, group, lambda k: scatter(lax.rem(mine + k, group), 0).wait_send())
    loop(1, seq_count, end)


def nt(a, b):
    return lax.dot_general(a, b, (((1,), (1,)), ((), ())), preferred_element_type=f32)


def split(a):
    high = a.astype(bf16)
    return high, (a - high.astype(f32)).astype(bf16)


def exact(a, b):
    return lax.dot_general(a, b, (((1,), (1,)), ((), ())), precision=highest)


class ChipScan:
    def __init__(self, count, chip, core, local, decays, gathered, sent, result, sems):
        self.count, self.chip, self.core = count, chip, core
        self.local, self.decays, self.gathered, self.sent, self.result = (
            local, decays, gathered, sent, result)
        self.width = local.shape[2]
        self.out_send, self.out_recv, self.back_send, self.back_recv = sems

    def columns(self, place):
        return pl.ds(pl.multiple_of(place * self.width, self.width), self.width)

    def outward(self, j, source):
        return remote(self.local.at[j], self.gathered.at[source],
                      self.out_send.at[j], self.out_recv.at[source], {"seq": 2 * j + self.core})

    def homeward(self, i, owner):
        return remote(self.sent.at[i], self.result.at[:, self.columns(owner)],
                      self.back_send.at[i], self.back_recv.at[owner], {"seq": 2 * i + self.core})

    def others(self, body):
        loop(1, self.count, lambda k: body(lax.rem(self.chip + k, self.count)))

    def start(self, total):
        for j in range(self.count):
            self.local[j] = total[:, j * self.width : (j + 1) * self.width].astype(bf16)
        self.others(lambda j: self.outward(j, self.chip).start())
        self.gathered[self.chip] = self.local[self.chip]

    def combine(self, reverse):
        def one(k, running):
            i = self.count - 1 - k if reverse else k

            @pl.when(i != self.chip)
            def _():
                self.outward(i, i).wait_recv()

            self.sent[i] = running.astype(bf16)
            new = self.decays[i] * running + self.gathered[i].astype(f32)

            @pl.when(i != self.chip)
            def _():
                self.homeward(i, self.chip).start()

            return new

        lax.fori_loop(0, self.count, one, jnp.zeros(self.gathered.shape[1:], f32))
        self.result[:, self.columns(self.chip)] = self.sent[self.chip]

    def arrive(self):
        self.others(lambda j: self.homeward(j, j).wait_recv())

    def drain(self):
        def one(j):
            self.outward(j, j).wait_send()
            self.homeward(j, j).wait_send()

        self.others(one)


def one_kernel(seq_count, dp_count, weight_hbm, log_decay_hbm, scan_hbm, back_hbm, read_hbm,
               input_hbm, decay_grad, total,
               log_decay, scan_rows, back_rows, read_rows, weight_rows, inputs,
               mine, pair, front_mine, front, scaled_scan, scaled_mine, scaled_got,
               kernel_mat, row_sums, col_sums, weights, write_mine, write_got,
               decay_out, decays, reverse_out, reverse_got, reverse_sent, reverse_home,
               forward_out, forward_got, forward_sent, forward_home,
               after, grad_after, prior, state_before, grad_mine, grad_got,
               part, pieces,
               load_sem, input_sem, l_send, l_recv, w_send, w_recv, d_send, d_recv,
               a_send, a_recv, b_send, b_recv, e_send, e_recv, f_send, f_recv,
               s_send, s_recv, g_send, g_recv, q_send, q_recv, m_send, m_recv):
    seq_me, dp_me = lax.axis_index("seq"), lax.axis_index("dp")
    core = lax.rem(seq_me, 2)
    other = 1 - core
    chip = seq_me // 2
    chips = seq_count // 2
    partner = {"seq": seq_me + 1 - 2 * core}
    group = chips * dp_count
    own = chip * dp_count + dp_me

    def place(g):
        return {"seq": 2 * (g // dp_count) + core, "dp": lax.rem(g, dp_count)}

    barrier = pltpu.get_barrier_semaphore()
    pl.semaphore_signal(barrier, inc=1, device_id=partner, device_id_type=MESH)
    loop(1, group, lambda k: pl.semaphore_signal(
        barrier, inc=1, device_id=place(lax.rem(own + k, group)), device_id_type=MESH))

    length, channels = scan_rows.shape
    half = channels // 2
    heads = channels // HEAD_DIM
    half_heads = heads // 2
    state_size = read_rows.shape[0]
    own_rows = weight_hbm.shape[1]
    side = own_rows // 2
    width = half // chips
    wide = side // chips

    def span(start, size):
        return pl.ds(pl.multiple_of(start, 128), size)

    loads = [
        pltpu.make_async_copy(log_decay_hbm, log_decay, load_sem.at[0]),
        pltpu.make_async_copy(back_hbm, back_rows, load_sem.at[1]),
        pltpu.make_async_copy(read_hbm, read_rows, load_sem.at[2]),
        pltpu.make_async_copy(weight_hbm.at[:, span(core * side, side)], weight_rows,
                              load_sem.at[3]),
        pltpu.make_async_copy(scan_hbm, scan_rows, load_sem.at[4]),
    ]
    for copy in loads:
        copy.start()
    my_rows = pl.ds(pl.multiple_of(core * length, length), length)

    def input_load(d):
        return pltpu.make_async_copy(
            input_hbm.at[:, span(d * own_rows + core * side, side)],
            inputs.at[my_rows, d * side : (d + 1) * side], input_sem.at[d])

    for d in range(dp_count):
        input_load(d).start()

    row_index = lax.broadcasted_iota(jnp.int32, (length, length), 0)
    col_index = lax.broadcasted_iota(jnp.int32, (length, length), 1)
    causal = row_index <= col_index
    before = (col_index < row_index).astype(f32)
    upto = (col_index <= row_index).astype(f32)
    onward = causal.astype(f32)
    owner = lax.broadcasted_iota(jnp.int32, (heads, channels), 0)
    spot = lax.broadcasted_iota(jnp.int32, (heads, channels), 1) - owner * HEAD_DIM
    member = ((spot >= 0) & (spot < HEAD_DIM)).astype(bf16)
    half_member = member[:half_heads, :half]

    def widen(a):
        high, low = split(a)
        return (jnp.dot(high, member, preferred_element_type=f32)
                + jnp.dot(low, member, preferred_element_type=f32))

    def per_head(a):
        high, low = split(a)
        return nt(half_member, high) + nt(half_member, low)

    loads[0].wait()
    run_cols = exact(upto, log_decay[...])
    run_rows = exact(log_decay[...], upto)
    overall = run_cols[length - 1 :, :]
    to_end = jnp.exp(overall - run_cols)
    from_start = jnp.exp(run_cols)
    decay_wide = widen(jnp.exp(jnp.broadcast_to(overall, (8, heads))))
    from_wide = widen(from_start)
    loads[1].wait()
    loads[2].wait()
    for h in range(2):
        at = slice(h * half, (h + 1) * half)
        back_high, back_low = split(back_rows[:, at].astype(f32) * from_wide[:, at])
        mine[h, :state_size] = (
            jnp.dot(read_rows[...], back_high, preferred_element_type=f32)
            + jnp.dot(read_rows[...], back_low, preferred_element_type=f32)
        )
        mine[h, state_size:] = decay_wide[:, at]
    loads[3].wait()
    weights[dp_me] = weight_rows[...].astype(bf16)

    def to_partner(src, dst, place):
        return remote(src, dst, m_send.at[place], m_recv.at[place], partner)

    def across(d, source):
        return remote(weights.at[dp_me], weights.at[source], w_send.at[d], w_recv.at[source],
                      {"dp": d})

    def lend(d, rows):
        return remote(input_hbm.at[:, span(d * own_rows + other * side, side)],
                      inputs.at[rows, d * side : (d + 1) * side],
                      l_send.at[d], l_recv.at[d], partner)

    def tell(j, source):
        return remote(decay_out.at[j], decays.at[source], d_send.at[j], d_recv.at[source],
                      {"seq": 2 * j + core})

    def scatter(g, source):
        return remote(part.at[g], pieces.at[source], s_send.at[g], s_recv.at[source], place(g))

    def columns(side_of, j):
        return span(side_of * side + j * wide, wide)

    def share(j, source):
        return remote(total.at[:, columns(core, source)], total.at[:, columns(core, source)],
                      g_send.at[j], g_recv.at[source], {"seq": 2 * j + core})

    def hand(j, from_core):
        return remote(total.at[:, columns(from_core, j)], total.at[:, columns(from_core, j)],
                      q_send.at[j], q_recv.at[j], partner)

    reverse = ChipScan(chips, chip, core, reverse_out, decays, reverse_got, reverse_sent,
                       reverse_home, (a_send, a_recv, b_send, b_recv))
    forward = ChipScan(chips, chip, core, forward_out, decays, forward_got, forward_sent,
                       forward_home, (e_send, e_recv, f_send, f_recv))

    pl.semaphore_wait(barrier, group)
    states_over = to_partner(mine.at[other], pair.at[core], 0)
    states_over.start()
    loop(1, dp_count, lambda k: across(lax.rem(dp_me + k, dp_count), dp_me).start())
    loads[4].wait()
    to_wide = widen(to_end)
    for h in range(2):
        at = slice(h * half, (h + 1) * half)
        scaled = scan_rows[:, at].astype(f32) * to_wide[:, at]
        scaled_scan[h] = scaled
        scaled_mine[h] = scaled.astype(bf16)
    pair[core] = mine[core]
    scaled_over = to_partner(scaled_mine.at[other], scaled_got, 1)
    scaled_over.start()
    for d in range(dp_count):
        lend(d, my_rows).start()

    states_over.wait_recv()
    first_decay = pair[0, state_size : state_size + 1]
    last_decay = pair[1, state_size : state_size + 1]
    chip_decay = first_decay * last_decay
    for j in range(chips):
        decay_out[j] = chip_decay[:, j * width : (j + 1) * width]
    reverse.others(lambda j: tell(j, chip).start())
    reverse.start(pair[0, :state_size] + first_decay * pair[1, :state_size])
    decays[chip] = decay_out[chip]

    kernel_sum = jnp.zeros((length, length), f32)
    for h in range(heads):
        at = slice(h * HEAD_DIM, (h + 1) * HEAD_DIM)
        crossed = nt(scan_rows[:, at], back_rows[:, at])
        spread = run_rows[h : h + 1, :] - run_cols[:, h : h + 1]
        term = jnp.where(causal, jnp.exp(jnp.minimum(spread, 0.0)), 0.0) * crossed
        kernel_mat[h] = term
        kernel_sum += term

    for d in range(dp_count):
        input_load(d).wait()
        lend(d, my_rows).wait_recv()
    loop(1, dp_count, lambda k: across(0, lax.rem(dp_me + k, dp_count)).wait_recv())
    some = nt(weights[0], inputs[:, :side])
    for d in range(1, dp_count):
        some += nt(weights[d], inputs[:, d * side : (d + 1) * side])
    for t in range(2):
        write_mine[t] = some[:, t * length : (t + 1) * length]
    write_over = to_partner(write_mine.at[other], write_got, 2)
    write_over.start()
    write_over.wait_recv()
    write = write_mine[core] + write_got[...]
    write_rows = write.T.astype(bf16)
    write = write.astype(bf16)
    for h in range(2):
        scan_high, scan_low = split(scaled_scan[h])
        front_mine[h] = (
            jnp.dot(write, scan_high, preferred_element_type=f32)
            + jnp.dot(write, scan_low, preferred_element_type=f32)
        )
    front_over = to_partner(front_mine.at[other], front.at[core], 3)
    front_over.start()
    front[core] = front_mine[core]

    reverse.others(lambda j: tell(j, j).wait_recv())
    reverse.combine(True)
    front_over.wait_recv()
    forward.start(last_decay * front[0] + front[1])

    sum_high, sum_low = split(kernel_sum)
    inner = nt(read_rows[...], sum_high) + nt(read_rows[...], sum_low)
    scaled_over.wait_recv()
    reverse.arrive()
    after[1] = reverse_home[...]
    after[0] = (pair[1, :state_size] + last_decay * reverse_home[...].astype(f32)).astype(bf16)
    grad_mine[core] = nt(after[core], scaled_mine[core]) + inner
    grad_mine[other] = nt(after[other], scaled_got[...])
    grad_over = to_partner(grad_mine, grad_got, 4)
    grad_over.start()
    after_over = to_partner(after.at[other], grad_after.at[core], 5)
    after_over.start()
    grad_after[core] = after[core]
    grad_over.wait_recv()
    grad_half = (grad_mine[...] + grad_got[...]).astype(bf16)
    grad_half = jnp.concatenate([grad_half[0], grad_half[1]], axis=1)
    for d in range(dp_count):
        for j in range(0, chips, 2):
            low = d * side + j * wide
            term = jnp.dot(grad_half, inputs[:, low : low + 2 * wide],
                           preferred_element_type=f32).astype(bf16)
            part[j * dp_count + d] = term[:, :wide]
            part[(j + 1) * dp_count + d] = term[:, wide:]
    loop(1, group, lambda k: scatter(lax.rem(own + k, group), own).start())

    forward.combine(False)
    read_turned = read_rows[...].astype(f32).T.astype(bf16)
    write_read = jnp.where(row_index < col_index, nt(write_rows, read_turned), 0.0)
    for h in range(heads):
        pairing = kernel_mat[h] * write_read
        row_sums[:, h : h + 1] = jnp.sum(pairing, axis=1, keepdims=True)
        col_sums[h : h + 1, :] = jnp.sum(pairing, axis=0, keepdims=True)
    after_over.wait_recv()
    second = []
    for h in range(2):
        grad_write = jnp.dot(write_rows, grad_after[h], preferred_element_type=f32)
        second.append(per_head(scan_rows[:, h * half : (h + 1) * half].astype(f32) * grad_write))
    overall_rows = run_rows[:, length - 1 :]
    second = (jnp.exp(overall_rows - run_rows) * jnp.concatenate(second, axis=0)
              + row_sums[...].T - col_sums[...])

    def collect(k, running):
        g = lax.rem(own + group - k, group)
        scatter(g, g).wait_recv()
        return running + pieces[g].astype(f32)

    total[:, columns(core, chip)] = lax.fori_loop(
        1, group, collect, part[own].astype(f32)).astype(bf16)
    reverse.others(lambda j: share(j, chip).start())
    hand(chip, core).start()

    forward.arrive()
    prior[0] = forward_home[...]
    prior[1] = (front[0] + first_decay * forward_home[...].astype(f32)).astype(bf16)
    prior_over = to_partner(prior.at[other], state_before.at[core], 6)
    prior_over.start()
    state_before[core] = prior[core]
    prior_over.wait_recv()
    third, first = [], []
    for h in range(2):
        at = slice(h * half, (h + 1) * half)
        state_read = jnp.dot(read_turned, state_before[h], preferred_element_type=f32)
        third.append(per_head(back_rows[:, at].astype(f32) * state_read))
        both = jnp.sum(grad_after[h].astype(f32) * state_before[h].astype(f32), axis=0,
                       keepdims=True)
        first.append(per_head(jnp.broadcast_to(both, (8, half)))[:, :1])
    decay_grad[...] = (
        jnp.exp(overall_rows) * jnp.concatenate(first, axis=0)
        + exact(second, before)
        + exact(jnp.exp(run_rows) * jnp.concatenate(third, axis=0), onward)
    )

    def pass_on(k):
        j = lax.rem(chip + chips - k, chips)
        share(j, j).wait_recv()
        hand(j, core).start()

    loop(1, chips, pass_on)
    loop(0, chips, lambda j: hand(j, other).wait_recv())

    loop(1, dp_count, lambda k: across(lax.rem(dp_me + k, dp_count), 0).wait_send())
    for d in range(dp_count):
        lend(d, my_rows).wait_send()
    for copy in (states_over, scaled_over, write_over, front_over, grad_over, after_over, prior_over):
        copy.wait_send()
    reverse.drain()
    forward.drain()
    reverse.others(lambda j: tell(j, 0).wait_send())
    loop(1, group, lambda k: scatter(lax.rem(own + k, group), 0).wait_send())
    reverse.others(lambda j: share(j, chip).wait_send())
    loop(0, chips, lambda j: hand(j, core).wait_send())


def dma(*sizes):
    return [pltpu.SemaphoreType.DMA((size,)) for size in sizes for _ in range(2)]


def adam_update(grad_rows, weight_rows, first_rows, second_rows):
    new_first = beta_one * first_rows + (1.0 - beta_one) * grad_rows
    new_second = beta_two * second_rows + (1.0 - beta_two) * grad_rows * grad_rows
    first_hat = new_first / (1.0 - beta_one**adam_count)
    second_hat = new_second / (1.0 - beta_two**adam_count)
    new_weight = weight_rows - learn_rate * (
        first_hat / (jnp.sqrt(second_hat) + epsilon) + weight_decay * weight_rows
    )
    return (new_weight, new_first, new_second)


def on_device(
    layer_input,
    scan_input,
    readout,
    log_decay,
    output_cotangent,
    write_weight,
    first_moment,
    second_moment,
):
    seq_count, dp_count = lax.axis_size("seq"), lax.axis_size("dp")
    input_rows = layer_input[0]
    scan_rows = scan_input[0]
    read_rows = readout[0]
    decay_rows = log_decay[0]
    back_rows = output_cotangent[0]
    length, model = input_rows.shape
    heads = decay_rows.shape[1]
    channels = scan_rows.shape[1]
    state_size = read_rows.shape[1]
    own_rows = write_weight.shape[0]
    width = channels // seq_count

    chips = seq_count // 2
    group = chips * dp_count
    fast = own_rows % (128 * seq_count) == 0 and channels % (128 * seq_count) == 0
    if fast:
        half = channels // 2
        wide = own_rows // seq_count
        piece = (state_size, wide)
        block = (chips, state_size, width)
        decay_grad, grad_sum = pl.pallas_call(
            functools.partial(one_kernel, seq_count, dp_count),
            out_shape=(
                jax.ShapeDtypeStruct((heads, length), f32),
                jax.ShapeDtypeStruct((state_size, own_rows), bf16),
            ),
            in_specs=[pl.BlockSpec(memory_space=pl.ANY)] * 6,
            out_specs=[VMEM] * 2,
            scratch_shapes=[
                pltpu.VMEM((heads, length), f32),
                pltpu.VMEM((length, channels), bf16),
                pltpu.VMEM((length, channels), bf16),
                pltpu.VMEM((state_size, length), bf16),
                pltpu.VMEM((state_size, own_rows // 2), f32),
                pltpu.VMEM((2 * length, model // 2), bf16),
                pltpu.VMEM((2, state_size + 8, half), f32),
                pltpu.VMEM((2, state_size + 8, half), f32),
                pltpu.VMEM((2, state_size, half), f32),
                pltpu.VMEM((2, state_size, half), f32),
                pltpu.VMEM((2, length, half), f32),
                pltpu.VMEM((2, length, half), bf16),
                pltpu.VMEM((length, half), bf16),
                pltpu.VMEM((heads, length, length), f32),
                pltpu.VMEM((length, heads), f32),
                pltpu.VMEM((heads, length), f32),
                pltpu.VMEM((dp_count, state_size, own_rows // 2), bf16),
                pltpu.VMEM((2, state_size, length), f32),
                pltpu.VMEM((state_size, length), f32),
                pltpu.VMEM((chips, 1, width), f32),
                pltpu.VMEM((chips, 1, width), f32),
            ]
            + ([pltpu.VMEM(block, bf16)] * 3 + [pltpu.VMEM((state_size, half), bf16)]) * 2
            + [pltpu.VMEM((2, state_size, half), bf16)] * 4
            + [pltpu.VMEM((2, state_size, length), f32)] * 2
            + [pltpu.VMEM((group,) + piece, bf16)] * 2
            + [pltpu.SemaphoreType.DMA((5,)), pltpu.SemaphoreType.DMA((dp_count,))]
            + dma(dp_count, dp_count, chips, chips, chips, chips, chips, group, chips, chips, 7),
            compiler_params=pltpu.CompilerParams(collective_id=3, has_side_effects=True,
                                                 vmem_limit_bytes=40 * 2**20),
            name="whole_step",
        )(write_weight.T, decay_rows.T, scan_rows, back_rows, read_rows.T, input_rows)
        decay_grad = decay_grad.T
        grad_rows = grad_sum.astype(f32).T
    else:
        row_index = lax.broadcasted_iota(jnp.int32, (length, length), 0)
        col_index = lax.broadcasted_iota(jnp.int32, (length, length), 1)
        upto = (col_index <= row_index).astype(f32)
        before = (col_index < row_index).astype(f32)
        running = jnp.dot(upto, decay_rows, precision=highest)
        overall = running[-1]
        to_end = jnp.exp(overall[None, :] - running)
        from_start = jnp.exp(running)
        decay_total = jnp.exp(overall)

        def widen(a):
            return jnp.repeat(a, HEAD_DIM, axis=1)

        scaled_scan = scan_rows.astype(f32) * widen(to_end)
        scaled_back = back_rows.astype(f32) * widen(from_start)

        def state_of(vectors, rows):
            return lax.dot_general(
                vectors.astype(f32), rows, (((0,), (0,)), ((), ())), precision=highest
            ).astype(bf16)

        reverse_local = state_of(read_rows, scaled_back)
        decay_lanes = widen(decay_total[None]).reshape(seq_count, 1, width)
        weight_half = write_weight.T.astype(bf16).reshape(2, state_size // 2, own_rows)
        exchange = [
            pltpu.VMEM((seq_count, state_size, width), bf16),
            pltpu.VMEM((seq_count, state_size, width), bf16),
        ]
        piece = (state_size * own_rows // seq_count // 128, 128)
        scan_split = scan_rows.reshape(length, heads, HEAD_DIM)
        back_split = back_rows.reshape(length, heads, HEAD_DIM)
        crossed = jnp.einsum("thp,shp->hts", scan_split, back_split, preferred_element_type=f32)
        heads_running = running.T
        spread = heads_running[:, None, :] - heads_running[:, :, None]
        kernel_mat = (
            jnp.where((row_index <= col_index)[None], jnp.exp(jnp.minimum(spread, 0.0)), 0.0) * crossed
        )
        weights, decays, grad_after = pl.pallas_call(
            functools.partial(first_kernel, seq_count, dp_count),
            out_shape=(
                jax.ShapeDtypeStruct((dp_count,) + weight_half.shape, bf16),
                jax.ShapeDtypeStruct(decay_lanes.shape, f32),
                jax.ShapeDtypeStruct((state_size, channels), bf16),
            ),
            in_specs=[VMEM] * 3,
            out_specs=[VMEM] * 3,
            scratch_shapes=exchange + dma(dp_count, dp_count, seq_count, seq_count, seq_count),
            compiler_params=pltpu.CompilerParams(collective_id=0, has_side_effects=True),
            name="gather_reverse",
        )(weight_half, reverse_local, decay_lanes)

        weight_all = weights.reshape(dp_count, state_size, own_rows).transpose(1, 0, 2)
        write_half = lax.dot_general(
            input_rows, weight_all.reshape(state_size, model), (((1,), (1,)), ((), ())),
            preferred_element_type=f32,
        ).astype(bf16)
        state_local = state_of(write_half, scaled_scan)
        state_before = pl.pallas_call(
            functools.partial(second_kernel, seq_count),
            out_shape=jax.ShapeDtypeStruct((state_size, channels), bf16),
            in_specs=[VMEM] * 2,
            out_specs=VMEM,
            scratch_shapes=exchange + dma(seq_count, seq_count),
            compiler_params=pltpu.CompilerParams(collective_id=1, has_side_effects=True),
            name="forward_states",
        )(state_local, decays)

        kernel_sum = jnp.sum(kernel_mat, axis=0)
        write_grad = jnp.dot(kernel_sum, read_rows.astype(f32), precision=highest)
        write_grad = write_grad + lax.dot_general(
            scaled_scan.astype(bf16), grad_after, (((1,), (1,)), ((), ())), preferred_element_type=f32
        )
        grad_half = write_grad.astype(bf16)
        partial = lax.dot_general(
            grad_half, input_rows, (((0,), (0,)), ((), ())), preferred_element_type=f32
        ).astype(bf16)
        part = partial.reshape(state_size, dp_count, chips, 2, own_rows // seq_count)
        part = part.transpose(3, 2, 1, 0, 4).reshape((2, chips * dp_count) + piece)
        grad_sum = pl.pallas_call(
            functools.partial(third_kernel, seq_count, dp_count),
            out_shape=jax.ShapeDtypeStruct((seq_count,) + piece, bf16),
            in_specs=[VMEM],
            out_specs=VMEM,
            scratch_shapes=[pltpu.VMEM((chips * dp_count,) + piece, bf16)] * 3
            + dma(chips * dp_count, chips * dp_count, seq_count),
            compiler_params=pltpu.CompilerParams(collective_id=2, has_side_effects=True),
            name="reduce_gradient",
        )(part)
        def per_head(a):
            return jnp.sum(a.reshape(a.shape[0], heads, HEAD_DIM), axis=2)

        term_one = decay_total * jnp.sum(
            per_head(grad_after.astype(f32) * state_before.astype(f32)), axis=0)
        grad_write = jnp.dot(write_half, grad_after, preferred_element_type=f32)
        second_rows = to_end * per_head(scan_rows.astype(f32) * grad_write)
        term_two = jnp.dot(before, second_rows, precision=highest)
        state_read = jnp.dot(read_rows, state_before, preferred_element_type=f32)
        third_rows = from_start * per_head(back_rows.astype(f32) * state_read)
        term_three = jnp.dot(upto.T, third_rows, precision=highest)
        write_read = jnp.dot(write_half, read_rows.T, preferred_element_type=f32)
        pairing = jnp.where((row_index < col_index)[None], kernel_mat * write_read[None], 0.0)
        balance = (jnp.sum(pairing, axis=2) - jnp.sum(pairing, axis=1)).T
        term_four = jnp.dot(before, balance, precision=highest)
        decay_grad = term_one[None, :] + term_two + term_three + term_four
        grad_rows = grad_sum.reshape(seq_count, state_size, own_rows // seq_count)
        grad_rows = grad_rows.transpose(1, 0, 2).reshape(state_size, own_rows).astype(f32).T
    new_weight, new_first, new_second = adam_update(
        grad_rows, write_weight, first_moment, second_moment
    )

    return (decay_grad[None], new_weight, new_first, new_second)


def solution(mesh):
    in_specs = (
        P("dp", "seq", None),
        P("dp", "seq", None),
        P("dp", "seq", None),
        P("dp", "seq", None),
        P("dp", "seq", None),
        P("dp", None),
        P("dp", None),
        P("dp", None),
    )
    out_specs = (P("dp", "seq", None), P("dp", None), P("dp", None), P("dp", None))
    return jax.shard_map(
        on_device, mesh=mesh, in_specs=in_specs, out_specs=out_specs, check_vma=False
    )
```

```python
import functools

import jax
import jax.numpy as jnp
from jax import lax
from jax.experimental import pallas as pl
from jax.experimental.pallas import tpu as pltpu
from jax.sharding import PartitionSpec as P

HEAD_DIM = 64

beta_one = 0.9
beta_two = 0.999
adam_count = 10.0
learn_rate = 0.01
weight_decay = 0.1
epsilon = 1e-08
highest = lax.Precision.HIGHEST
f32 = jnp.float32
bf16 = jnp.bfloat16
MESH = pl.DeviceIdType.MESH
VMEM = pl.BlockSpec(memory_space=pltpu.VMEM)


def remote(src, dst, send_sem, recv_sem, where):
    return pltpu.make_async_remote_copy(
        src_ref=src, dst_ref=dst, send_sem=send_sem, recv_sem=recv_sem, device_id=where,
        device_id_type=MESH,
    )


def loop(low, high, body):
    lax.fori_loop(low, high, lambda i, carry: (body(i), carry)[1], 0)


class Scan:
    def __init__(self, count, me, local, decay, gathered, sent, result, sems):
        self.count, self.me = count, me
        self.local, self.decay, self.gathered, self.sent, self.result = (
            local, decay, gathered, sent, result)
        self.width = local.shape[1] // count
        self.out_send, self.out_recv, self.back_send, self.back_recv = sems

    def columns(self, place):
        return pl.ds(pl.multiple_of(place * self.width, self.width), self.width)

    def outward(self, j, source):
        return remote(self.local.at[:, self.columns(j)], self.gathered.at[source],
                      self.out_send.at[j], self.out_recv.at[source], {"seq": j})

    def homeward(self, i, owner):
        return remote(self.sent.at[i], self.result.at[:, self.columns(owner)],
                      self.back_send.at[i], self.back_recv.at[owner], {"seq": i})

    def start(self):
        loop(1, self.count,
             lambda k: self.outward(lax.rem(self.me + k, self.count), self.me).start())
        self.gathered[self.me] = self.local[:, self.columns(self.me)]

    def combine(self, reverse):
        count, me = self.count, self.me

        def one(k, running):
            i = count - 1 - k if reverse else k

            @pl.when(i != me)
            def _():
                self.outward(i, i).wait_recv()

            self.sent[i] = running.astype(bf16)
            new = self.decay[i] * running + self.gathered[i].astype(f32)

            @pl.when(i != me)
            def _():
                self.homeward(i, me).start()

            return new

        lax.fori_loop(0, count, one, jnp.zeros(self.gathered.shape[1:], f32))
        self.result[:, self.columns(me)] = self.sent[me]

    def arrive(self):
        def one(k):
            j = lax.rem(self.me + k, self.count)
            self.homeward(j, j).wait_recv()

        loop(1, self.count, one)

    def drain(self):
        def one(k):
            j = lax.rem(self.me + k, self.count)
            self.outward(j, j).wait_send()
            self.homeward(j, j).wait_send()

        loop(1, self.count, one)

    def finish(self):
        self.arrive()
        self.drain()


def greet(seq_count, dp_count, same_core):
    seq_me, dp_me = lax.axis_index("seq"), lax.axis_index("dp")
    barrier = pltpu.get_barrier_semaphore()
    loop(1, seq_count, lambda k: pl.semaphore_signal(
        barrier, inc=1, device_id={"seq": lax.rem(seq_me + k, seq_count)}, device_id_type=MESH))
    total = seq_count - 1
    places = seq_count // 2 if same_core else 1

    def over(k):
        d = lax.rem(dp_me + 1 + k // places, dp_count)
        s = lax.rem(seq_me + 2 * (k % places), seq_count)
        pl.semaphore_signal(barrier, inc=1, device_id={"seq": s, "dp": d}, device_id_type=MESH)

    loop(0, (dp_count - 1) * places, over)
    return lambda: pl.semaphore_wait(barrier, total + (dp_count - 1) * places)


def first_kernel(seq_count, dp_count, weight, local, decay, weights, decays, result,
                 gathered, sent, w_send, w_recv, p_send, p_recv, d_send, d_recv,
                 a_send, a_recv, b_send, b_recv):
    seq_me, dp_me = lax.axis_index("seq"), lax.axis_index("dp")
    core = lax.rem(seq_me, 2)
    partner = seq_me + 1 - 2 * core
    greet(seq_count, dp_count, False)()

    def across(d, source):
        return remote(weight.at[core], weights.at[source, core], w_send.at[d], w_recv.at[source],
                      {"dp": d})

    def beside(d, half):
        return remote(weights.at[d, half], weights.at[d, half], p_send.at[d], p_recv.at[d],
                      {"seq": partner})

    def tell(j, source):
        return remote(decay.at[j], decays.at[source], d_send.at[j], d_recv.at[source], {"seq": j})

    loop(1, dp_count, lambda k: across(lax.rem(dp_me + k, dp_count), dp_me).start())
    loop(1, seq_count, lambda k: tell(lax.rem(seq_me + k, seq_count), seq_me).start())
    scan = Scan(seq_count, seq_me, local, decays, gathered, sent, result,
                (a_send, a_recv, b_send, b_recv))
    scan.start()
    decays[seq_me] = decay[seq_me]
    weights[dp_me] = weight[...]

    def told(k):
        j = lax.rem(seq_me + k, seq_count)
        tell(j, j).wait_recv()

    loop(1, seq_count, told)

    def pass_on(k):
        d = lax.rem(dp_me + k, dp_count)
        across(d, d).wait_recv()
        beside(d, core).start()

    loop(1, dp_count, pass_on)
    scan.combine(True)

    def end(k):
        d = lax.rem(dp_me + k, dp_count)
        across(d, d).wait_send()
        beside(d, core).wait_send()
        beside(d, 1 - core).wait_recv()

    loop(1, dp_count, end)
    loop(1, seq_count, lambda k: tell(lax.rem(seq_me + k, seq_count), 0).wait_send())
    scan.finish()


def second_kernel(seq_count, local, decays, result, gathered, sent, a_send, a_recv, b_send, b_recv):
    greet(seq_count, 1, False)()
    scan = Scan(seq_count, lax.axis_index("seq"), local, decays, gathered, sent, result,
                (a_send, a_recv, b_send, b_recv))
    scan.start()
    scan.combine(False)
    scan.finish()


def third_kernel(seq_count, dp_count, part, total, halves, summed, pieces,
                 h_send, h_recv, s_send, s_recv, g_send, g_recv):
    seq_me, dp_me = lax.axis_index("seq"), lax.axis_index("dp")
    core = lax.rem(seq_me, 2)
    chip = seq_me // 2
    partner = seq_me + 1 - 2 * core
    group = (seq_count // 2) * dp_count
    mine = chip * dp_count + dp_me
    greet(seq_count, dp_count, True)()

    def half(g):
        return remote(part.at[1 - core, g], halves.at[g], h_send.at[g], h_recv.at[g],
                      {"seq": partner})

    def scatter(g, source):
        return remote(summed.at[g], pieces.at[source], s_send.at[g], s_recv.at[source],
                      {"seq": 2 * (g // dp_count) + core, "dp": g % dp_count})

    def share(j, source):
        return remote(total.at[seq_me], total.at[source], g_send.at[j], g_recv.at[source],
                      {"seq": j})

    loop(1, group + 1, lambda k: half(lax.rem(mine + k, group)).start())

    def pair(k):
        g = lax.rem(mine + k, group)
        half(g).wait_recv()
        summed[g] = (part[core, g].astype(f32) + halves[g].astype(f32)).astype(bf16)

        @pl.when(g != mine)
        def _():
            scatter(g, mine).start()

    loop(1, group + 1, pair)

    def collect(k, running):
        g = lax.rem(mine + group - k, group)
        scatter(g, g).wait_recv()
        return running + pieces[g].astype(f32)

    own = part[core, mine].astype(f32) + halves[mine].astype(f32)
    total[seq_me] = lax.fori_loop(1, group, collect, own).astype(bf16)
    loop(1, seq_count, lambda k: share(lax.rem(seq_me + k, seq_count), seq_me).start())

    def end(k):
        j = lax.rem(seq_me + seq_count - k, seq_count)
        share(j, j).wait_recv()
        share(j, j).wait_send()

    loop(1, group + 1, lambda k: half(lax.rem(mine + k, group)).wait_send())
    loop(1, group, lambda k: scatter(lax.rem(mine + k, group), 0).wait_send())
    loop(1, seq_count, end)


def nt(a, b):
    return lax.dot_general(a, b, (((1,), (1,)), ((), ())), preferred_element_type=f32)


def split(a):
    high = a.astype(bf16)
    return high, (a - high.astype(f32)).astype(bf16)


def exact(a, b):
    return lax.dot_general(a, b, (((1,), (1,)), ((), ())), precision=highest)


def stack_split(a, axis, parts=2):
    pieces, rest = [], a
    for _ in range(parts):
        pieces.append(rest.astype(bf16))
        rest = rest - pieces[-1].astype(f32)
    return jnp.concatenate(pieces, axis=axis)


def repeat(a, axis, parts=2):
    return jnp.concatenate([a] * parts, axis=axis)


def dot(a, b):
    return jnp.dot(a, b, preferred_element_type=f32)


class Owners:
    def __init__(self, chips, chip, mid=True):
        self.count = chips // 2 if mid and chips % 4 == 0 else chips
        self.base = (chips - self.count) // 2
        self.me = chip - self.base
        self.is_me = (self.me >= 0) & (self.me < self.count)

    def chip(self, o):
        return self.base + o


class ChipScan:
    def __init__(self, count, chip, core, owners, reverse, local, decays, gathered, sent, result,
                 sems):
        self.count, self.chip, self.core, self.owners, self.reverse = (
            count, chip, core, owners, reverse)
        self.local, self.decays, self.gathered, self.sent, self.result = (
            local, decays, gathered, sent, result)
        self.width = local.shape[2]
        self.out_send, self.out_recv, self.back_send, self.back_recv = sems
        self.head, self.tail = (count - 1, 0) if reverse else (0, count - 1)

    def columns(self, o):
        return pl.ds(pl.multiple_of(o * self.width, self.width), self.width)

    def outward(self, o, source):
        return remote(self.local.at[o], self.gathered.at[source], self.out_send.at[o],
                      self.out_recv.at[source], {"seq": 2 * self.owners.chip(o) + self.core})

    def homeward(self, i, o):
        return remote(self.sent.at[i], self.result.at[:, self.columns(o)],
                      self.back_send.at[i], self.back_recv.at[o], {"seq": 2 * i + self.core})

    def to_owners(self, body):
        def one(k):
            o = lax.rem(self.chip + k, self.owners.count)

            @pl.when(o != self.owners.me)
            def _():
                body(o)

        loop(0, self.owners.count, one)

    def others(self, body):
        loop(1, self.count, lambda k: body(lax.rem(self.chip + k, self.count)))

    def start(self, total):
        for o in range(self.owners.count):
            self.local[o] = total[:, o * self.width : (o + 1) * self.width].astype(bf16)

        @pl.when(self.chip != self.tail)
        def _():
            self.to_owners(lambda o: self.outward(o, self.chip).start())

        @pl.when(self.owners.is_me)
        def _():
            self.gathered[self.chip] = self.local[self.owners.me]

    def combine(self):
        def one(k, running):
            i = self.count - 1 - k if self.reverse else k

            @pl.when((i != self.chip) & (i != self.tail))
            def _():
                self.outward(0, i).wait_recv()

            self.sent[i] = running.astype(bf16)

            @pl.when((i != self.chip) & (i != self.head))
            def _():
                self.homeward(i, self.owners.me).start()

            if k == self.count - 1:
                return running
            return self.decays[i] * running + self.gathered[i].astype(f32)

        @pl.when(self.owners.is_me)
        def _():
            running = jnp.zeros(self.gathered.shape[1:], f32)
            for k in range(self.count):
                running = one(k, running)
            self.result[:, self.columns(self.owners.me)] = self.sent[self.chip]

    def arrive(self):
        @pl.when(self.chip != self.head)
        def _():
            self.to_owners(lambda o: self.homeward(self.chip, o).wait_recv())

        @pl.when(self.chip == self.head)
        def _():
            self.result[...] = jnp.zeros_like(self.result)

    def drain(self):
        @pl.when(self.chip != self.tail)
        def _():
            self.to_owners(lambda o: self.outward(o, 0).wait_send())

        def one(j):
            @pl.when(j != self.head)
            def _():
                self.homeward(j, 0).wait_send()

        @pl.when(self.owners.is_me)
        def _():
            self.others(one)


def one_kernel(seq_count, dp_count, weight_hbm, log_decay_hbm, scan_hbm, back_hbm, read_hbm,
               input_hbm, decay_grad, total,
               log_decay, scan_rows, back_rows, read_rows, weight_rows, inputs,
               mine, pair, front_mine, front, scaled_scan, scaled_mine, scaled_got,
               kernel_mat, row_sums, col_sums, weights, write_mine, write_got,
               decay_out, decays, reverse_out, reverse_got, reverse_sent, reverse_home,
               forward_out, forward_got, forward_sent, forward_home,
               after, grad_after, prior, state_before, grad_mine, grad_got,
               part, pieces,
               load_sem, input_sem, l_send, l_recv, w_send, w_recv, d_send, d_recv,
               a_send, a_recv, b_send, b_recv, e_send, e_recv, f_send, f_recv,
               s_send, s_recv, g_send, g_recv, q_send, q_recv, m_send, m_recv):
    seq_me, dp_me = lax.axis_index("seq"), lax.axis_index("dp")
    core = lax.rem(seq_me, 2)
    other = 1 - core
    chip = seq_me // 2
    chips = seq_count // 2
    partner = {"seq": seq_me + 1 - 2 * core}
    group = chips * dp_count
    own = chip * dp_count + dp_me

    owners = Owners(chips, chip, False)
    keep = Owners(chips, chip, True)
    held = keep.count * dp_count
    own_held = keep.me * dp_count + dp_me

    def place(g):
        return {"seq": 2 * (g // dp_count) + core, "dp": lax.rem(g, dp_count)}

    barrier = pltpu.get_barrier_semaphore()
    pl.semaphore_signal(barrier, inc=1, device_id=partner, device_id_type=MESH)
    loop(1, group, lambda k: pl.semaphore_signal(
        barrier, inc=1, device_id=place(lax.rem(own + k, group)), device_id_type=MESH))

    length, channels = scan_rows.shape
    half = channels // 2
    heads = channels // HEAD_DIM
    half_heads = heads // 2
    state_size = read_rows.shape[0]
    own_rows = weight_hbm.shape[1]
    side = own_rows // 2
    width = half // owners.count
    wide = side // keep.count

    def span(start, size):
        return pl.ds(pl.multiple_of(start, 128), size)

    loads = [
        pltpu.make_async_copy(log_decay_hbm, log_decay, load_sem.at[0]),
        pltpu.make_async_copy(back_hbm, back_rows, load_sem.at[1]),
        pltpu.make_async_copy(read_hbm, read_rows, load_sem.at[2]),
        pltpu.make_async_copy(weight_hbm.at[:, span(core * side, side)], weight_rows,
                              load_sem.at[3]),
        pltpu.make_async_copy(scan_hbm, scan_rows, load_sem.at[4]),
    ]
    for copy in loads:
        copy.start()
    my_rows = pl.ds(pl.multiple_of(core * length, length), length)

    def input_load(d):
        return pltpu.make_async_copy(
            input_hbm.at[:, span(d * own_rows + core * side, side)],
            inputs.at[my_rows, d * side : (d + 1) * side], input_sem.at[d])

    for d in range(dp_count):
        input_load(d).start()

    row_index = lax.broadcasted_iota(jnp.int32, (length, length), 0)
    col_index = lax.broadcasted_iota(jnp.int32, (length, length), 1)
    causal = row_index <= col_index
    upto = repeat((col_index <= row_index).astype(f32).astype(bf16), 1, 3)
    owner = lax.broadcasted_iota(jnp.int32, (heads, channels), 0)
    spot = lax.broadcasted_iota(jnp.int32, (heads, channels), 1) - owner * HEAD_DIM
    member = ((spot >= 0) & (spot < HEAD_DIM)).astype(bf16)
    half_member = member[:half_heads, :half]
    member = repeat(member, 0)

    def widen(a):
        return dot(stack_split(a, 1), member)

    def per_head(a):
        high, low = split(a)
        return nt(half_member, high) + nt(half_member, low)

    loads[0].wait()
    decay_parts = stack_split(log_decay[...], 1, 3)
    run_cols = nt(upto, decay_parts)
    overall = run_cols[length - 1 :, :]
    from_wide = widen(jnp.exp(run_cols))
    decay_wide = from_wide[length - 1 :, :]
    loads[1].wait()
    loads[2].wait()
    read_twice = repeat(read_rows[...], 1)
    for h in range(2):
        at = slice(h * half, (h + 1) * half)
        scaled = back_rows[:, at].astype(f32) * from_wide[:, at]
        mine[h, :state_size] = dot(read_twice, stack_split(scaled, 0))
        mine[h, state_size:] = jnp.broadcast_to(decay_wide[:, at], (8, half))
    loads[3].wait()
    weights[dp_me] = weight_rows[...].astype(bf16)

    def to_partner(src, dst, place):
        return remote(src, dst, m_send.at[place], m_recv.at[place], partner)

    def across(d, source):
        return remote(weights.at[dp_me], weights.at[source], w_send.at[d], w_recv.at[source],
                      {"dp": d})

    def lend(d, rows):
        return remote(input_hbm.at[:, span(d * own_rows + other * side, side)],
                      inputs.at[rows, d * side : (d + 1) * side],
                      l_send.at[d], l_recv.at[d], partner)

    def tell(o, source):
        return remote(decay_out.at[o], decays.at[source], d_send.at[o], d_recv.at[source],
                      {"seq": 2 * owners.chip(o) + core})

    def scatter(g, source):
        return remote(part.at[g], pieces.at[source], s_send.at[g], s_recv.at[source],
                      place(keep.base * dp_count + g))

    def columns(side_of, o):
        return span(side_of * side + o * wide, wide)

    def share(j, o):
        return remote(total.at[:, columns(core, o)], total.at[:, columns(core, o)],
                      g_send.at[j], g_recv.at[o], {"seq": 2 * j + core})

    def hand(o, from_core):
        return remote(total.at[:, columns(from_core, o)], total.at[:, columns(from_core, o)],
                      q_send.at[o], q_recv.at[o], partner)

    reverse = ChipScan(chips, chip, core, owners, True, reverse_out, decays, reverse_got,
                       reverse_sent, reverse_home, (a_send, a_recv, b_send, b_recv))
    forward = ChipScan(chips, chip, core, owners, False, forward_out, decays, forward_got,
                       forward_sent, forward_home, (e_send, e_recv, f_send, f_recv))

    def to_keepers(body):
        def one(k):
            o = lax.rem(chip + k, keep.count)

            @pl.when(o != keep.me)
            def _():
                body(o)

        loop(0, keep.count, one)

    def to_holders(body):
        def one(k):
            g = lax.rem(own + k, held)

            @pl.when(g != own_held)
            def _():
                body(g)

        loop(0, held, one)

    pl.semaphore_wait(barrier, group)
    states_over = to_partner(mine.at[other], pair.at[core], 0)
    states_over.start()
    loop(1, dp_count, lambda k: across(lax.rem(dp_me + k, dp_count), dp_me).start())
    pair[core] = mine[core]
    run_rows = nt(decay_parts, upto)
    loads[4].wait()
    to_wide = widen(jnp.exp(overall - run_cols))
    for h in range(2):
        at = slice(h * half, (h + 1) * half)
        scaled = scan_rows[:, at].astype(f32) * to_wide[:, at]
        scaled_scan[h] = scaled
        scaled_mine[h] = scaled.astype(bf16)
    scaled_over = to_partner(scaled_mine.at[other], scaled_got, 1)
    states_over.wait_recv()
    first_decay = pair[0, state_size : state_size + 1]
    last_decay = pair[1, state_size : state_size + 1]
    chip_decay = first_decay * last_decay
    for o in range(owners.count):
        decay_out[o] = chip_decay[:, o * width : (o + 1) * width]
    reverse.to_owners(lambda o: tell(o, chip).start())
    reverse.start(pair[0, :state_size] + first_decay * pair[1, :state_size])
    for d in range(dp_count):
        lend(d, my_rows).start()

    @pl.when(owners.is_me)
    def _():
        decays[chip] = decay_out[owners.me]

    scaled_over.start()
    kernel_sum = jnp.zeros((length, length), f32)

    def kernels(low, high, kernel_sum):
        for h in range(low, high):
            at = slice(h * HEAD_DIM, (h + 1) * HEAD_DIM)
            crossed = nt(scan_rows[:, at], back_rows[:, at])
            spread = run_rows[h : h + 1, :] - run_cols[:, h : h + 1]
            term = jnp.where(causal, jnp.exp(jnp.minimum(spread, 0.0)), 0.0) * crossed
            kernel_mat[h] = term
            kernel_sum += term
        return kernel_sum

    kernel_sum = kernels(0, heads * 3 // 8, kernel_sum)
    for d in range(dp_count):
        input_load(d).wait()
        lend(d, my_rows).wait_recv()
    loop(1, dp_count, lambda k: across(0, lax.rem(dp_me + k, dp_count)).wait_recv())
    some = nt(weights[0], inputs[:, :side])
    for d in range(1, dp_count):
        some += nt(weights[d], inputs[:, d * side : (d + 1) * side])
    for t in range(2):
        write_mine[t] = some[:, t * length : (t + 1) * length]
    write_over = to_partner(write_mine.at[other], write_got, 2)
    write_over.start()

    @pl.when(owners.is_me)
    def _():
        reverse.others(lambda j: tell(0, j).wait_recv())

    reverse.combine()
    kernel_sum = kernels(heads * 3 // 8, heads * 5 // 8, kernel_sum)
    write_over.wait_recv()
    write = write_mine[core] + write_got[...]
    write_rows = write.T.astype(bf16)
    write = repeat(write.astype(bf16), 1)
    for h in range(2):
        front_mine[h] = dot(write, stack_split(scaled_scan[h], 0))
    front_over = to_partner(front_mine.at[other], front.at[core], 3)
    front_over.start()
    front[core] = front_mine[core]
    front_over.wait_recv()
    forward.start(last_decay * front[0] + front[1])
    kernel_sum = kernels(heads * 5 // 8, heads, kernel_sum)
    inner = dot(read_twice, stack_split(kernel_sum.T, 0))
    scaled_over.wait_recv()
    reverse.arrive()
    after[1] = reverse_home[...]
    after[0] = (pair[1, :state_size] + last_decay * reverse_home[...].astype(f32)).astype(bf16)
    grad_mine[core] = nt(after[core], scaled_mine[core]) + inner
    grad_mine[other] = nt(after[other], scaled_got[...])
    grad_over = to_partner(grad_mine, grad_got, 4)
    grad_over.start()
    after_over = to_partner(after.at[other], grad_after.at[core], 5)
    after_over.start()
    grad_after[core] = after[core]
    grad_over.wait_recv()
    grad_half = (grad_mine[...] + grad_got[...]).astype(bf16)
    grad_half = jnp.concatenate([grad_half[0], grad_half[1]], axis=1)
    for d in range(dp_count):
        for o in range(keep.count):
            low = d * side + o * wide
            part[o * dp_count + d] = dot(grad_half, inputs[:, low : low + wide]).astype(bf16)
    to_holders(lambda g: scatter(g, own).start())
    forward.combine()
    read_turned = read_rows[...].astype(f32).T.astype(bf16)
    write_read = jnp.where(row_index < col_index, nt(write_rows, read_turned), 0.0)
    for h in range(heads):
        pairing = kernel_mat[h] * write_read
        row_sums[:, h : h + 1] = jnp.sum(pairing, axis=1, keepdims=True)
        col_sums[h : h + 1, :] = jnp.sum(pairing, axis=0, keepdims=True)
    after_over.wait_recv()
    second = []
    for h in range(2):
        grad_write = jnp.dot(write_rows, grad_after[h], preferred_element_type=f32)
        second.append(per_head(scan_rows[:, h * half : (h + 1) * half].astype(f32) * grad_write))
    overall_rows = run_rows[:, length - 1 :]
    before = repeat((col_index < row_index).astype(f32).astype(bf16), 1, 3)
    onward = repeat(causal.astype(f32).astype(bf16), 1, 3)
    second = (jnp.exp(overall_rows - run_rows) * jnp.concatenate(second, axis=0)
              + row_sums[...].T - col_sums[...])

    def collect(k, running):
        g = lax.rem(own + group - k, group)
        scatter(0, g).wait_recv()
        return running + pieces[g].astype(f32)

    @pl.when(keep.is_me)
    def _():
        total[:, columns(core, keep.me)] = lax.fori_loop(
            1, group, collect, part[own_held].astype(f32)).astype(bf16)
        reverse.others(lambda j: share(j, keep.me).start())
        hand(keep.me, core).start()

    forward.arrive()
    prior[0] = forward_home[...]
    prior[1] = (front[0] + first_decay * forward_home[...].astype(f32)).astype(bf16)
    prior_over = to_partner(prior.at[other], state_before.at[core], 6)
    prior_over.start()
    state_before[core] = prior[core]
    prior_over.wait_recv()
    third, first = [], []
    for h in range(2):
        at = slice(h * half, (h + 1) * half)
        state_read = jnp.dot(read_turned, state_before[h], preferred_element_type=f32)
        third.append(per_head(back_rows[:, at].astype(f32) * state_read))
        both = jnp.sum(grad_after[h].astype(f32) * state_before[h].astype(f32), axis=0,
                       keepdims=True)
        first.append(per_head(jnp.broadcast_to(both, (8, half)))[:, :1])
    decay_grad[...] = (
        jnp.exp(overall_rows) * jnp.concatenate(first, axis=0)
        + nt(stack_split(second, 1, 3), before)
        + nt(stack_split(jnp.exp(run_rows) * jnp.concatenate(third, axis=0), 1, 3), onward)
    )

    def pass_on(o):
        share(chip, o).wait_recv()
        hand(o, core).start()

    to_keepers(pass_on)
    loop(0, keep.count, lambda o: hand(o, other).wait_recv())

    loop(1, dp_count, lambda k: across(lax.rem(dp_me + k, dp_count), 0).wait_send())
    for d in range(dp_count):
        lend(d, my_rows).wait_send()
    for copy in (states_over, scaled_over, write_over, front_over, grad_over, after_over, prior_over):
        copy.wait_send()
    reverse.drain()
    forward.drain()
    reverse.to_owners(lambda o: tell(o, 0).wait_send())
    to_holders(lambda g: scatter(g, 0).wait_send())

    @pl.when(keep.is_me)
    def _():
        reverse.others(lambda j: share(j, 0).wait_send())

    loop(0, keep.count, lambda o: hand(o, core).wait_send())


def dma(*sizes):
    return [pltpu.SemaphoreType.DMA((size,)) for size in sizes for _ in range(2)]


def adam_update(grad_rows, weight_rows, first_rows, second_rows):
    new_first = beta_one * first_rows + (1.0 - beta_one) * grad_rows
    new_second = beta_two * second_rows + (1.0 - beta_two) * grad_rows * grad_rows
    first_hat = new_first / (1.0 - beta_one**adam_count)
    second_hat = new_second / (1.0 - beta_two**adam_count)
    new_weight = weight_rows - learn_rate * (
        first_hat / (jnp.sqrt(second_hat) + epsilon) + weight_decay * weight_rows
    )
    return (new_weight, new_first, new_second)


def on_device(
    layer_input,
    scan_input,
    readout,
    log_decay,
    output_cotangent,
    write_weight,
    first_moment,
    second_moment,
):
    seq_count, dp_count = lax.axis_size("seq"), lax.axis_size("dp")
    input_rows = layer_input[0]
    scan_rows = scan_input[0]
    read_rows = readout[0]
    decay_rows = log_decay[0]
    back_rows = output_cotangent[0]
    length, model = input_rows.shape
    heads = decay_rows.shape[1]
    channels = scan_rows.shape[1]
    state_size = read_rows.shape[1]
    own_rows = write_weight.shape[0]
    width = channels // seq_count

    chips = seq_count // 2
    group = chips * dp_count
    fast = own_rows % (128 * seq_count) == 0 and channels % (128 * seq_count) == 0
    if fast:
        half = channels // 2
        owners = Owners(chips, 0, False).count
        keep = Owners(chips, 0, True).count
        held = keep * dp_count
        lanes = half // owners
        piece = (state_size, own_rows // 2 // keep)
        block = pltpu.VMEM((chips, state_size, lanes), bf16)
        decay_grad, grad_sum = pl.pallas_call(
            functools.partial(one_kernel, seq_count, dp_count),
            out_shape=(
                pltpu.VMEM((heads, length), f32),
                pltpu.VMEM((state_size, own_rows), bf16),
            ),
            in_specs=[pl.BlockSpec(memory_space=pltpu.HBM)] * 6,
            out_specs=[VMEM] * 2,
            scratch_shapes=[
                pltpu.VMEM((heads, length), f32),
                pltpu.VMEM((length, channels), bf16),
                pltpu.VMEM((length, channels), bf16),
                pltpu.VMEM((state_size, length), bf16),
                pltpu.VMEM((state_size, own_rows // 2), f32),
                pltpu.VMEM((2 * length, model // 2), bf16),
                pltpu.VMEM((2, state_size + 8, half), f32),
                pltpu.VMEM((2, state_size + 8, half), f32),
                pltpu.VMEM((2, state_size, half), f32),
                pltpu.VMEM((2, state_size, half), f32),
                pltpu.VMEM((2, length, half), f32),
                pltpu.VMEM((2, length, half), bf16),
                pltpu.VMEM((length, half), bf16),
                pltpu.VMEM((heads, length, length), f32),
                pltpu.VMEM((length, heads), f32),
                pltpu.VMEM((heads, length), f32),
                pltpu.VMEM((dp_count, state_size, own_rows // 2), bf16),
                pltpu.VMEM((2, state_size, length), f32),
                pltpu.VMEM((state_size, length), f32),
                pltpu.VMEM((owners, 1, lanes), f32),
                pltpu.VMEM((chips, 1, lanes), f32),
            ]
            + [pltpu.VMEM((owners, state_size, lanes), bf16), block, block,
               pltpu.VMEM((state_size, half), bf16)] * 2
            + [pltpu.VMEM((2, state_size, half), bf16)] * 4
            + [pltpu.VMEM((2, state_size, length), f32)] * 2
            + [pltpu.VMEM((held,) + piece, bf16), pltpu.VMEM((group,) + piece, bf16)]
            + [pltpu.SemaphoreType.DMA((5,)), pltpu.SemaphoreType.DMA((dp_count,))]
            + dma(dp_count, dp_count, chips, chips, chips, chips, chips, group, chips, keep, 7),
            compiler_params=pltpu.CompilerParams(collective_id=3, has_side_effects=True,
                                                 vmem_limit_bytes=60000000),
            name="whole_step",
        )(write_weight.T, decay_rows.T, scan_rows, back_rows, read_rows.T, input_rows)
        decay_grad = decay_grad.T
        grad_rows = grad_sum.astype(f32).T
    else:
        row_index = lax.broadcasted_iota(jnp.int32, (length, length), 0)
        col_index = lax.broadcasted_iota(jnp.int32, (length, length), 1)
        upto = (col_index <= row_index).astype(f32)
        before = (col_index < row_index).astype(f32)
        running = jnp.dot(upto, decay_rows, precision=highest)
        overall = running[-1]
        to_end = jnp.exp(overall[None, :] - running)
        from_start = jnp.exp(running)
        decay_total = jnp.exp(overall)

        def widen(a):
            return jnp.repeat(a, HEAD_DIM, axis=1)

        scaled_scan = scan_rows.astype(f32) * widen(to_end)
        scaled_back = back_rows.astype(f32) * widen(from_start)

        def state_of(vectors, rows):
            return lax.dot_general(
                vectors.astype(f32), rows, (((0,), (0,)), ((), ())), precision=highest
            ).astype(bf16)

        reverse_local = state_of(read_rows, scaled_back)
        decay_lanes = widen(decay_total[None]).reshape(seq_count, 1, width)
        weight_half = write_weight.T.astype(bf16).reshape(2, state_size // 2, own_rows)
        exchange = [
            pltpu.VMEM((seq_count, state_size, width), bf16),
            pltpu.VMEM((seq_count, state_size, width), bf16),
        ]
        piece = (state_size * own_rows // seq_count // 128, 128)
        scan_split = scan_rows.reshape(length, heads, HEAD_DIM)
        back_split = back_rows.reshape(length, heads, HEAD_DIM)
        crossed = jnp.einsum("thp,shp->hts", scan_split, back_split, preferred_element_type=f32)
        heads_running = running.T
        spread = heads_running[:, None, :] - heads_running[:, :, None]
        kernel_mat = (
            jnp.where((row_index <= col_index)[None], jnp.exp(jnp.minimum(spread, 0.0)), 0.0) * crossed
        )
        weights, decays, grad_after = pl.pallas_call(
            functools.partial(first_kernel, seq_count, dp_count),
            out_shape=(
                jax.ShapeDtypeStruct((dp_count,) + weight_half.shape, bf16),
                jax.ShapeDtypeStruct(decay_lanes.shape, f32),
                jax.ShapeDtypeStruct((state_size, channels), bf16),
            ),
            in_specs=[VMEM] * 3,
            out_specs=[VMEM] * 3,
            scratch_shapes=exchange + dma(dp_count, dp_count, seq_count, seq_count, seq_count),
            compiler_params=pltpu.CompilerParams(collective_id=0, has_side_effects=True),
            name="gather_reverse",
        )(weight_half, reverse_local, decay_lanes)

        weight_all = weights.reshape(dp_count, state_size, own_rows).transpose(1, 0, 2)
        write_half = lax.dot_general(
            input_rows, weight_all.reshape(state_size, model), (((1,), (1,)), ((), ())),
            preferred_element_type=f32,
        ).astype(bf16)
        state_local = state_of(write_half, scaled_scan)
        state_before = pl.pallas_call(
            functools.partial(second_kernel, seq_count),
            out_shape=jax.ShapeDtypeStruct((state_size, channels), bf16),
            in_specs=[VMEM] * 2,
            out_specs=VMEM,
            scratch_shapes=exchange + dma(seq_count, seq_count),
            compiler_params=pltpu.CompilerParams(collective_id=1, has_side_effects=True),
            name="forward_states",
        )(state_local, decays)

        kernel_sum = jnp.sum(kernel_mat, axis=0)
        write_grad = jnp.dot(kernel_sum, read_rows.astype(f32), precision=highest)
        write_grad = write_grad + lax.dot_general(
            scaled_scan.astype(bf16), grad_after, (((1,), (1,)), ((), ())), preferred_element_type=f32
        )
        grad_half = write_grad.astype(bf16)
        partial = lax.dot_general(
            grad_half, input_rows, (((0,), (0,)), ((), ())), preferred_element_type=f32
        ).astype(bf16)
        part = partial.reshape(state_size, dp_count, chips, 2, own_rows // seq_count)
        part = part.transpose(3, 2, 1, 0, 4).reshape((2, chips * dp_count) + piece)
        grad_sum = pl.pallas_call(
            functools.partial(third_kernel, seq_count, dp_count),
            out_shape=jax.ShapeDtypeStruct((seq_count,) + piece, bf16),
            in_specs=[VMEM],
            out_specs=VMEM,
            scratch_shapes=[pltpu.VMEM((chips * dp_count,) + piece, bf16)] * 3
            + dma(chips * dp_count, chips * dp_count, seq_count),
            compiler_params=pltpu.CompilerParams(collective_id=2, has_side_effects=True),
            name="reduce_gradient",
        )(part)
        def per_head(a):
            return jnp.sum(a.reshape(a.shape[0], heads, HEAD_DIM), axis=2)

        term_one = decay_total * jnp.sum(
            per_head(grad_after.astype(f32) * state_before.astype(f32)), axis=0)
        grad_write = jnp.dot(write_half, grad_after, preferred_element_type=f32)
        second_rows = to_end * per_head(scan_rows.astype(f32) * grad_write)
        term_two = jnp.dot(before, second_rows, precision=highest)
        state_read = jnp.dot(read_rows, state_before, preferred_element_type=f32)
        third_rows = from_start * per_head(back_rows.astype(f32) * state_read)
        term_three = jnp.dot(upto.T, third_rows, precision=highest)
        write_read = jnp.dot(write_half, read_rows.T, preferred_element_type=f32)
        pairing = jnp.where((row_index < col_index)[None], kernel_mat * write_read[None], 0.0)
        balance = (jnp.sum(pairing, axis=2) - jnp.sum(pairing, axis=1)).T
        term_four = jnp.dot(before, balance, precision=highest)
        decay_grad = term_one[None, :] + term_two + term_three + term_four
        grad_rows = grad_sum.reshape(seq_count, state_size, own_rows // seq_count)
        grad_rows = grad_rows.transpose(1, 0, 2).reshape(state_size, own_rows).astype(f32).T
    new_weight, new_first, new_second = adam_update(
        grad_rows, write_weight, first_moment, second_moment
    )

    return (decay_grad[None], new_weight, new_first, new_second)


def solution(mesh):
    in_specs = (
        P("dp", "seq", None),
        P("dp", "seq", None),
        P("dp", "seq", None),
        P("dp", "seq", None),
        P("dp", "seq", None),
        P("dp", None),
        P("dp", None),
        P("dp", None),
    )
    out_specs = (P("dp", "seq", None), P("dp", None), P("dp", None), P("dp", None))
    return jax.shard_map(
        on_device, mesh=mesh, in_specs=in_specs, out_specs=out_specs, check_vma=False
    )
```

```python
import functools

import jax
import jax.numpy as jnp
from jax import lax
from jax.experimental import pallas as pl
from jax.experimental.pallas import tpu as pltpu
from jax.sharding import PartitionSpec as P

HEAD_DIM = 64
PARTS = 2

beta_one = 0.9
beta_two = 0.999
adam_count = 10.0
learn_rate = 0.01
weight_decay = 0.1
epsilon = 1e-08
highest = lax.Precision.HIGHEST
f32 = jnp.float32
bf16 = jnp.bfloat16
MESH = pl.DeviceIdType.MESH
REVERSE_OUT, REVERSE_HOME = bf16, bf16
FORWARD_OUT, FORWARD_HOME = bf16, bf16
VMEM = pl.BlockSpec(memory_space=pltpu.VMEM)


def remote(src, dst, send_sem, recv_sem, where):
    return pltpu.make_async_remote_copy(
        src_ref=src, dst_ref=dst, send_sem=send_sem, recv_sem=recv_sem, device_id=where,
        device_id_type=MESH,
    )


def loop(low, high, body):
    lax.fori_loop(low, high, lambda i, carry: (body(i), carry)[1], 0)


class Scan:
    def __init__(self, count, me, local, decay, gathered, sent, result, sems):
        self.count, self.me = count, me
        self.local, self.decay, self.gathered, self.sent, self.result = (
            local, decay, gathered, sent, result)
        self.width = local.shape[1] // count
        self.out_send, self.out_recv, self.back_send, self.back_recv = sems

    def columns(self, place):
        return pl.ds(pl.multiple_of(place * self.width, self.width), self.width)

    def outward(self, j, source):
        return remote(self.local.at[:, self.columns(j)], self.gathered.at[source],
                      self.out_send.at[j], self.out_recv.at[source], {"seq": j})

    def homeward(self, i, owner):
        return remote(self.sent.at[i], self.result.at[:, self.columns(owner)],
                      self.back_send.at[i], self.back_recv.at[owner], {"seq": i})

    def start(self):
        loop(1, self.count,
             lambda k: self.outward(lax.rem(self.me + k, self.count), self.me).start())
        self.gathered[self.me] = self.local[:, self.columns(self.me)]

    def combine(self, reverse):
        count, me = self.count, self.me

        def one(k, running):
            i = count - 1 - k if reverse else k

            @pl.when(i != me)
            def _():
                self.outward(i, i).wait_recv()

            self.sent[i] = running.astype(bf16)
            new = self.decay[i] * running + self.gathered[i].astype(f32)

            @pl.when(i != me)
            def _():
                self.homeward(i, me).start()

            return new

        lax.fori_loop(0, count, one, jnp.zeros(self.gathered.shape[1:], f32))
        self.result[:, self.columns(me)] = self.sent[me]

    def arrive(self):
        def one(k):
            j = lax.rem(self.me + k, self.count)
            self.homeward(j, j).wait_recv()

        loop(1, self.count, one)

    def drain(self):
        def one(k):
            j = lax.rem(self.me + k, self.count)
            self.outward(j, j).wait_send()
            self.homeward(j, j).wait_send()

        loop(1, self.count, one)

    def finish(self):
        self.arrive()
        self.drain()


def greet(seq_count, dp_count, same_core):
    seq_me, dp_me = lax.axis_index("seq"), lax.axis_index("dp")
    barrier = pltpu.get_barrier_semaphore()
    loop(1, seq_count, lambda k: pl.semaphore_signal(
        barrier, inc=1, device_id={"seq": lax.rem(seq_me + k, seq_count)}, device_id_type=MESH))
    total = seq_count - 1
    places = seq_count // 2 if same_core else 1

    def over(k):
        d = lax.rem(dp_me + 1 + k // places, dp_count)
        s = lax.rem(seq_me + 2 * (k % places), seq_count)
        pl.semaphore_signal(barrier, inc=1, device_id={"seq": s, "dp": d}, device_id_type=MESH)

    loop(0, (dp_count - 1) * places, over)
    return lambda: pl.semaphore_wait(barrier, total + (dp_count - 1) * places)


def first_kernel(seq_count, dp_count, weight, local, decay, weights, decays, result,
                 gathered, sent, w_send, w_recv, p_send, p_recv, d_send, d_recv,
                 a_send, a_recv, b_send, b_recv):
    seq_me, dp_me = lax.axis_index("seq"), lax.axis_index("dp")
    core = lax.rem(seq_me, 2)
    partner = seq_me + 1 - 2 * core
    greet(seq_count, dp_count, False)()

    def across(d, source):
        return remote(weight.at[core], weights.at[source, core], w_send.at[d], w_recv.at[source],
                      {"dp": d})

    def beside(d, half):
        return remote(weights.at[d, half], weights.at[d, half], p_send.at[d], p_recv.at[d],
                      {"seq": partner})

    def tell(j, source):
        return remote(decay.at[j], decays.at[source], d_send.at[j], d_recv.at[source], {"seq": j})

    loop(1, dp_count, lambda k: across(lax.rem(dp_me + k, dp_count), dp_me).start())
    loop(1, seq_count, lambda k: tell(lax.rem(seq_me + k, seq_count), seq_me).start())
    scan = Scan(seq_count, seq_me, local, decays, gathered, sent, result,
                (a_send, a_recv, b_send, b_recv))
    scan.start()
    decays[seq_me] = decay[seq_me]
    weights[dp_me] = weight[...]

    def told(k):
        j = lax.rem(seq_me + k, seq_count)
        tell(j, j).wait_recv()

    loop(1, seq_count, told)

    def pass_on(k):
        d = lax.rem(dp_me + k, dp_count)
        across(d, d).wait_recv()
        beside(d, core).start()

    loop(1, dp_count, pass_on)
    scan.combine(True)

    def end(k):
        d = lax.rem(dp_me + k, dp_count)
        across(d, d).wait_send()
        beside(d, core).wait_send()
        beside(d, 1 - core).wait_recv()

    loop(1, dp_count, end)
    loop(1, seq_count, lambda k: tell(lax.rem(seq_me + k, seq_count), 0).wait_send())
    scan.finish()


def second_kernel(seq_count, local, decays, result, gathered, sent, a_send, a_recv, b_send, b_recv):
    greet(seq_count, 1, False)()
    scan = Scan(seq_count, lax.axis_index("seq"), local, decays, gathered, sent, result,
                (a_send, a_recv, b_send, b_recv))
    scan.start()
    scan.combine(False)
    scan.finish()


def third_kernel(seq_count, dp_count, part, total, halves, summed, pieces,
                 h_send, h_recv, s_send, s_recv, g_send, g_recv):
    seq_me, dp_me = lax.axis_index("seq"), lax.axis_index("dp")
    core = lax.rem(seq_me, 2)
    chip = seq_me // 2
    partner = seq_me + 1 - 2 * core
    group = (seq_count // 2) * dp_count
    mine = chip * dp_count + dp_me
    greet(seq_count, dp_count, True)()

    def half(g):
        return remote(part.at[1 - core, g], halves.at[g], h_send.at[g], h_recv.at[g],
                      {"seq": partner})

    def scatter(g, source):
        return remote(summed.at[g], pieces.at[source], s_send.at[g], s_recv.at[source],
                      {"seq": 2 * (g // dp_count) + core, "dp": g % dp_count})

    def share(j, source):
        return remote(total.at[seq_me], total.at[source], g_send.at[j], g_recv.at[source],
                      {"seq": j})

    loop(1, group + 1, lambda k: half(lax.rem(mine + k, group)).start())

    def pair(k):
        g = lax.rem(mine + k, group)
        half(g).wait_recv()
        summed[g] = (part[core, g].astype(f32) + halves[g].astype(f32)).astype(bf16)

        @pl.when(g != mine)
        def _():
            scatter(g, mine).start()

    loop(1, group + 1, pair)

    def collect(k, running):
        g = lax.rem(mine + group - k, group)
        scatter(g, g).wait_recv()
        return running + pieces[g].astype(f32)

    own = part[core, mine].astype(f32) + halves[mine].astype(f32)
    total[seq_me] = lax.fori_loop(1, group, collect, own).astype(bf16)
    loop(1, seq_count, lambda k: share(lax.rem(seq_me + k, seq_count), seq_me).start())

    def end(k):
        j = lax.rem(seq_me + seq_count - k, seq_count)
        share(j, j).wait_recv()
        share(j, j).wait_send()

    loop(1, group + 1, lambda k: half(lax.rem(mine + k, group)).wait_send())
    loop(1, group, lambda k: scatter(lax.rem(mine + k, group), 0).wait_send())
    loop(1, seq_count, end)


def nt(a, b):
    return lax.dot_general(a, b, (((1,), (1,)), ((), ())), preferred_element_type=f32)


def split(a):
    high = a.astype(bf16)
    return high, (a - high.astype(f32)).astype(bf16)


def exact(a, b):
    return lax.dot_general(a, b, (((1,), (1,)), ((), ())), precision=highest)


def stack_split(a, axis, parts=2):
    pieces, rest = [], a
    for _ in range(parts):
        pieces.append(rest.astype(bf16))
        rest = rest - pieces[-1].astype(f32)
    return jnp.concatenate(pieces, axis=axis)


def repeat(a, axis, parts=2):
    return jnp.concatenate([a] * parts, axis=axis)


def dot(a, b):
    return jnp.dot(a, b, preferred_element_type=f32)


class Owners:
    def __init__(self, chips, chip, mid=True):
        self.count = chips // 2 if mid and chips % 4 == 0 else chips
        self.base = (chips - self.count) // 2
        self.me = chip - self.base
        self.is_me = (self.me >= 0) & (self.me < self.count)

    def chip(self, o):
        return self.base + o


class ChipScan:
    def __init__(self, count, chip, core, owners, reverse, local, decays, gathered, sent, result,
                 sems):
        self.count, self.chip, self.core, self.owners, self.reverse = (
            count, chip, core, owners, reverse)
        self.local, self.decays, self.gathered, self.sent, self.result = (
            local, decays, gathered, sent, result)
        self.width = local.shape[2]
        self.out_send, self.out_recv, self.back_send, self.back_recv = sems
        self.head, self.tail = (count - 1, 0) if reverse else (0, count - 1)

    def columns(self, o):
        return pl.ds(pl.multiple_of(o * self.width, self.width), self.width)

    def outward(self, o, source):
        return remote(self.local.at[o], self.gathered.at[source], self.out_send.at[o],
                      self.out_recv.at[source], {"seq": 2 * self.owners.chip(o) + self.core})

    def homeward(self, i, o):
        return remote(self.sent.at[i], self.result.at[:, self.columns(o)],
                      self.back_send.at[i], self.back_recv.at[o], {"seq": 2 * i + self.core})

    def to_owners(self, body):
        def one(k):
            o = lax.rem(self.chip + k, self.owners.count)

            @pl.when(o != self.owners.me)
            def _():
                body(o)

        loop(0, self.owners.count, one)

    def others(self, body):
        loop(1, self.count, lambda k: body(lax.rem(self.chip + k, self.count)))

    def start(self, total):
        for o in range(self.owners.count):
            self.local[o] = total[:, o * self.width : (o + 1) * self.width].astype(self.local.dtype)

        @pl.when(self.chip != self.tail)
        def _():
            self.to_owners(lambda o: self.outward(o, self.chip).start())

        @pl.when(self.owners.is_me)
        def _():
            self.gathered[self.chip] = self.local[self.owners.me]

    def combine(self, visit):
        def one(k, running):
            i = self.count - 1 - k if self.reverse else k

            @pl.when((i != self.chip) & (i != self.tail))
            def _():
                self.outward(0, i).wait_recv()

            self.sent[i] = running.astype(self.sent.dtype)

            @pl.when((i != self.chip) & (i != self.head))
            def _():
                self.homeward(i, self.owners.me).start()

            visit(i, running)
            if k == self.count - 1:
                return running
            return self.decays[i] * running + self.gathered[i].astype(f32)

        @pl.when(self.owners.is_me)
        def _():
            running = jnp.zeros(self.gathered.shape[1:], f32)
            for k in range(self.count):
                running = one(k, running)
            self.result[:, self.columns(self.owners.me)] = self.sent[self.chip]

    def arrive(self):
        @pl.when(self.chip != self.head)
        def _():
            self.to_owners(lambda o: self.homeward(self.chip, o).wait_recv())

        @pl.when(self.chip == self.head)
        def _():
            self.result[...] = jnp.zeros_like(self.result)

    def drain(self):
        @pl.when(self.chip != self.tail)
        def _():
            self.to_owners(lambda o: self.outward(o, 0).wait_send())

        def one(j):
            @pl.when(j != self.head)
            def _():
                self.homeward(j, 0).wait_send()

        @pl.when(self.owners.is_me)
        def _():
            self.others(one)


def one_kernel(seq_count, dp_count, weight_hbm, log_decay_hbm, scan_hbm, back_hbm, read_hbm,
               input_hbm, first_hbm, second_hbm, decay_grad, total, weight_out, first_out, second_out,
               log_decay, scan_rows, back_rows, read_rows, weight_rows, inputs,
               mine, pair, front_mine, front, scaled_scan, scaled_mine, scaled_got,
               kernel_mat, row_sums, col_sums, weights, write_mine, write_got,
               decay_out, decays, reverse_out, reverse_got, reverse_sent, reverse_home,
               forward_out, forward_got, forward_sent, forward_home,
               after, grad_after, prior, state_before, grad_mine, grad_got,
               part, pieces, kept, meet_out, meet_home,
               load_sem, input_sem, pass_sem, l_send, l_recv, w_send, w_recv, d_send, d_recv,
               a_send, a_recv, b_send, b_recv, e_send, e_recv, f_send, f_recv,
               t_send, t_recv, m_send, m_recv, s_send, s_recv, g_send, g_recv, q_send, q_recv):
    seq_me, dp_me = lax.axis_index("seq"), lax.axis_index("dp")
    core = lax.rem(seq_me, 2)
    other = 1 - core
    chip = seq_me // 2
    chips = seq_count // 2
    partner = {"seq": seq_me + 1 - 2 * core}
    group = chips * dp_count
    own = chip * dp_count + dp_me

    owners = Owners(chips, chip, False)
    keep = Owners(chips, chip, True)
    held = keep.count * dp_count
    own_held = keep.me * dp_count + dp_me

    def place(g):
        return {"seq": 2 * (g // dp_count) + core, "dp": lax.rem(g, dp_count)}

    barrier = pltpu.get_barrier_semaphore()
    pl.semaphore_signal(barrier, inc=1, device_id=partner, device_id_type=MESH)
    loop(1, group, lambda k: pl.semaphore_signal(
        barrier, inc=1, device_id=place(lax.rem(own + k, group)), device_id_type=MESH))

    length, channels = scan_rows.shape
    half = channels // 2
    heads = channels // HEAD_DIM
    half_heads = heads // 2
    state_size = read_rows.shape[0]
    own_rows = weight_hbm.shape[1]
    side = own_rows // 2
    width = half // owners.count
    wide = side // keep.count

    def span(start, size):
        return pl.ds(pl.multiple_of(start, 128), size)

    loads = [
        pltpu.make_async_copy(log_decay_hbm, log_decay, load_sem.at[0]),
        pltpu.make_async_copy(back_hbm, back_rows, load_sem.at[1]),
        pltpu.make_async_copy(read_hbm, read_rows, load_sem.at[2]),
        pltpu.make_async_copy(weight_hbm.at[:, span(core * side, side)], weight_rows,
                              load_sem.at[3]),
        pltpu.make_async_copy(scan_hbm, scan_rows, load_sem.at[4]),
    ]
    for copy in loads:
        copy.start()
    my_rows = pl.ds(pl.multiple_of(core * length, length), length)

    def input_load(d):
        return pltpu.make_async_copy(
            input_hbm.at[:, span(d * own_rows + core * side, side)],
            inputs.at[my_rows, d * side : (d + 1) * side], input_sem.at[d])

    for d in range(dp_count):
        input_load(d).start()

    passed = [
        pltpu.make_async_copy(src, dst, pass_sem.at[i])
        for i, (src, dst) in enumerate(
            ((weight_hbm, weight_out), (first_hbm, first_out), (second_hbm, second_out)))
    ]
    row_index = lax.broadcasted_iota(jnp.int32, (length, length), 0)
    col_index = lax.broadcasted_iota(jnp.int32, (length, length), 1)
    causal = row_index <= col_index
    upto = repeat((col_index <= row_index).astype(f32).astype(bf16), 1, 3)
    owner = lax.broadcasted_iota(jnp.int32, (heads, channels), 0)
    spot = lax.broadcasted_iota(jnp.int32, (heads, channels), 1) - owner * HEAD_DIM
    member = ((spot >= 0) & (spot < HEAD_DIM)).astype(bf16)
    half_member = member[:half_heads, :half]
    member = repeat(member, 0)

    def widen(a):
        return dot(stack_split(a, 1), member)

    def per_head(a):
        high, low = split(a)
        return nt(half_member, high) + nt(half_member, low)

    loads[0].wait()
    decay_parts = stack_split(log_decay[...], 1, 3)
    run_cols = nt(upto, decay_parts)
    overall = run_cols[length - 1 :, :]
    from_wide = widen(jnp.exp(run_cols))
    decay_wide = from_wide[length - 1 :, :]
    loads[1].wait()
    loads[2].wait()
    read_twice = repeat(read_rows[...], 1)
    for h in range(2):
        at = slice(h * half, (h + 1) * half)
        scaled = back_rows[:, at].astype(f32) * from_wide[:, at]
        mine[h, :state_size] = dot(read_twice, stack_split(scaled, 0))
        mine[h, state_size:] = jnp.broadcast_to(decay_wide[:, at], (8, half))
    loads[3].wait()
    weights[dp_me] = weight_rows[...].astype(bf16)

    def to_partner(src, dst, place):
        return remote(src, dst, m_send.at[place], m_recv.at[place], partner)

    def across(d, source):
        return remote(weights.at[dp_me], weights.at[source], w_send.at[d], w_recv.at[source],
                      {"dp": d})

    def lend(d, rows):
        return remote(input_hbm.at[:, span(d * own_rows + other * side, side)],
                      inputs.at[rows, d * side : (d + 1) * side],
                      l_send.at[d], l_recv.at[d], partner)

    def tell(o, source):
        return remote(decay_out.at[o], decays.at[source], d_send.at[o], d_recv.at[source],
                      {"seq": 2 * owners.chip(o) + core})

    parts = part.shape[0]
    rows = state_size // parts

    def scatter(g, source, n):
        return remote(part.at[n, g], pieces.at[n, source], s_send.at[n, g], s_recv.at[n, source],
                      place(keep.base * dp_count + g))

    def columns(side_of, o):
        return span(side_of * side + o * wide, wide)

    def meeting(i, o):
        return remote(meet_out.at[i], meet_home.at[o], t_send.at[i], t_recv.at[o],
                      {"seq": 2 * i + core})

    def share(j, o, n):
        spot = total.at[n * rows : (n + 1) * rows, columns(core, o)]
        return remote(spot, spot, g_send.at[n, j], g_recv.at[n, o], {"seq": 2 * j + core})

    def hand(o, from_core, n):
        spot = total.at[n * rows : (n + 1) * rows, columns(from_core, o)]
        return remote(spot, spot, q_send.at[n, o], q_recv.at[n, o], partner)

    reverse = ChipScan(chips, chip, core, owners, True, reverse_out, decays, reverse_got,
                       reverse_sent, reverse_home, (a_send, a_recv, b_send, b_recv))
    forward = ChipScan(chips, chip, core, owners, False, forward_out, decays, forward_got,
                       forward_sent, forward_home, (e_send, e_recv, f_send, f_recv))

    def to_keepers(body):
        def one(k):
            o = lax.rem(chip + k, keep.count)

            @pl.when(o != keep.me)
            def _():
                body(o)

        loop(0, keep.count, one)

    def to_holders(body):
        def one(k):
            g = lax.rem(own + k, held)

            @pl.when(g != own_held)
            def _():
                body(g)

        loop(0, held, one)

    pl.semaphore_wait(barrier, group)
    states_over = to_partner(mine.at[other], pair.at[core], 0)
    states_over.start()
    loop(1, dp_count, lambda k: across(lax.rem(dp_me + k, dp_count), dp_me).start())
    pair[core] = mine[core]
    run_rows = nt(decay_parts, upto)
    loads[4].wait()
    to_wide = widen(jnp.exp(overall - run_cols))
    for h in range(2):
        at = slice(h * half, (h + 1) * half)
        scaled = scan_rows[:, at].astype(f32) * to_wide[:, at]
        scaled_scan[h] = scaled
        scaled_mine[h] = scaled.astype(bf16)
    scaled_over = to_partner(scaled_mine.at[other], scaled_got, 1)
    states_over.wait_recv()
    first_decay = pair[0, state_size : state_size + 1]
    last_decay = pair[1, state_size : state_size + 1]
    chip_decay = first_decay * last_decay
    for o in range(owners.count):
        decay_out[o] = chip_decay[:, o * width : (o + 1) * width]
    reverse.to_owners(lambda o: tell(o, chip).start())
    reverse.start(pair[0, :state_size] + first_decay * pair[1, :state_size])
    for d in range(dp_count):
        lend(d, my_rows).start()

    @pl.when(owners.is_me)
    def _():
        decays[chip] = decay_out[owners.me]

    scaled_over.start()
    for copy in passed:
        copy.start()
    kernel_sum = jnp.zeros((length, length), f32)

    def kernels(low, high, kernel_sum):
        for h in range(low, high):
            at = slice(h * HEAD_DIM, (h + 1) * HEAD_DIM)
            crossed = nt(scan_rows[:, at], back_rows[:, at])
            spread = run_rows[h : h + 1, :] - run_cols[:, h : h + 1]
            term = jnp.where(causal, jnp.exp(jnp.minimum(spread, 0.0)), 0.0) * crossed
            kernel_mat[h] = term
            kernel_sum += term
        return kernel_sum

    kernel_sum = kernels(0, heads * 3 // 8, kernel_sum)
    for d in range(dp_count):
        input_load(d).wait()
        lend(d, my_rows).wait_recv()
    loop(1, dp_count, lambda k: across(0, lax.rem(dp_me + k, dp_count)).wait_recv())
    some = nt(weights[0], inputs[:, :side])
    for d in range(1, dp_count):
        some += nt(weights[d], inputs[:, d * side : (d + 1) * side])
    for t in range(2):
        write_mine[t] = some[:, t * length : (t + 1) * length]
    write_over = to_partner(write_mine.at[other], write_got, 2)
    write_over.start()

    @pl.when(owners.is_me)
    def _():
        reverse.others(lambda j: tell(0, j).wait_recv())


    def keep_after(i, running):
        kept[i] = running

    reverse.combine(keep_after)
    kernel_sum = kernels(heads * 3 // 8, heads * 5 // 8, kernel_sum)
    write_over.wait_recv()
    write = write_mine[core] + write_got[...]
    write_rows = write.T.astype(bf16)
    write = repeat(write.astype(bf16), 1)
    for h in range(2):
        front_mine[h] = dot(write, stack_split(scaled_scan[h], 0))
    front_over = to_partner(front_mine.at[other], front.at[core], 3)
    front_over.start()
    front[core] = front_mine[core]
    front_over.wait_recv()
    forward.start(last_decay * front[0] + front[1])
    kernel_sum = kernels(heads * 5 // 8, heads, kernel_sum)
    inner = dot(read_twice, stack_split(kernel_sum.T, 0))
    scaled_over.wait_recv()
    reverse.arrive()
    after[1] = reverse_home[...].astype(f32)
    after[0] = pair[1, :state_size] + last_decay * reverse_home[...].astype(f32)
    grad_mine[core] = nt(after[core].astype(bf16), scaled_mine[core]) + inner
    grad_mine[other] = nt(after[other].astype(bf16), scaled_got[...])
    grad_over = to_partner(grad_mine, grad_got, 4)
    grad_over.start()
    after_over = to_partner(after.at[other], grad_after.at[core], 5)
    grad_over.wait_recv()
    after_over.start()
    grad_after[core] = after[core]
    grad_half = (grad_mine[...] + grad_got[...]).astype(bf16)
    grad_half = jnp.concatenate([grad_half[0], grad_half[1]], axis=1)
    for k in range(held):
        g = lax.rem(own + k, held)
        low = lax.rem(g, dp_count) * side + g // dp_count * wide
        term = dot(grad_half, inputs[:, span(low, wide)]).astype(bf16)
        for n in range(parts):
            part[n, g] = term[n * rows : (n + 1) * rows]

        @pl.when(g != own_held)
        def _():
            scatter(g, own, 0).start()

    for n in range(1, parts):
        to_holders(lambda g: scatter(g, own, n).start())
    def meet(i, running):
        meet_out[i] = jnp.sum(kept[i] * running, axis=0, keepdims=True)

        @pl.when(i != chip)
        def _():
            meeting(i, owners.me).start()

    forward.combine(meet)

    @pl.when(owners.is_me)
    def _():
        meet_home[owners.me] = meet_out[chip]

    read_turned = read_rows[...].astype(f32).T.astype(bf16)
    write_read = jnp.where(row_index < col_index, nt(write_rows, read_turned), 0.0)
    for h in range(heads):
        pairing = kernel_mat[h] * write_read
        row_sums[:, h : h + 1] = jnp.sum(pairing, axis=1, keepdims=True)
        col_sums[h : h + 1, :] = jnp.sum(pairing, axis=0, keepdims=True)
    after_over.wait_recv()
    second = []
    for h in range(2):
        grad_write = dot(repeat(write_rows, 1), stack_split(grad_after[h], 0))
        second.append(per_head(scan_rows[:, h * half : (h + 1) * half].astype(f32) * grad_write))
    overall_rows = run_rows[:, length - 1 :]
    before = repeat((col_index < row_index).astype(f32).astype(bf16), 1, 3)
    onward = repeat(causal.astype(f32).astype(bf16), 1, 3)
    second = (jnp.exp(overall_rows - run_rows) * jnp.concatenate(second, axis=0)
              + row_sums[...].T - col_sums[...])

    @pl.when(keep.is_me)
    def _():
        for n in range(parts):
            def collect(k, running):
                g = lax.rem(own + group - k, group)
                scatter(0, g, n).wait_recv()
                return running + pieces[n, g].astype(f32)

            total[n * rows : (n + 1) * rows, columns(core, keep.me)] = lax.fori_loop(
                1, group, collect, part[n, own_held].astype(f32)).astype(bf16)
            reverse.others(lambda j: share(j, keep.me, n).start())
            hand(keep.me, core, n).start()

    forward.arrive()
    reverse.to_owners(lambda o: meeting(chip, o).wait_recv())
    met = jnp.concatenate([meet_home[o] for o in range(owners.count)], axis=1)
    came = forward_home[...].astype(f32)
    both = (last_decay * met + jnp.sum(pair[1, :state_size] * came, axis=0, keepdims=True),
            first_decay * met + jnp.sum(after[1] * front[0], axis=0, keepdims=True))
    prior[0, :state_size] = came
    prior[1, :state_size] = front[0] + first_decay * came
    for t in range(2):
        prior[t, state_size:] = jnp.broadcast_to(both[t], (8, half))
    prior_over = to_partner(prior.at[other], state_before.at[core], 6)
    prior_over.start()
    state_before[core] = prior[core]
    prior_over.wait_recv()
    third, first = [], []
    for h in range(2):
        at = slice(h * half, (h + 1) * half)
        state_read = dot(repeat(read_turned, 1), stack_split(state_before[h, :state_size], 0))
        third.append(per_head(back_rows[:, at].astype(f32) * state_read))
        first.append(per_head(state_before[h, state_size:])[:, :1])
    decay_grad[...] = (
        jnp.exp(overall_rows) * jnp.concatenate(first, axis=0)
        + nt(stack_split(second, 1, 3), before)
        + nt(stack_split(jnp.exp(run_rows) * jnp.concatenate(third, axis=0), 1, 3), onward)
    )

    for n in range(parts):
        def pass_on(o):
            share(chip, o, n).wait_recv()
            hand(o, core, n).start()

        to_keepers(pass_on)
    for n in range(parts):
        loop(0, keep.count, lambda o: hand(o, other, n).wait_recv())

    for copy in passed:
        copy.wait()
    loop(1, dp_count, lambda k: across(lax.rem(dp_me + k, dp_count), 0).wait_send())
    for d in range(dp_count):
        lend(d, my_rows).wait_send()
    for copy in (states_over, scaled_over, write_over, front_over, grad_over, after_over, prior_over):
        copy.wait_send()
    reverse.drain()
    forward.drain()

    @pl.when(owners.is_me)
    def _():
        reverse.others(lambda j: meeting(j, 0).wait_send())

    reverse.to_owners(lambda o: tell(o, 0).wait_send())
    for n in range(parts):
        to_holders(lambda g: scatter(g, 0, n).wait_send())

        @pl.when(keep.is_me)
        def _():
            reverse.others(lambda j: share(j, 0, n).wait_send())

        loop(0, keep.count, lambda o: hand(o, core, n).wait_send())


def dma(*sizes):
    shapes = [size if isinstance(size, tuple) else (size,) for size in sizes]
    return [pltpu.SemaphoreType.DMA(shape) for shape in shapes for _ in range(2)]


def adam_update(grad_rows, weight_rows, first_rows, second_rows):
    new_first = beta_one * first_rows + (1.0 - beta_one) * grad_rows
    new_second = beta_two * second_rows + (1.0 - beta_two) * grad_rows * grad_rows
    first_hat = new_first / (1.0 - beta_one**adam_count)
    second_hat = new_second / (1.0 - beta_two**adam_count)
    new_weight = weight_rows - learn_rate * (
        first_hat / (jnp.sqrt(second_hat) + epsilon) + weight_decay * weight_rows
    )
    return (new_weight, new_first, new_second)


def update_kernel(steps, decay, grad, weight, first, second, decay_out, weight_out, first_out,
                  second_out, new_weight, new_first, new_second, out_sem, decay_sem):
    decay_copy = pltpu.make_async_copy(decay, decay_out, decay_sem)
    decay_copy.start()
    size = grad.shape[1] // steps
    copies = []
    for step in range(steps):
        at = slice(step * size, (step + 1) * size)
        results = adam_update(grad[:, at].astype(f32), weight[:, at], first[:, at], second[:, at])
        for i, (value, held, out) in enumerate(zip(
                results, (new_weight, new_first, new_second),
                (weight_out, first_out, second_out))):
            held[:, at] = value
            copies.append(pltpu.make_async_copy(held.at[:, at], out.at[:, at], out_sem.at[i, step]))
            copies[-1].start()
    decay_copy.wait()
    for copy in copies:
        copy.wait()


def on_device(
    layer_input,
    scan_input,
    readout,
    log_decay,
    output_cotangent,
    write_weight,
    first_moment,
    second_moment,
):
    seq_count, dp_count = lax.axis_size("seq"), lax.axis_size("dp")
    input_rows = layer_input[0]
    scan_rows = scan_input[0]
    read_rows = readout[0]
    decay_rows = log_decay[0]
    back_rows = output_cotangent[0]
    length, model = input_rows.shape
    heads = decay_rows.shape[1]
    channels = scan_rows.shape[1]
    state_size = read_rows.shape[1]
    own_rows = write_weight.shape[0]
    width = channels // seq_count

    chips = seq_count // 2
    group = chips * dp_count
    fast = own_rows % (128 * seq_count) == 0 and channels % (128 * seq_count) == 0
    if fast:
        half = channels // 2
        owners = Owners(chips, 0, False).count
        keep = Owners(chips, 0, True).count
        held = keep * dp_count
        lanes = half // owners
        parts = PARTS if state_size % (16 * PARTS) == 0 else 1
        piece = (state_size // parts, own_rows // 2 // keep)
        results = pl.pallas_call(
            functools.partial(one_kernel, seq_count, dp_count),
            out_shape=(
                pltpu.VMEM((heads, length), f32),
                pltpu.VMEM((state_size, own_rows), bf16),
            ) + (pltpu.VMEM((state_size, own_rows), f32),) * 3,
            in_specs=[pl.BlockSpec(memory_space=pltpu.HBM)] * 8,
            out_specs=[VMEM] * 5,
            scratch_shapes=[
                pltpu.VMEM((heads, length), f32),
                pltpu.VMEM((length, channels), bf16),
                pltpu.VMEM((length, channels), bf16),
                pltpu.VMEM((state_size, length), bf16),
                pltpu.VMEM((state_size, own_rows // 2), f32),
                pltpu.VMEM((2 * length, model // 2), bf16),
                pltpu.VMEM((2, state_size + 8, half), f32),
                pltpu.VMEM((2, state_size + 8, half), f32),
                pltpu.VMEM((2, state_size, half), f32),
                pltpu.VMEM((2, state_size, half), f32),
                pltpu.VMEM((2, length, half), f32),
                pltpu.VMEM((2, length, half), bf16),
                pltpu.VMEM((length, half), bf16),
                pltpu.VMEM((heads, length, length), f32),
                pltpu.VMEM((length, heads), f32),
                pltpu.VMEM((heads, length), f32),
                pltpu.VMEM((dp_count, state_size, own_rows // 2), bf16),
                pltpu.VMEM((2, state_size, length), f32),
                pltpu.VMEM((state_size, length), f32),
                pltpu.VMEM((owners, 1, lanes), f32),
                pltpu.VMEM((chips, 1, lanes), f32),
            ]
            + [pltpu.VMEM(shape, kind)
               for out_kind, home_kind in ((REVERSE_OUT, REVERSE_HOME), (FORWARD_OUT, FORWARD_HOME))
               for shape, kind in (
                   ((owners, state_size, lanes), out_kind), ((chips, state_size, lanes), out_kind),
                   ((chips, state_size, lanes), home_kind), ((state_size, half), home_kind))]
            + [pltpu.VMEM((2, state_size, half), f32)] * 2
            + [pltpu.VMEM((2, state_size + 8, half), f32)] * 2
            + [pltpu.VMEM((2, state_size, length), f32)] * 2
            + [pltpu.VMEM((parts, held) + piece, bf16), pltpu.VMEM((parts, group) + piece, bf16),
               pltpu.VMEM((chips, state_size, lanes), f32), pltpu.VMEM((chips, 1, lanes), f32),
               pltpu.VMEM((owners, 1, lanes), f32)]
            + [pltpu.SemaphoreType.DMA((5,)), pltpu.SemaphoreType.DMA((dp_count,)),
               pltpu.SemaphoreType.DMA((3,))]
            + dma(dp_count, dp_count, chips, chips, chips, chips, chips, chips, 7, (parts, group), (parts, chips), (parts, keep)),
            compiler_params=pltpu.CompilerParams(collective_id=3, has_side_effects=True,
                                                 vmem_limit_bytes=60000000),
            name="whole_step",
        )(write_weight.T, decay_rows.T, scan_rows, back_rows, read_rows.T, input_rows,
          first_moment.T, second_moment.T)
        steps = 4
        decay_grad, new_weight, new_first, new_second = pl.pallas_call(
            functools.partial(update_kernel, steps),
            out_shape=(jax.ShapeDtypeStruct((heads, length), f32),)
            + (jax.ShapeDtypeStruct((state_size, own_rows), f32),) * 3,
            in_specs=[VMEM] * 5,
            out_specs=[pl.BlockSpec(memory_space=pltpu.HBM)] * 4,
            scratch_shapes=[pltpu.VMEM((state_size, own_rows), f32)] * 3
            + [pltpu.SemaphoreType.DMA((3, steps)), pltpu.SemaphoreType.DMA],
            compiler_params=pltpu.CompilerParams(vmem_limit_bytes=16 * 2**20),
            name="update",
        )(*results)
        return decay_grad.T[None], new_weight.T, new_first.T, new_second.T
    else:
        row_index = lax.broadcasted_iota(jnp.int32, (length, length), 0)
        col_index = lax.broadcasted_iota(jnp.int32, (length, length), 1)
        upto = (col_index <= row_index).astype(f32)
        before = (col_index < row_index).astype(f32)
        running = jnp.dot(upto, decay_rows, precision=highest)
        overall = running[-1]
        to_end = jnp.exp(overall[None, :] - running)
        from_start = jnp.exp(running)
        decay_total = jnp.exp(overall)

        def widen(a):
            return jnp.repeat(a, HEAD_DIM, axis=1)

        scaled_scan = scan_rows.astype(f32) * widen(to_end)
        scaled_back = back_rows.astype(f32) * widen(from_start)

        def state_of(vectors, rows):
            return lax.dot_general(
                vectors.astype(f32), rows, (((0,), (0,)), ((), ())), precision=highest
            ).astype(bf16)

        reverse_local = state_of(read_rows, scaled_back)
        decay_lanes = widen(decay_total[None]).reshape(seq_count, 1, width)
        weight_half = write_weight.T.astype(bf16).reshape(2, state_size // 2, own_rows)
        exchange = [
            pltpu.VMEM((seq_count, state_size, width), bf16),
            pltpu.VMEM((seq_count, state_size, width), bf16),
        ]
        piece = (state_size * own_rows // seq_count // 128, 128)
        scan_split = scan_rows.reshape(length, heads, HEAD_DIM)
        back_split = back_rows.reshape(length, heads, HEAD_DIM)
        crossed = jnp.einsum("thp,shp->hts", scan_split, back_split, preferred_element_type=f32)
        heads_running = running.T
        spread = heads_running[:, None, :] - heads_running[:, :, None]
        kernel_mat = (
            jnp.where((row_index <= col_index)[None], jnp.exp(jnp.minimum(spread, 0.0)), 0.0) * crossed
        )
        weights, decays, grad_after = pl.pallas_call(
            functools.partial(first_kernel, seq_count, dp_count),
            out_shape=(
                jax.ShapeDtypeStruct((dp_count,) + weight_half.shape, bf16),
                jax.ShapeDtypeStruct(decay_lanes.shape, f32),
                jax.ShapeDtypeStruct((state_size, channels), bf16),
            ),
            in_specs=[VMEM] * 3,
            out_specs=[VMEM] * 3,
            scratch_shapes=exchange + dma(dp_count, dp_count, seq_count, seq_count, seq_count),
            compiler_params=pltpu.CompilerParams(collective_id=0, has_side_effects=True),
            name="gather_reverse",
        )(weight_half, reverse_local, decay_lanes)

        weight_all = weights.reshape(dp_count, state_size, own_rows).transpose(1, 0, 2)
        write_half = lax.dot_general(
            input_rows, weight_all.reshape(state_size, model), (((1,), (1,)), ((), ())),
            preferred_element_type=f32,
        ).astype(bf16)
        state_local = state_of(write_half, scaled_scan)
        state_before = pl.pallas_call(
            functools.partial(second_kernel, seq_count),
            out_shape=jax.ShapeDtypeStruct((state_size, channels), bf16),
            in_specs=[VMEM] * 2,
            out_specs=VMEM,
            scratch_shapes=exchange + dma(seq_count, seq_count),
            compiler_params=pltpu.CompilerParams(collective_id=1, has_side_effects=True),
            name="forward_states",
        )(state_local, decays)

        kernel_sum = jnp.sum(kernel_mat, axis=0)
        write_grad = jnp.dot(kernel_sum, read_rows.astype(f32), precision=highest)
        write_grad = write_grad + lax.dot_general(
            scaled_scan.astype(bf16), grad_after, (((1,), (1,)), ((), ())), preferred_element_type=f32
        )
        grad_half = write_grad.astype(bf16)
        partial = lax.dot_general(
            grad_half, input_rows, (((0,), (0,)), ((), ())), preferred_element_type=f32
        ).astype(bf16)
        part = partial.reshape(state_size, dp_count, chips, 2, own_rows // seq_count)
        part = part.transpose(3, 2, 1, 0, 4).reshape((2, chips * dp_count) + piece)
        grad_sum = pl.pallas_call(
            functools.partial(third_kernel, seq_count, dp_count),
            out_shape=jax.ShapeDtypeStruct((seq_count,) + piece, bf16),
            in_specs=[VMEM],
            out_specs=VMEM,
            scratch_shapes=[pltpu.VMEM((chips * dp_count,) + piece, bf16)] * 3
            + dma(chips * dp_count, chips * dp_count, seq_count),
            compiler_params=pltpu.CompilerParams(collective_id=2, has_side_effects=True),
            name="reduce_gradient",
        )(part)
        def per_head(a):
            return jnp.sum(a.reshape(a.shape[0], heads, HEAD_DIM), axis=2)

        term_one = decay_total * jnp.sum(
            per_head(grad_after.astype(f32) * state_before.astype(f32)), axis=0)
        grad_write = jnp.dot(write_half, grad_after, preferred_element_type=f32)
        second_rows = to_end * per_head(scan_rows.astype(f32) * grad_write)
        term_two = jnp.dot(before, second_rows, precision=highest)
        state_read = jnp.dot(read_rows, state_before, preferred_element_type=f32)
        third_rows = from_start * per_head(back_rows.astype(f32) * state_read)
        term_three = jnp.dot(upto.T, third_rows, precision=highest)
        write_read = jnp.dot(write_half, read_rows.T, preferred_element_type=f32)
        pairing = jnp.where((row_index < col_index)[None], kernel_mat * write_read[None], 0.0)
        balance = (jnp.sum(pairing, axis=2) - jnp.sum(pairing, axis=1)).T
        term_four = jnp.dot(before, balance, precision=highest)
        decay_grad = term_one[None, :] + term_two + term_three + term_four
        grad_rows = grad_sum.reshape(seq_count, state_size, own_rows // seq_count)
        grad_rows = grad_rows.transpose(1, 0, 2).reshape(state_size, own_rows).astype(f32).T
    new_weight, new_first, new_second = adam_update(
        grad_rows, write_weight, first_moment, second_moment
    )

    return (decay_grad[None], new_weight, new_first, new_second)


def solution(mesh):
    in_specs = (
        P("dp", "seq", None),
        P("dp", "seq", None),
        P("dp", "seq", None),
        P("dp", "seq", None),
        P("dp", "seq", None),
        P("dp", None),
        P("dp", None),
        P("dp", None),
    )
    out_specs = (P("dp", "seq", None), P("dp", None), P("dp", None), P("dp", None))
    return jax.shard_map(
        on_device, mesh=mesh, in_specs=in_specs, out_specs=out_specs, check_vma=False
    )
```

```python
import functools

import jax
import jax.numpy as jnp
from jax import lax
from jax.experimental import pallas as pl
from jax.experimental.pallas import tpu as pltpu
from jax.sharding import PartitionSpec as P

HEAD_DIM = 64
PARTS = 2

beta_one = 0.9
beta_two = 0.999
adam_count = 10.0
learn_rate = 0.01
weight_decay = 0.1
epsilon = 1e-08
highest = lax.Precision.HIGHEST
f32 = jnp.float32
bf16 = jnp.bfloat16
MESH = pl.DeviceIdType.MESH
REVERSE_OUT, REVERSE_HOME = bf16, bf16
FORWARD_OUT, FORWARD_HOME = bf16, bf16
VMEM = pl.BlockSpec(memory_space=pltpu.VMEM)


def remote(src, dst, send_sem, recv_sem, where):
    return pltpu.make_async_remote_copy(
        src_ref=src, dst_ref=dst, send_sem=send_sem, recv_sem=recv_sem, device_id=where,
        device_id_type=MESH,
    )


def loop(low, high, body):
    lax.fori_loop(low, high, lambda i, carry: (body(i), carry)[1], 0)


class Scan:
    def __init__(self, count, me, local, decay, gathered, sent, result, sems):
        self.count, self.me = count, me
        self.local, self.decay, self.gathered, self.sent, self.result = (
            local, decay, gathered, sent, result)
        self.width = local.shape[1] // count
        self.out_send, self.out_recv, self.back_send, self.back_recv = sems

    def columns(self, place):
        return pl.ds(pl.multiple_of(place * self.width, self.width), self.width)

    def outward(self, j, source):
        return remote(self.local.at[:, self.columns(j)], self.gathered.at[source],
                      self.out_send.at[j], self.out_recv.at[source], {"seq": j})

    def homeward(self, i, owner):
        return remote(self.sent.at[i], self.result.at[:, self.columns(owner)],
                      self.back_send.at[i], self.back_recv.at[owner], {"seq": i})

    def start(self):
        loop(1, self.count,
             lambda k: self.outward(lax.rem(self.me + k, self.count), self.me).start())
        self.gathered[self.me] = self.local[:, self.columns(self.me)]

    def combine(self, reverse):
        count, me = self.count, self.me

        def one(k, running):
            i = count - 1 - k if reverse else k

            @pl.when(i != me)
            def _():
                self.outward(i, i).wait_recv()

            self.sent[i] = running.astype(bf16)
            new = self.decay[i] * running + self.gathered[i].astype(f32)

            @pl.when(i != me)
            def _():
                self.homeward(i, me).start()

            return new

        lax.fori_loop(0, count, one, jnp.zeros(self.gathered.shape[1:], f32))
        self.result[:, self.columns(me)] = self.sent[me]

    def arrive(self):
        def one(k):
            j = lax.rem(self.me + k, self.count)
            self.homeward(j, j).wait_recv()

        loop(1, self.count, one)

    def drain(self):
        def one(k):
            j = lax.rem(self.me + k, self.count)
            self.outward(j, j).wait_send()
            self.homeward(j, j).wait_send()

        loop(1, self.count, one)

    def finish(self):
        self.arrive()
        self.drain()


def greet(seq_count, dp_count, same_core):
    seq_me, dp_me = lax.axis_index("seq"), lax.axis_index("dp")
    barrier = pltpu.get_barrier_semaphore()
    loop(1, seq_count, lambda k: pl.semaphore_signal(
        barrier, inc=1, device_id={"seq": lax.rem(seq_me + k, seq_count)}, device_id_type=MESH))
    total = seq_count - 1
    places = seq_count // 2 if same_core else 1

    def over(k):
        d = lax.rem(dp_me + 1 + k // places, dp_count)
        s = lax.rem(seq_me + 2 * (k % places), seq_count)
        pl.semaphore_signal(barrier, inc=1, device_id={"seq": s, "dp": d}, device_id_type=MESH)

    loop(0, (dp_count - 1) * places, over)
    return lambda: pl.semaphore_wait(barrier, total + (dp_count - 1) * places)


def first_kernel(seq_count, dp_count, weight, local, decay, weights, decays, result,
                 gathered, sent, w_send, w_recv, p_send, p_recv, d_send, d_recv,
                 a_send, a_recv, b_send, b_recv):
    seq_me, dp_me = lax.axis_index("seq"), lax.axis_index("dp")
    core = lax.rem(seq_me, 2)
    partner = seq_me + 1 - 2 * core
    greet(seq_count, dp_count, False)()

    def across(d, source):
        return remote(weight.at[core], weights.at[source, core], w_send.at[d], w_recv.at[source],
                      {"dp": d})

    def beside(d, half):
        return remote(weights.at[d, half], weights.at[d, half], p_send.at[d], p_recv.at[d],
                      {"seq": partner})

    def tell(j, source):
        return remote(decay.at[j], decays.at[source], d_send.at[j], d_recv.at[source], {"seq": j})

    loop(1, dp_count, lambda k: across(lax.rem(dp_me + k, dp_count), dp_me).start())
    loop(1, seq_count, lambda k: tell(lax.rem(seq_me + k, seq_count), seq_me).start())
    scan = Scan(seq_count, seq_me, local, decays, gathered, sent, result,
                (a_send, a_recv, b_send, b_recv))
    scan.start()
    decays[seq_me] = decay[seq_me]
    weights[dp_me] = weight[...]

    def told(k):
        j = lax.rem(seq_me + k, seq_count)
        tell(j, j).wait_recv()

    loop(1, seq_count, told)

    def pass_on(k):
        d = lax.rem(dp_me + k, dp_count)
        across(d, d).wait_recv()
        beside(d, core).start()

    loop(1, dp_count, pass_on)
    scan.combine(True)

    def end(k):
        d = lax.rem(dp_me + k, dp_count)
        across(d, d).wait_send()
        beside(d, core).wait_send()
        beside(d, 1 - core).wait_recv()

    loop(1, dp_count, end)
    loop(1, seq_count, lambda k: tell(lax.rem(seq_me + k, seq_count), 0).wait_send())
    scan.finish()


def second_kernel(seq_count, local, decays, result, gathered, sent, a_send, a_recv, b_send, b_recv):
    greet(seq_count, 1, False)()
    scan = Scan(seq_count, lax.axis_index("seq"), local, decays, gathered, sent, result,
                (a_send, a_recv, b_send, b_recv))
    scan.start()
    scan.combine(False)
    scan.finish()


def third_kernel(seq_count, dp_count, part, total, halves, summed, pieces,
                 h_send, h_recv, s_send, s_recv, g_send, g_recv):
    seq_me, dp_me = lax.axis_index("seq"), lax.axis_index("dp")
    core = lax.rem(seq_me, 2)
    chip = seq_me // 2
    partner = seq_me + 1 - 2 * core
    group = (seq_count // 2) * dp_count
    mine = chip * dp_count + dp_me
    greet(seq_count, dp_count, True)()

    def half(g):
        return remote(part.at[1 - core, g], halves.at[g], h_send.at[g], h_recv.at[g],
                      {"seq": partner})

    def scatter(g, source):
        return remote(summed.at[g], pieces.at[source], s_send.at[g], s_recv.at[source],
                      {"seq": 2 * (g // dp_count) + core, "dp": g % dp_count})

    def share(j, source):
        return remote(total.at[seq_me], total.at[source], g_send.at[j], g_recv.at[source],
                      {"seq": j})

    loop(1, group + 1, lambda k: half(lax.rem(mine + k, group)).start())

    def pair(k):
        g = lax.rem(mine + k, group)
        half(g).wait_recv()
        summed[g] = (part[core, g].astype(f32) + halves[g].astype(f32)).astype(bf16)

        @pl.when(g != mine)
        def _():
            scatter(g, mine).start()

    loop(1, group + 1, pair)

    def collect(k, running):
        g = lax.rem(mine + group - k, group)
        scatter(g, g).wait_recv()
        return running + pieces[g].astype(f32)

    own = part[core, mine].astype(f32) + halves[mine].astype(f32)
    total[seq_me] = lax.fori_loop(1, group, collect, own).astype(bf16)
    loop(1, seq_count, lambda k: share(lax.rem(seq_me + k, seq_count), seq_me).start())

    def end(k):
        j = lax.rem(seq_me + seq_count - k, seq_count)
        share(j, j).wait_recv()
        share(j, j).wait_send()

    loop(1, group + 1, lambda k: half(lax.rem(mine + k, group)).wait_send())
    loop(1, group, lambda k: scatter(lax.rem(mine + k, group), 0).wait_send())
    loop(1, seq_count, end)


def nt(a, b):
    return lax.dot_general(a, b, (((1,), (1,)), ((), ())), preferred_element_type=f32)


def split(a):
    high = a.astype(bf16)
    return high, (a - high.astype(f32)).astype(bf16)


def exact(a, b):
    return lax.dot_general(a, b, (((1,), (1,)), ((), ())), precision=highest)


def stack_split(a, axis, parts=2):
    pieces, rest = [], a
    for _ in range(parts):
        pieces.append(rest.astype(bf16))
        rest = rest - pieces[-1].astype(f32)
    return jnp.concatenate(pieces, axis=axis)


def repeat(a, axis, parts=2):
    return jnp.concatenate([a] * parts, axis=axis)


def dot(a, b):
    return jnp.dot(a, b, preferred_element_type=f32)


class Owners:
    def __init__(self, chips, chip, mid=True):
        self.count = chips // 2 if mid and chips % 4 == 0 else chips
        self.base = (chips - self.count) // 2
        self.me = chip - self.base
        self.is_me = (self.me >= 0) & (self.me < self.count)

    def chip(self, o):
        return self.base + o


class ChipScan:
    def __init__(self, count, chip, core, owners, reverse, local, decays, gathered, sent, result,
                 sems):
        self.count, self.chip, self.core, self.owners, self.reverse = (
            count, chip, core, owners, reverse)
        self.local, self.decays, self.gathered, self.sent, self.result = (
            local, decays, gathered, sent, result)
        self.width = local.shape[2]
        self.out_send, self.out_recv, self.back_send, self.back_recv = sems
        self.head, self.tail = (count - 1, 0) if reverse else (0, count - 1)

    def columns(self, o):
        return pl.ds(pl.multiple_of(o * self.width, self.width), self.width)

    def outward(self, o, source):
        return remote(self.local.at[o], self.gathered.at[source], self.out_send.at[o],
                      self.out_recv.at[source], {"seq": 2 * self.owners.chip(o) + self.core})

    def homeward(self, i, o):
        return remote(self.sent.at[i], self.result.at[:, self.columns(o)],
                      self.back_send.at[i], self.back_recv.at[o], {"seq": 2 * i + self.core})

    def to_owners(self, body):
        def one(k):
            o = lax.rem(self.chip + k, self.owners.count)

            @pl.when(o != self.owners.me)
            def _():
                body(o)

        loop(0, self.owners.count, one)

    def others(self, body):
        loop(1, self.count, lambda k: body(lax.rem(self.chip + k, self.count)))

    def start(self, total):
        for o in range(self.owners.count):
            self.local[o] = total[:, o * self.width : (o + 1) * self.width].astype(self.local.dtype)

        @pl.when(self.chip != self.tail)
        def _():
            self.to_owners(lambda o: self.outward(o, self.chip).start())

        @pl.when(self.owners.is_me)
        def _():
            self.gathered[self.chip] = self.local[self.owners.me]

    def combine(self, visit):
        def one(k, running):
            i = self.count - 1 - k if self.reverse else k

            @pl.when((i != self.chip) & (i != self.tail))
            def _():
                self.outward(0, i).wait_recv()

            self.sent[i] = running.astype(self.sent.dtype)

            @pl.when((i != self.chip) & (i != self.head))
            def _():
                self.homeward(i, self.owners.me).start()

            visit(i, running)
            if k == self.count - 1:
                return running
            return self.decays[i] * running + self.gathered[i].astype(f32)

        @pl.when(self.owners.is_me)
        def _():
            running = jnp.zeros(self.gathered.shape[1:], f32)
            for k in range(self.count):
                running = one(k, running)
            self.result[:, self.columns(self.owners.me)] = self.sent[self.chip]

    def arrive(self):
        @pl.when(self.chip != self.head)
        def _():
            self.to_owners(lambda o: self.homeward(self.chip, o).wait_recv())

        @pl.when(self.chip == self.head)
        def _():
            self.result[...] = jnp.zeros_like(self.result)

    def drain(self):
        @pl.when(self.chip != self.tail)
        def _():
            self.to_owners(lambda o: self.outward(o, 0).wait_send())

        def one(j):
            @pl.when(j != self.head)
            def _():
                self.homeward(j, 0).wait_send()

        @pl.when(self.owners.is_me)
        def _():
            self.others(one)


def one_kernel(seq_count, dp_count, weight_hbm, log_decay_hbm, scan_hbm, back_hbm, read_hbm,
               input_hbm, first_hbm, second_hbm, decay_grad, total, weight_out, first_out, second_out,
               log_decay, scan_rows, back_rows, read_rows, weight_rows, inputs,
               mine, pair, front_mine, front, scaled_scan, scaled_mine, scaled_got,
               kernel_mat, row_sums, col_sums, weights, write_mine, write_got,
               decay_out, decays, reverse_out, reverse_got, reverse_sent, reverse_home,
               forward_out, forward_got, forward_sent, forward_home,
               after, grad_after, prior, state_before, grad_mine, grad_got,
               part, pieces, kept, meet_out, meet_home,
               load_sem, input_sem, pass_sem, l_send, l_recv, w_send, w_recv, d_send, d_recv,
               a_send, a_recv, b_send, b_recv, e_send, e_recv, f_send, f_recv,
               t_send, t_recv, m_send, m_recv, s_send, s_recv, g_send, g_recv, q_send, q_recv):
    seq_me, dp_me = lax.axis_index("seq"), lax.axis_index("dp")
    core = lax.rem(seq_me, 2)
    other = 1 - core
    chip = seq_me // 2
    chips = seq_count // 2
    partner = {"seq": seq_me + 1 - 2 * core}
    group = chips * dp_count
    own = chip * dp_count + dp_me

    owners = Owners(chips, chip, False)
    keep = Owners(chips, chip, True)
    held = keep.count * dp_count
    own_held = keep.me * dp_count + dp_me

    def place(g):
        return {"seq": 2 * (g // dp_count) + core, "dp": lax.rem(g, dp_count)}

    barrier = pltpu.get_barrier_semaphore()
    pl.semaphore_signal(barrier, inc=1, device_id=partner, device_id_type=MESH)
    loop(1, group, lambda k: pl.semaphore_signal(
        barrier, inc=1, device_id=place(lax.rem(own + k, group)), device_id_type=MESH))

    length, channels = scan_rows.shape
    half = channels // 2
    heads = channels // HEAD_DIM
    half_heads = heads // 2
    state_size = read_rows.shape[0]
    own_rows = weight_hbm.shape[1]
    side = own_rows // 2
    width = half // owners.count
    wide = side // keep.count

    def span(start, size):
        return pl.ds(pl.multiple_of(start, 128), size)

    loads = [
        pltpu.make_async_copy(log_decay_hbm, log_decay, load_sem.at[0]),
        pltpu.make_async_copy(back_hbm, back_rows, load_sem.at[1]),
        pltpu.make_async_copy(read_hbm, read_rows, load_sem.at[2]),
        pltpu.make_async_copy(weight_hbm.at[:, span(core * side, side)], weight_rows,
                              load_sem.at[3]),
        pltpu.make_async_copy(scan_hbm, scan_rows, load_sem.at[4]),
    ]
    for copy in loads:
        copy.start()
    my_rows = pl.ds(pl.multiple_of(core * length, length), length)

    def input_load(d):
        return pltpu.make_async_copy(
            input_hbm.at[:, span(d * own_rows + core * side, side)],
            inputs.at[my_rows, d * side : (d + 1) * side], input_sem.at[d])

    for d in range(dp_count):
        input_load(d).start()

    passed = [
        pltpu.make_async_copy(src, dst, pass_sem.at[i])
        for i, (src, dst) in enumerate(
            ((weight_hbm, weight_out), (first_hbm, first_out), (second_hbm, second_out)))
    ]
    row_index = lax.broadcasted_iota(jnp.int32, (length, length), 0)
    col_index = lax.broadcasted_iota(jnp.int32, (length, length), 1)
    causal = row_index <= col_index
    upto = repeat((col_index <= row_index).astype(f32).astype(bf16), 1, 3)
    owner = lax.broadcasted_iota(jnp.int32, (heads, channels), 0)
    spot = lax.broadcasted_iota(jnp.int32, (heads, channels), 1) - owner * HEAD_DIM
    member = ((spot >= 0) & (spot < HEAD_DIM)).astype(bf16)
    half_member = member[:half_heads, :half]
    member = repeat(member, 0)

    def widen(a):
        return dot(stack_split(a, 1), member)

    def per_head(a):
        high, low = split(a)
        return nt(half_member, high) + nt(half_member, low)

    loads[0].wait()
    decay_parts = stack_split(log_decay[...], 1, 3)
    run_cols = nt(upto, decay_parts)
    overall = run_cols[length - 1 :, :]
    from_wide = widen(jnp.exp(run_cols))
    decay_wide = from_wide[length - 1 :, :]
    loads[1].wait()
    loads[2].wait()
    read_twice = repeat(read_rows[...], 1)
    for h in range(2):
        at = slice(h * half, (h + 1) * half)
        scaled = back_rows[:, at].astype(f32) * from_wide[:, at]
        mine[h, :state_size] = dot(read_twice, stack_split(scaled, 0))
        mine[h, state_size:] = jnp.broadcast_to(decay_wide[:, at], (8, half))
    loads[3].wait()
    weights[dp_me] = weight_rows[...].astype(bf16)

    def to_partner(src, dst, place):
        return remote(src, dst, m_send.at[place], m_recv.at[place], partner)

    def across(d, source):
        return remote(weights.at[dp_me], weights.at[source], w_send.at[d], w_recv.at[source],
                      {"dp": d})

    def lend(d, rows):
        return remote(input_hbm.at[:, span(d * own_rows + other * side, side)],
                      inputs.at[rows, d * side : (d + 1) * side],
                      l_send.at[d], l_recv.at[d], partner)

    def tell(o, source):
        return remote(decay_out.at[o], decays.at[source], d_send.at[o], d_recv.at[source],
                      {"seq": 2 * owners.chip(o) + core})

    parts = part.shape[0]
    rows = state_size // parts

    def scatter(g, source, n):
        return remote(part.at[n, g], pieces.at[n, source], s_send.at[n, g], s_recv.at[n, source],
                      place(keep.base * dp_count + g))

    def columns(side_of, o):
        return span(side_of * side + o * wide, wide)

    def meeting(i, o):
        return remote(meet_out.at[i], meet_home.at[o], t_send.at[i], t_recv.at[o],
                      {"seq": 2 * i + core})

    def share(j, o, n):
        spot = total.at[n * rows : (n + 1) * rows, columns(core, o)]
        return remote(spot, spot, g_send.at[n, j], g_recv.at[n, o], {"seq": 2 * j + core})

    def hand(o, from_core, n):
        spot = total.at[n * rows : (n + 1) * rows, columns(from_core, o)]
        return remote(spot, spot, q_send.at[n, o], q_recv.at[n, o], partner)

    reverse = ChipScan(chips, chip, core, owners, True, reverse_out, decays, reverse_got,
                       reverse_sent, reverse_home, (a_send, a_recv, b_send, b_recv))
    forward = ChipScan(chips, chip, core, owners, False, forward_out, decays, forward_got,
                       forward_sent, forward_home, (e_send, e_recv, f_send, f_recv))

    def to_keepers(body):
        def one(k):
            o = lax.rem(chip + k, keep.count)

            @pl.when(o != keep.me)
            def _():
                body(o)

        loop(0, keep.count, one)

    def to_holders(body):
        def one(k):
            g = lax.rem(own + k, held)

            @pl.when(g != own_held)
            def _():
                body(g)

        loop(0, held, one)

    pl.semaphore_wait(barrier, group)
    states_over = to_partner(mine.at[other], pair.at[core], 0)
    states_over.start()
    loop(1, dp_count, lambda k: across(lax.rem(dp_me + k, dp_count), dp_me).start())
    pair[core] = mine[core]
    run_rows = nt(decay_parts, upto)
    loads[4].wait()
    to_wide = widen(jnp.exp(overall - run_cols))
    for h in range(2):
        at = slice(h * half, (h + 1) * half)
        scaled = scan_rows[:, at].astype(f32) * to_wide[:, at]
        scaled_scan[h] = scaled
        scaled_mine[h] = scaled.astype(bf16)
    scaled_over = to_partner(scaled_mine.at[other], scaled_got, 1)
    states_over.wait_recv()
    first_decay = pair[0, state_size : state_size + 1]
    last_decay = pair[1, state_size : state_size + 1]
    chip_decay = first_decay * last_decay
    for o in range(owners.count):
        decay_out[o] = chip_decay[:, o * width : (o + 1) * width]
    reverse.to_owners(lambda o: tell(o, chip).start())
    reverse.start(pair[0, :state_size] + first_decay * pair[1, :state_size])
    for d in range(dp_count):
        lend(d, my_rows).start()

    @pl.when(owners.is_me)
    def _():
        decays[chip] = decay_out[owners.me]

    scaled_over.start()
    for copy in passed:
        copy.start()
    kernel_sum = jnp.zeros((length, length), f32)

    def kernels(low, high, kernel_sum):
        for h in range(low, high):
            at = slice(h * HEAD_DIM, (h + 1) * HEAD_DIM)
            crossed = nt(scan_rows[:, at], back_rows[:, at])
            spread = run_rows[h : h + 1, :] - run_cols[:, h : h + 1]
            term = jnp.where(causal, jnp.exp(jnp.minimum(spread, 0.0)), 0.0) * crossed
            kernel_mat[h] = term
            kernel_sum += term
        return kernel_sum

    kernel_sum = kernels(0, heads * 3 // 8, kernel_sum)
    for d in range(dp_count):
        input_load(d).wait()
        lend(d, my_rows).wait_recv()
    loop(1, dp_count, lambda k: across(0, lax.rem(dp_me + k, dp_count)).wait_recv())
    some = nt(weights[0], inputs[:, :side])
    for d in range(1, dp_count):
        some += nt(weights[d], inputs[:, d * side : (d + 1) * side])
    for t in range(2):
        write_mine[t] = some[:, t * length : (t + 1) * length]
    write_over = to_partner(write_mine.at[other], write_got, 2)
    write_over.start()

    @pl.when(owners.is_me)
    def _():
        reverse.others(lambda j: tell(0, j).wait_recv())


    def keep_after(i, running):
        kept[i] = running

    reverse.combine(keep_after)
    kernel_sum = kernels(heads * 3 // 8, heads * 5 // 8, kernel_sum)
    write_over.wait_recv()
    write = write_mine[core] + write_got[...]
    write_rows = write.T.astype(bf16)
    write = repeat(write.astype(bf16), 1)
    for h in range(2):
        front_mine[h] = dot(write, stack_split(scaled_scan[h], 0))
    front_over = to_partner(front_mine.at[other], front.at[core], 3)
    front_over.start()
    front[core] = front_mine[core]
    front_over.wait_recv()
    forward.start(last_decay * front[0] + front[1])
    kernel_sum = kernels(heads * 5 // 8, heads, kernel_sum)
    inner = dot(read_twice, stack_split(kernel_sum.T, 0))
    scaled_over.wait_recv()
    reverse.arrive()
    after[1] = reverse_home[...].astype(f32)
    after[0] = pair[1, :state_size] + last_decay * reverse_home[...].astype(f32)
    grad_mine[core] = nt(after[core].astype(bf16), scaled_mine[core]) + inner
    grad_mine[other] = nt(after[other].astype(bf16), scaled_got[...])
    grad_over = to_partner(grad_mine, grad_got, 4)
    grad_over.start()
    after_over = to_partner(after.at[other], grad_after.at[core], 5)
    grad_over.wait_recv()
    grad_half = (grad_mine[...] + grad_got[...]).astype(bf16)
    grad_half = jnp.concatenate([grad_half[0], grad_half[1]], axis=1)
    for k in range(held):
        g = lax.rem(own + k, held)
        low = lax.rem(g, dp_count) * side + g // dp_count * wide
        term = dot(grad_half, inputs[:, span(low, wide)]).astype(bf16)
        for n in range(parts):
            part[n, g] = term[n * rows : (n + 1) * rows]

        @pl.when(g != own_held)
        def _():
            scatter(g, own, 0).start()

    for n in range(1, parts):
        to_holders(lambda g: scatter(g, own, n).start())
    after_over.start()
    grad_after[core] = after[core]
    def meet(i, running):
        meet_out[i] = jnp.sum(kept[i] * running, axis=0, keepdims=True)

        @pl.when(i != chip)
        def _():
            meeting(i, owners.me).start()

    forward.combine(meet)

    @pl.when(owners.is_me)
    def _():
        meet_home[owners.me] = meet_out[chip]

    read_turned = read_rows[...].astype(f32).T.astype(bf16)
    write_read = jnp.where(row_index < col_index, nt(write_rows, read_turned), 0.0)
    for h in range(heads):
        pairing = kernel_mat[h] * write_read
        row_sums[:, h : h + 1] = jnp.sum(pairing, axis=1, keepdims=True)
        col_sums[h : h + 1, :] = jnp.sum(pairing, axis=0, keepdims=True)
    after_over.wait_recv()
    second = []
    for h in range(2):
        grad_write = dot(repeat(write_rows, 1), stack_split(grad_after[h], 0))
        second.append(per_head(scan_rows[:, h * half : (h + 1) * half].astype(f32) * grad_write))
    overall_rows = run_rows[:, length - 1 :]
    before = repeat((col_index < row_index).astype(f32).astype(bf16), 1, 3)
    onward = repeat(causal.astype(f32).astype(bf16), 1, 3)
    second = (jnp.exp(overall_rows - run_rows) * jnp.concatenate(second, axis=0)
              + row_sums[...].T - col_sums[...])

    @pl.when(keep.is_me)
    def _():
        for n in range(parts):
            def collect(k, running):
                g = lax.rem(own + group - k, group)
                scatter(0, g, n).wait_recv()
                return running + pieces[n, g].astype(f32)

            total[n * rows : (n + 1) * rows, columns(core, keep.me)] = lax.fori_loop(
                1, group, collect, part[n, own_held].astype(f32)).astype(bf16)
            reverse.others(lambda j: share(j, keep.me, n).start())
            hand(keep.me, core, n).start()

    forward.arrive()
    reverse.to_owners(lambda o: meeting(chip, o).wait_recv())
    met = jnp.concatenate([meet_home[o] for o in range(owners.count)], axis=1)
    came = forward_home[...].astype(f32)
    both = (last_decay * met + jnp.sum(pair[1, :state_size] * came, axis=0, keepdims=True),
            first_decay * met + jnp.sum(after[1] * front[0], axis=0, keepdims=True))
    prior[0, :state_size] = came
    prior[1, :state_size] = front[0] + first_decay * came
    for t in range(2):
        prior[t, state_size:] = jnp.broadcast_to(both[t], (8, half))
    prior_over = to_partner(prior.at[other], state_before.at[core], 6)
    prior_over.start()
    state_before[core] = prior[core]
    prior_over.wait_recv()
    third, first = [], []
    for h in range(2):
        at = slice(h * half, (h + 1) * half)
        state_read = dot(repeat(read_turned, 1), stack_split(state_before[h, :state_size], 0))
        third.append(per_head(back_rows[:, at].astype(f32) * state_read))
        first.append(per_head(state_before[h, state_size:])[:, :1])
    decay_grad[...] = (
        jnp.exp(overall_rows) * jnp.concatenate(first, axis=0)
        + nt(stack_split(second, 1, 3), before)
        + nt(stack_split(jnp.exp(run_rows) * jnp.concatenate(third, axis=0), 1, 3), onward)
    )

    for copy in passed:
        copy.wait()
    loop(1, dp_count, lambda k: across(lax.rem(dp_me + k, dp_count), 0).wait_send())
    for d in range(dp_count):
        lend(d, my_rows).wait_send()
    for copy in (states_over, scaled_over, write_over, front_over, grad_over, after_over, prior_over):
        copy.wait_send()
    reverse.drain()
    forward.drain()

    @pl.when(owners.is_me)
    def _():
        reverse.others(lambda j: meeting(j, 0).wait_send())

    reverse.to_owners(lambda o: tell(o, 0).wait_send())
    for n in range(parts):
        to_holders(lambda g: scatter(g, 0, n).wait_send())
    for n in range(parts):
        def pass_on(o):
            share(chip, o, n).wait_recv()
            hand(o, core, n).start()

        to_keepers(pass_on)
    for n in range(parts):
        loop(0, keep.count, lambda o: hand(o, other, n).wait_recv())

    for n in range(parts):
        @pl.when(keep.is_me)
        def _():
            reverse.others(lambda j: share(j, 0, n).wait_send())

        loop(0, keep.count, lambda o: hand(o, core, n).wait_send())


def dma(*sizes):
    shapes = [size if isinstance(size, tuple) else (size,) for size in sizes]
    return [pltpu.SemaphoreType.DMA(shape) for shape in shapes for _ in range(2)]


def adam_update(grad_rows, weight_rows, first_rows, second_rows):
    new_first = beta_one * first_rows + (1.0 - beta_one) * grad_rows
    new_second = beta_two * second_rows + (1.0 - beta_two) * grad_rows * grad_rows
    first_hat = new_first / (1.0 - beta_one**adam_count)
    second_hat = new_second / (1.0 - beta_two**adam_count)
    new_weight = weight_rows - learn_rate * (
        first_hat / (jnp.sqrt(second_hat) + epsilon) + weight_decay * weight_rows
    )
    return (new_weight, new_first, new_second)


def update_kernel(steps, decay, grad, weight, first, second, decay_out, weight_out, first_out,
                  second_out, new_weight, new_first, new_second, out_sem, decay_sem):
    decay_copy = pltpu.make_async_copy(decay, decay_out, decay_sem)
    decay_copy.start()
    size = grad.shape[1] // steps
    copies = []
    for step in range(steps):
        at = slice(step * size, (step + 1) * size)
        results = adam_update(grad[:, at].astype(f32), weight[:, at], first[:, at], second[:, at])
        for i, (value, held, out) in enumerate(zip(
                results, (new_weight, new_first, new_second),
                (weight_out, first_out, second_out))):
            held[:, at] = value
            copies.append(pltpu.make_async_copy(held.at[:, at], out.at[:, at], out_sem.at[i, step]))
            copies[-1].start()
    decay_copy.wait()
    for copy in copies:
        copy.wait()


def on_device(
    layer_input,
    scan_input,
    readout,
    log_decay,
    output_cotangent,
    write_weight,
    first_moment,
    second_moment,
):
    seq_count, dp_count = lax.axis_size("seq"), lax.axis_size("dp")
    input_rows = layer_input[0]
    scan_rows = scan_input[0]
    read_rows = readout[0]
    decay_rows = log_decay[0]
    back_rows = output_cotangent[0]
    length, model = input_rows.shape
    heads = decay_rows.shape[1]
    channels = scan_rows.shape[1]
    state_size = read_rows.shape[1]
    own_rows = write_weight.shape[0]
    width = channels // seq_count

    chips = seq_count // 2
    group = chips * dp_count
    fast = own_rows % (128 * seq_count) == 0 and channels % (128 * seq_count) == 0
    if fast:
        half = channels // 2
        owners = Owners(chips, 0, False).count
        keep = Owners(chips, 0, True).count
        held = keep * dp_count
        lanes = half // owners
        parts = PARTS if state_size % (16 * PARTS) == 0 else 1
        piece = (state_size // parts, own_rows // 2 // keep)
        results = pl.pallas_call(
            functools.partial(one_kernel, seq_count, dp_count),
            out_shape=(
                pltpu.VMEM((heads, length), f32),
                pltpu.VMEM((state_size, own_rows), bf16),
            ) + (pltpu.VMEM((state_size, own_rows), f32),) * 3,
            in_specs=[pl.BlockSpec(memory_space=pltpu.HBM)] * 8,
            out_specs=[VMEM] * 5,
            scratch_shapes=[
                pltpu.VMEM((heads, length), f32),
                pltpu.VMEM((length, channels), bf16),
                pltpu.VMEM((length, channels), bf16),
                pltpu.VMEM((state_size, length), bf16),
                pltpu.VMEM((state_size, own_rows // 2), f32),
                pltpu.VMEM((2 * length, model // 2), bf16),
                pltpu.VMEM((2, state_size + 8, half), f32),
                pltpu.VMEM((2, state_size + 8, half), f32),
                pltpu.VMEM((2, state_size, half), f32),
                pltpu.VMEM((2, state_size, half), f32),
                pltpu.VMEM((2, length, half), f32),
                pltpu.VMEM((2, length, half), bf16),
                pltpu.VMEM((length, half), bf16),
                pltpu.VMEM((heads, length, length), f32),
                pltpu.VMEM((length, heads), f32),
                pltpu.VMEM((heads, length), f32),
                pltpu.VMEM((dp_count, state_size, own_rows // 2), bf16),
                pltpu.VMEM((2, state_size, length), f32),
                pltpu.VMEM((state_size, length), f32),
                pltpu.VMEM((owners, 1, lanes), f32),
                pltpu.VMEM((chips, 1, lanes), f32),
            ]
            + [pltpu.VMEM(shape, kind)
               for out_kind, home_kind in ((REVERSE_OUT, REVERSE_HOME), (FORWARD_OUT, FORWARD_HOME))
               for shape, kind in (
                   ((owners, state_size, lanes), out_kind), ((chips, state_size, lanes), out_kind),
                   ((chips, state_size, lanes), home_kind), ((state_size, half), home_kind))]
            + [pltpu.VMEM((2, state_size, half), f32)] * 2
            + [pltpu.VMEM((2, state_size + 8, half), f32)] * 2
            + [pltpu.VMEM((2, state_size, length), f32)] * 2
            + [pltpu.VMEM((parts, held) + piece, bf16), pltpu.VMEM((parts, group) + piece, bf16),
               pltpu.VMEM((chips, state_size, lanes), f32), pltpu.VMEM((chips, 1, lanes), f32),
               pltpu.VMEM((owners, 1, lanes), f32)]
            + [pltpu.SemaphoreType.DMA((5,)), pltpu.SemaphoreType.DMA((dp_count,)),
               pltpu.SemaphoreType.DMA((3,))]
            + dma(dp_count, dp_count, chips, chips, chips, chips, chips, chips, 7, (parts, group), (parts, chips), (parts, keep)),
            compiler_params=pltpu.CompilerParams(collective_id=3, has_side_effects=True,
                                                 vmem_limit_bytes=60000000),
            name="whole_step",
        )(write_weight.T, decay_rows.T, scan_rows, back_rows, read_rows.T, input_rows,
          first_moment.T, second_moment.T)
        steps = 4
        decay_grad, new_weight, new_first, new_second = pl.pallas_call(
            functools.partial(update_kernel, steps),
            out_shape=(jax.ShapeDtypeStruct((heads, length), f32),)
            + (jax.ShapeDtypeStruct((state_size, own_rows), f32),) * 3,
            in_specs=[VMEM] * 5,
            out_specs=[pl.BlockSpec(memory_space=pltpu.HBM)] * 4,
            scratch_shapes=[pltpu.VMEM((state_size, own_rows), f32)] * 3
            + [pltpu.SemaphoreType.DMA((3, steps)), pltpu.SemaphoreType.DMA],
            compiler_params=pltpu.CompilerParams(vmem_limit_bytes=16 * 2**20),
            name="update",
        )(*results)
        return decay_grad.T[None], new_weight.T, new_first.T, new_second.T
    else:
        row_index = lax.broadcasted_iota(jnp.int32, (length, length), 0)
        col_index = lax.broadcasted_iota(jnp.int32, (length, length), 1)
        upto = (col_index <= row_index).astype(f32)
        before = (col_index < row_index).astype(f32)
        running = jnp.dot(upto, decay_rows, precision=highest)
        overall = running[-1]
        to_end = jnp.exp(overall[None, :] - running)
        from_start = jnp.exp(running)
        decay_total = jnp.exp(overall)

        def widen(a):
            return jnp.repeat(a, HEAD_DIM, axis=1)

        scaled_scan = scan_rows.astype(f32) * widen(to_end)
        scaled_back = back_rows.astype(f32) * widen(from_start)

        def state_of(vectors, rows):
            return lax.dot_general(
                vectors.astype(f32), rows, (((0,), (0,)), ((), ())), precision=highest
            ).astype(bf16)

        reverse_local = state_of(read_rows, scaled_back)
        decay_lanes = widen(decay_total[None]).reshape(seq_count, 1, width)
        weight_half = write_weight.T.astype(bf16).reshape(2, state_size // 2, own_rows)
        exchange = [
            pltpu.VMEM((seq_count, state_size, width), bf16),
            pltpu.VMEM((seq_count, state_size, width), bf16),
        ]
        piece = (state_size * own_rows // seq_count // 128, 128)
        scan_split = scan_rows.reshape(length, heads, HEAD_DIM)
        back_split = back_rows.reshape(length, heads, HEAD_DIM)
        crossed = jnp.einsum("thp,shp->hts", scan_split, back_split, preferred_element_type=f32)
        heads_running = running.T
        spread = heads_running[:, None, :] - heads_running[:, :, None]
        kernel_mat = (
            jnp.where((row_index <= col_index)[None], jnp.exp(jnp.minimum(spread, 0.0)), 0.0) * crossed
        )
        weights, decays, grad_after = pl.pallas_call(
            functools.partial(first_kernel, seq_count, dp_count),
            out_shape=(
                jax.ShapeDtypeStruct((dp_count,) + weight_half.shape, bf16),
                jax.ShapeDtypeStruct(decay_lanes.shape, f32),
                jax.ShapeDtypeStruct((state_size, channels), bf16),
            ),
            in_specs=[VMEM] * 3,
            out_specs=[VMEM] * 3,
            scratch_shapes=exchange + dma(dp_count, dp_count, seq_count, seq_count, seq_count),
            compiler_params=pltpu.CompilerParams(collective_id=0, has_side_effects=True),
            name="gather_reverse",
        )(weight_half, reverse_local, decay_lanes)

        weight_all = weights.reshape(dp_count, state_size, own_rows).transpose(1, 0, 2)
        write_half = lax.dot_general(
            input_rows, weight_all.reshape(state_size, model), (((1,), (1,)), ((), ())),
            preferred_element_type=f32,
        ).astype(bf16)
        state_local = state_of(write_half, scaled_scan)
        state_before = pl.pallas_call(
            functools.partial(second_kernel, seq_count),
            out_shape=jax.ShapeDtypeStruct((state_size, channels), bf16),
            in_specs=[VMEM] * 2,
            out_specs=VMEM,
            scratch_shapes=exchange + dma(seq_count, seq_count),
            compiler_params=pltpu.CompilerParams(collective_id=1, has_side_effects=True),
            name="forward_states",
        )(state_local, decays)

        kernel_sum = jnp.sum(kernel_mat, axis=0)
        write_grad = jnp.dot(kernel_sum, read_rows.astype(f32), precision=highest)
        write_grad = write_grad + lax.dot_general(
            scaled_scan.astype(bf16), grad_after, (((1,), (1,)), ((), ())), preferred_element_type=f32
        )
        grad_half = write_grad.astype(bf16)
        partial = lax.dot_general(
            grad_half, input_rows, (((0,), (0,)), ((), ())), preferred_element_type=f32
        ).astype(bf16)
        part = partial.reshape(state_size, dp_count, chips, 2, own_rows // seq_count)
        part = part.transpose(3, 2, 1, 0, 4).reshape((2, chips * dp_count) + piece)
        grad_sum = pl.pallas_call(
            functools.partial(third_kernel, seq_count, dp_count),
            out_shape=jax.ShapeDtypeStruct((seq_count,) + piece, bf16),
            in_specs=[VMEM],
            out_specs=VMEM,
            scratch_shapes=[pltpu.VMEM((chips * dp_count,) + piece, bf16)] * 3
            + dma(chips * dp_count, chips * dp_count, seq_count),
            compiler_params=pltpu.CompilerParams(collective_id=2, has_side_effects=True),
            name="reduce_gradient",
        )(part)
        def per_head(a):
            return jnp.sum(a.reshape(a.shape[0], heads, HEAD_DIM), axis=2)

        term_one = decay_total * jnp.sum(
            per_head(grad_after.astype(f32) * state_before.astype(f32)), axis=0)
        grad_write = jnp.dot(write_half, grad_after, preferred_element_type=f32)
        second_rows = to_end * per_head(scan_rows.astype(f32) * grad_write)
        term_two = jnp.dot(before, second_rows, precision=highest)
        state_read = jnp.dot(read_rows, state_before, preferred_element_type=f32)
        third_rows = from_start * per_head(back_rows.astype(f32) * state_read)
        term_three = jnp.dot(upto.T, third_rows, precision=highest)
        write_read = jnp.dot(write_half, read_rows.T, preferred_element_type=f32)
        pairing = jnp.where((row_index < col_index)[None], kernel_mat * write_read[None], 0.0)
        balance = (jnp.sum(pairing, axis=2) - jnp.sum(pairing, axis=1)).T
        term_four = jnp.dot(before, balance, precision=highest)
        decay_grad = term_one[None, :] + term_two + term_three + term_four
        grad_rows = grad_sum.reshape(seq_count, state_size, own_rows // seq_count)
        grad_rows = grad_rows.transpose(1, 0, 2).reshape(state_size, own_rows).astype(f32).T
    new_weight, new_first, new_second = adam_update(
        grad_rows, write_weight, first_moment, second_moment
    )

    return (decay_grad[None], new_weight, new_first, new_second)


def solution(mesh):
    in_specs = (
        P("dp", "seq", None),
        P("dp", "seq", None),
        P("dp", "seq", None),
        P("dp", "seq", None),
        P("dp", "seq", None),
        P("dp", None),
        P("dp", None),
        P("dp", None),
    )
    out_specs = (P("dp", "seq", None), P("dp", None), P("dp", None), P("dp", None))
    return jax.shard_map(
        on_device, mesh=mesh, in_specs=in_specs, out_specs=out_specs, check_vma=False
    )
```

```python
import functools

import jax
import jax.numpy as jnp
from jax import lax
from jax.experimental import pallas as pl
from jax.experimental.pallas import tpu as pltpu
from jax.sharding import PartitionSpec as P

HEAD_DIM = 64
PARTS = 2

beta_one = 0.9
beta_two = 0.999
adam_count = 10.0
learn_rate = 0.01
weight_decay = 0.1
epsilon = 1e-08
highest = lax.Precision.HIGHEST
f32 = jnp.float32
bf16 = jnp.bfloat16
MESH = pl.DeviceIdType.MESH
REVERSE_OUT, REVERSE_HOME = bf16, bf16
FORWARD_OUT, FORWARD_HOME = bf16, bf16
VMEM = pl.BlockSpec(memory_space=pltpu.VMEM)


def remote(src, dst, send_sem, recv_sem, where):
    return pltpu.make_async_remote_copy(
        src_ref=src, dst_ref=dst, send_sem=send_sem, recv_sem=recv_sem, device_id=where,
        device_id_type=MESH,
    )


def loop(low, high, body):
    lax.fori_loop(low, high, lambda i, carry: (body(i), carry)[1], 0, unroll=high - low <= 16)


class Scan:
    def __init__(self, count, me, local, decay, gathered, sent, result, sems):
        self.count, self.me = count, me
        self.local, self.decay, self.gathered, self.sent, self.result = (
            local, decay, gathered, sent, result)
        self.width = local.shape[1] // count
        self.out_send, self.out_recv, self.back_send, self.back_recv = sems

    def columns(self, place):
        return pl.ds(pl.multiple_of(place * self.width, self.width), self.width)

    def outward(self, j, source):
        return remote(self.local.at[:, self.columns(j)], self.gathered.at[source],
                      self.out_send.at[j], self.out_recv.at[source], {"seq": j})

    def homeward(self, i, owner):
        return remote(self.sent.at[i], self.result.at[:, self.columns(owner)],
                      self.back_send.at[i], self.back_recv.at[owner], {"seq": i})

    def start(self):
        loop(1, self.count,
             lambda k: self.outward(lax.rem(self.me + k, self.count), self.me).start())
        self.gathered[self.me] = self.local[:, self.columns(self.me)]

    def combine(self, reverse):
        count, me = self.count, self.me

        def one(k, running):
            i = count - 1 - k if reverse else k

            @pl.when(i != me)
            def _():
                self.outward(i, i).wait_recv()

            self.sent[i] = running.astype(bf16)
            new = self.decay[i] * running + self.gathered[i].astype(f32)

            @pl.when(i != me)
            def _():
                self.homeward(i, me).start()

            return new

        lax.fori_loop(0, count, one, jnp.zeros(self.gathered.shape[1:], f32))
        self.result[:, self.columns(me)] = self.sent[me]

    def arrive(self):
        def one(k):
            j = lax.rem(self.me + k, self.count)
            self.homeward(j, j).wait_recv()

        loop(1, self.count, one)

    def drain(self):
        def one(k):
            j = lax.rem(self.me + k, self.count)
            self.outward(j, j).wait_send()
            self.homeward(j, j).wait_send()

        loop(1, self.count, one)

    def finish(self):
        self.arrive()
        self.drain()


def greet(seq_count, dp_count, same_core):
    seq_me, dp_me = lax.axis_index("seq"), lax.axis_index("dp")
    barrier = pltpu.get_barrier_semaphore()
    loop(1, seq_count, lambda k: pl.semaphore_signal(
        barrier, inc=1, device_id={"seq": lax.rem(seq_me + k, seq_count)}, device_id_type=MESH))
    total = seq_count - 1
    places = seq_count // 2 if same_core else 1

    def over(k):
        d = lax.rem(dp_me + 1 + k // places, dp_count)
        s = lax.rem(seq_me + 2 * (k % places), seq_count)
        pl.semaphore_signal(barrier, inc=1, device_id={"seq": s, "dp": d}, device_id_type=MESH)

    loop(0, (dp_count - 1) * places, over)
    return lambda: pl.semaphore_wait(barrier, total + (dp_count - 1) * places)


def first_kernel(seq_count, dp_count, weight, local, decay, weights, decays, result,
                 gathered, sent, w_send, w_recv, p_send, p_recv, d_send, d_recv,
                 a_send, a_recv, b_send, b_recv):
    seq_me, dp_me = lax.axis_index("seq"), lax.axis_index("dp")
    core = lax.rem(seq_me, 2)
    partner = seq_me + 1 - 2 * core
    greet(seq_count, dp_count, False)()

    def across(d, source):
        return remote(weight.at[core], weights.at[source, core], w_send.at[d], w_recv.at[source],
                      {"dp": d})

    def beside(d, half):
        return remote(weights.at[d, half], weights.at[d, half], p_send.at[d], p_recv.at[d],
                      {"seq": partner})

    def tell(j, source):
        return remote(decay.at[j], decays.at[source], d_send.at[j], d_recv.at[source], {"seq": j})

    loop(1, dp_count, lambda k: across(lax.rem(dp_me + k, dp_count), dp_me).start())
    loop(1, seq_count, lambda k: tell(lax.rem(seq_me + k, seq_count), seq_me).start())
    scan = Scan(seq_count, seq_me, local, decays, gathered, sent, result,
                (a_send, a_recv, b_send, b_recv))
    scan.start()
    decays[seq_me] = decay[seq_me]
    weights[dp_me] = weight[...]

    def told(k):
        j = lax.rem(seq_me + k, seq_count)
        tell(j, j).wait_recv()

    loop(1, seq_count, told)

    def pass_on(k):
        d = lax.rem(dp_me + k, dp_count)
        across(d, d).wait_recv()
        beside(d, core).start()

    loop(1, dp_count, pass_on)
    scan.combine(True)

    def end(k):
        d = lax.rem(dp_me + k, dp_count)
        across(d, d).wait_send()
        beside(d, core).wait_send()
        beside(d, 1 - core).wait_recv()

    loop(1, dp_count, end)
    loop(1, seq_count, lambda k: tell(lax.rem(seq_me + k, seq_count), 0).wait_send())
    scan.finish()


def second_kernel(seq_count, local, decays, result, gathered, sent, a_send, a_recv, b_send, b_recv):
    greet(seq_count, 1, False)()
    scan = Scan(seq_count, lax.axis_index("seq"), local, decays, gathered, sent, result,
                (a_send, a_recv, b_send, b_recv))
    scan.start()
    scan.combine(False)
    scan.finish()


def third_kernel(seq_count, dp_count, part, total, halves, summed, pieces,
                 h_send, h_recv, s_send, s_recv, g_send, g_recv):
    seq_me, dp_me = lax.axis_index("seq"), lax.axis_index("dp")
    core = lax.rem(seq_me, 2)
    chip = seq_me // 2
    partner = seq_me + 1 - 2 * core
    group = (seq_count // 2) * dp_count
    mine = chip * dp_count + dp_me
    greet(seq_count, dp_count, True)()

    def half(g):
        return remote(part.at[1 - core, g], halves.at[g], h_send.at[g], h_recv.at[g],
                      {"seq": partner})

    def scatter(g, source):
        return remote(summed.at[g], pieces.at[source], s_send.at[g], s_recv.at[source],
                      {"seq": 2 * (g // dp_count) + core, "dp": g % dp_count})

    def share(j, source):
        return remote(total.at[seq_me], total.at[source], g_send.at[j], g_recv.at[source],
                      {"seq": j})

    loop(1, group + 1, lambda k: half(lax.rem(mine + k, group)).start())

    def pair(k):
        g = lax.rem(mine + k, group)
        half(g).wait_recv()
        summed[g] = (part[core, g].astype(f32) + halves[g].astype(f32)).astype(bf16)

        @pl.when(g != mine)
        def _():
            scatter(g, mine).start()

    loop(1, group + 1, pair)

    def collect(k, running):
        g = lax.rem(mine + group - k, group)
        scatter(g, g).wait_recv()
        return running + pieces[g].astype(f32)

    own = part[core, mine].astype(f32) + halves[mine].astype(f32)
    total[seq_me] = lax.fori_loop(1, group, collect, own).astype(bf16)
    loop(1, seq_count, lambda k: share(lax.rem(seq_me + k, seq_count), seq_me).start())

    def end(k):
        j = lax.rem(seq_me + seq_count - k, seq_count)
        share(j, j).wait_recv()
        share(j, j).wait_send()

    loop(1, group + 1, lambda k: half(lax.rem(mine + k, group)).wait_send())
    loop(1, group, lambda k: scatter(lax.rem(mine + k, group), 0).wait_send())
    loop(1, seq_count, end)


def nt(a, b):
    return lax.dot_general(a, b, (((1,), (1,)), ((), ())), preferred_element_type=f32)


def split(a):
    high = a.astype(bf16)
    return high, (a - high.astype(f32)).astype(bf16)


def exact(a, b):
    return lax.dot_general(a, b, (((1,), (1,)), ((), ())), precision=highest)


def stack_split(a, axis, parts=2):
    pieces, rest = [], a
    for _ in range(parts):
        pieces.append(rest.astype(bf16))
        rest = rest - pieces[-1].astype(f32)
    return jnp.concatenate(pieces, axis=axis)


def repeat(a, axis, parts=2):
    return jnp.concatenate([a] * parts, axis=axis)


def dot(a, b):
    return jnp.dot(a, b, preferred_element_type=f32)


class Owners:
    def __init__(self, chips, chip, mid=True):
        self.count = chips // 2 if mid and chips % 4 == 0 else chips
        self.base = (chips - self.count) // 2
        self.me = chip - self.base
        self.is_me = (self.me >= 0) & (self.me < self.count)

    def chip(self, o):
        return self.base + o


class ChipScan:
    def __init__(self, count, chip, core, owners, reverse, local, decays, gathered, sent, result,
                 sems):
        self.count, self.chip, self.core, self.owners, self.reverse = (
            count, chip, core, owners, reverse)
        self.local, self.decays, self.gathered, self.sent, self.result = (
            local, decays, gathered, sent, result)
        self.width = local.shape[2]
        self.out_send, self.out_recv, self.back_send, self.back_recv = sems
        self.head, self.tail = (count - 1, 0) if reverse else (0, count - 1)

    def columns(self, o):
        return pl.ds(pl.multiple_of(o * self.width, self.width), self.width)

    def outward(self, o, source):
        return remote(self.local.at[o], self.gathered.at[source], self.out_send.at[o],
                      self.out_recv.at[source], {"seq": 2 * self.owners.chip(o) + self.core})

    def homeward(self, i, o):
        return remote(self.sent.at[i], self.result.at[:, self.columns(o)],
                      self.back_send.at[i], self.back_recv.at[o], {"seq": 2 * i + self.core})

    def to_owners(self, body):
        def one(k):
            o = lax.rem(self.chip + k, self.owners.count)

            @pl.when(o != self.owners.me)
            def _():
                body(o)

        loop(0, self.owners.count, one)

    def others(self, body):
        loop(1, self.count, lambda k: body(lax.rem(self.chip + k, self.count)))

    def start(self, total):
        for o in range(self.owners.count):
            self.local[o] = total[:, o * self.width : (o + 1) * self.width].astype(self.local.dtype)

        @pl.when(self.chip != self.tail)
        def _():
            self.to_owners(lambda o: self.outward(o, self.chip).start())

        @pl.when(self.owners.is_me)
        def _():
            self.gathered[self.chip] = self.local[self.owners.me]

    def combine(self, visit):
        def one(k, running):
            i = self.count - 1 - k if self.reverse else k

            @pl.when((i != self.chip) & (i != self.tail))
            def _():
                self.outward(0, i).wait_recv()

            self.sent[i] = running.astype(self.sent.dtype)

            @pl.when((i != self.chip) & (i != self.head))
            def _():
                self.homeward(i, self.owners.me).start()

            visit(i, running)
            if k == self.count - 1:
                return running
            return self.decays[i] * running + self.gathered[i].astype(f32)

        @pl.when(self.owners.is_me)
        def _():
            running = jnp.zeros(self.gathered.shape[1:], f32)
            for k in range(self.count):
                running = one(k, running)
            self.result[:, self.columns(self.owners.me)] = self.sent[self.chip]

    def arrive(self):
        @pl.when(self.chip != self.head)
        def _():
            self.to_owners(lambda o: self.homeward(self.chip, o).wait_recv())

        @pl.when(self.chip == self.head)
        def _():
            self.result[...] = jnp.zeros_like(self.result)

    def drain(self):
        @pl.when(self.chip != self.tail)
        def _():
            self.to_owners(lambda o: self.outward(o, 0).wait_send())

        def one(j):
            @pl.when(j != self.head)
            def _():
                self.homeward(j, 0).wait_send()

        @pl.when(self.owners.is_me)
        def _():
            self.others(one)


def one_kernel(seq_count, dp_count, weight_hbm, log_decay_hbm, scan_hbm, back_hbm, read_hbm,
               input_hbm, first_hbm, second_hbm, decay_grad, total, weight_out, first_out, second_out,
               log_decay, scan_rows, back_rows, read_rows, weight_rows, inputs,
               mine, pair, front_mine, front, scaled_scan, scaled_mine, scaled_got,
               kernel_mat, row_sums, col_sums, weights, write_mine, write_got,
               decay_out, decays, reverse_out, reverse_got, reverse_sent, reverse_home,
               forward_out, forward_got, forward_sent, forward_home,
               after, grad_after, prior, state_before, grad_mine, grad_got,
               part, pieces, kept, meet_out, meet_home,
               load_sem, input_sem, pass_sem, l_send, l_recv, w_send, w_recv, d_send, d_recv,
               a_send, a_recv, b_send, b_recv, e_send, e_recv, f_send, f_recv,
               t_send, t_recv, m_send, m_recv, s_send, s_recv, g_send, g_recv, q_send, q_recv):
    seq_me, dp_me = lax.axis_index("seq"), lax.axis_index("dp")
    core = lax.rem(seq_me, 2)
    other = 1 - core
    chip = seq_me // 2
    chips = seq_count // 2
    partner = {"seq": seq_me + 1 - 2 * core}
    group = chips * dp_count
    own = chip * dp_count + dp_me

    owners = Owners(chips, chip, False)
    keep = Owners(chips, chip, True)
    held = keep.count * dp_count
    own_held = keep.me * dp_count + dp_me

    def place(g):
        return {"seq": 2 * (g // dp_count) + core, "dp": lax.rem(g, dp_count)}

    barrier = pltpu.get_barrier_semaphore()
    pl.semaphore_signal(barrier, inc=1, device_id=partner, device_id_type=MESH)
    loop(1, group, lambda k: pl.semaphore_signal(
        barrier, inc=1, device_id=place(lax.rem(own + k, group)), device_id_type=MESH))

    length, channels = scan_rows.shape
    half = channels // 2
    heads = channels // HEAD_DIM
    half_heads = heads // 2
    state_size = read_rows.shape[0]
    own_rows = weight_hbm.shape[1]
    side = own_rows // 2
    width = half // owners.count
    wide = side // keep.count

    def span(start, size):
        return pl.ds(pl.multiple_of(start, 128), size)

    loads = [
        pltpu.make_async_copy(log_decay_hbm, log_decay, load_sem.at[0]),
        pltpu.make_async_copy(back_hbm, back_rows, load_sem.at[1]),
        pltpu.make_async_copy(read_hbm, read_rows, load_sem.at[2]),
        pltpu.make_async_copy(weight_hbm.at[:, span(core * side, side)], weight_rows,
                              load_sem.at[3]),
        pltpu.make_async_copy(scan_hbm, scan_rows, load_sem.at[4]),
    ]
    for copy in loads:
        copy.start()
    my_rows = pl.ds(pl.multiple_of(core * length, length), length)

    def input_load(d):
        return pltpu.make_async_copy(
            input_hbm.at[:, span(d * own_rows + core * side, side)],
            inputs.at[my_rows, d * side : (d + 1) * side], input_sem.at[d])

    for d in range(dp_count):
        input_load(d).start()

    passed = [
        pltpu.make_async_copy(src, dst, pass_sem.at[i])
        for i, (src, dst) in enumerate(
            ((weight_hbm, weight_out), (first_hbm, first_out), (second_hbm, second_out)))
    ]
    row_index = lax.broadcasted_iota(jnp.int32, (length, length), 0)
    col_index = lax.broadcasted_iota(jnp.int32, (length, length), 1)
    causal = row_index <= col_index
    upto = repeat((col_index <= row_index).astype(f32).astype(bf16), 1, 3)
    owner = lax.broadcasted_iota(jnp.int32, (heads, channels), 0)
    spot = lax.broadcasted_iota(jnp.int32, (heads, channels), 1) - owner * HEAD_DIM
    member = ((spot >= 0) & (spot < HEAD_DIM)).astype(bf16)
    half_member = member[:half_heads, :half]
    member = repeat(member, 0)

    def widen(a):
        return dot(stack_split(a, 1), member)

    def per_head(a):
        high, low = split(a)
        return nt(half_member, high) + nt(half_member, low)

    loads[0].wait()
    decay_parts = stack_split(log_decay[...], 1, 3)
    run_cols = nt(upto, decay_parts)
    overall = run_cols[length - 1 :, :]
    from_wide = widen(jnp.exp(run_cols))
    decay_wide = from_wide[length - 1 :, :]
    loads[1].wait()
    loads[2].wait()
    read_twice = repeat(read_rows[...], 1)
    for h in range(2):
        at = slice(h * half, (h + 1) * half)
        scaled = back_rows[:, at].astype(f32) * from_wide[:, at]
        mine[h, :state_size] = dot(read_twice, stack_split(scaled, 0))
        mine[h, state_size:] = jnp.broadcast_to(decay_wide[:, at], (8, half))
    loads[3].wait()
    weights[dp_me] = weight_rows[...].astype(bf16)

    def to_partner(src, dst, place):
        return remote(src, dst, m_send.at[place], m_recv.at[place], partner)

    def across(d, source):
        return remote(weights.at[dp_me], weights.at[source], w_send.at[d], w_recv.at[source],
                      {"dp": d})

    def lend(d, rows):
        return remote(input_hbm.at[:, span(d * own_rows + other * side, side)],
                      inputs.at[rows, d * side : (d + 1) * side],
                      l_send.at[d], l_recv.at[d], partner)

    def tell(o, source):
        return remote(decay_out.at[o], decays.at[source], d_send.at[o], d_recv.at[source],
                      {"seq": 2 * owners.chip(o) + core})

    parts = part.shape[0]
    rows = state_size // parts

    def scatter(g, source, n):
        return remote(part.at[n, g], pieces.at[n, source], s_send.at[n, g], s_recv.at[n, source],
                      place(keep.base * dp_count + g))

    def columns(side_of, o):
        return span(side_of * side + o * wide, wide)

    def meeting(i, o):
        return remote(meet_out.at[i], meet_home.at[o], t_send.at[i], t_recv.at[o],
                      {"seq": 2 * i + core})

    def share(j, o, n):
        spot = total.at[n * rows : (n + 1) * rows, columns(core, o)]
        return remote(spot, spot, g_send.at[n, j], g_recv.at[n, o], {"seq": 2 * j + core})

    def hand(o, from_core, n):
        spot = total.at[n * rows : (n + 1) * rows, columns(from_core, o)]
        return remote(spot, spot, q_send.at[n, o], q_recv.at[n, o], partner)

    reverse = ChipScan(chips, chip, core, owners, True, reverse_out, decays, reverse_got,
                       reverse_sent, reverse_home, (a_send, a_recv, b_send, b_recv))
    forward = ChipScan(chips, chip, core, owners, False, forward_out, decays, forward_got,
                       forward_sent, forward_home, (e_send, e_recv, f_send, f_recv))

    def to_keepers(body):
        def one(k):
            o = lax.rem(chip + k, keep.count)

            @pl.when(o != keep.me)
            def _():
                body(o)

        loop(0, keep.count, one)

    def to_holders(body):
        def one(k):
            g = lax.rem(own + k, held)

            @pl.when(g != own_held)
            def _():
                body(g)

        loop(0, held, one)

    pl.semaphore_wait(barrier, group)
    states_over = to_partner(mine.at[other], pair.at[core], 0)
    states_over.start()
    loop(1, dp_count, lambda k: across(lax.rem(dp_me + k, dp_count), dp_me).start())
    pair[core] = mine[core]
    run_rows = nt(decay_parts, upto)
    loads[4].wait()
    to_wide = widen(jnp.exp(overall - run_cols))
    for h in range(2):
        at = slice(h * half, (h + 1) * half)
        scaled = scan_rows[:, at].astype(f32) * to_wide[:, at]
        scaled_scan[h] = scaled
        scaled_mine[h] = scaled.astype(bf16)
    scaled_over = to_partner(scaled_mine.at[other], scaled_got, 1)
    states_over.wait_recv()
    first_decay = pair[0, state_size : state_size + 1]
    last_decay = pair[1, state_size : state_size + 1]
    chip_decay = first_decay * last_decay
    for o in range(owners.count):
        decay_out[o] = chip_decay[:, o * width : (o + 1) * width]
    reverse.to_owners(lambda o: tell(o, chip).start())
    reverse.start(pair[0, :state_size] + first_decay * pair[1, :state_size])
    for d in range(dp_count):
        lend(d, my_rows).start()

    @pl.when(owners.is_me)
    def _():
        decays[chip] = decay_out[owners.me]

    scaled_over.start()
    for copy in passed:
        copy.start()
    kernel_sum = jnp.zeros((length, length), f32)

    def kernels(low, high, kernel_sum):
        for h in range(low, high):
            at = slice(h * HEAD_DIM, (h + 1) * HEAD_DIM)
            crossed = nt(scan_rows[:, at], back_rows[:, at])
            spread = run_rows[h : h + 1, :] - run_cols[:, h : h + 1]
            term = jnp.where(causal, jnp.exp(jnp.minimum(spread, 0.0)), 0.0) * crossed
            kernel_mat[h] = term
            kernel_sum += term
        return kernel_sum

    kernel_sum = kernels(0, heads * 3 // 8, kernel_sum)
    for d in range(dp_count):
        input_load(d).wait()
        lend(d, my_rows).wait_recv()
    loop(1, dp_count, lambda k: across(0, lax.rem(dp_me + k, dp_count)).wait_recv())
    some = nt(weights[0], inputs[:, :side])
    for d in range(1, dp_count):
        some += nt(weights[d], inputs[:, d * side : (d + 1) * side])
    for t in range(2):
        write_mine[t] = some[:, t * length : (t + 1) * length]
    write_over = to_partner(write_mine.at[other], write_got, 2)
    write_over.start()

    @pl.when(owners.is_me)
    def _():
        reverse.others(lambda j: tell(0, j).wait_recv())


    def keep_after(i, running):
        kept[i] = running

    reverse.combine(keep_after)
    kernel_sum = kernels(heads * 3 // 8, heads * 5 // 8, kernel_sum)
    write_over.wait_recv()
    write = write_mine[core] + write_got[...]
    write_rows = write.T.astype(bf16)
    write = repeat(write.astype(bf16), 1)
    for h in range(2):
        front_mine[h] = dot(write, stack_split(scaled_scan[h], 0))
    front_over = to_partner(front_mine.at[other], front.at[core], 3)
    front_over.start()
    front[core] = front_mine[core]
    front_over.wait_recv()
    forward.start(last_decay * front[0] + front[1])
    kernel_sum = kernels(heads * 5 // 8, heads, kernel_sum)
    inner = dot(read_twice, stack_split(kernel_sum.T, 0))
    scaled_over.wait_recv()
    reverse.arrive()
    after[1] = reverse_home[...].astype(f32)
    after[0] = pair[1, :state_size] + last_decay * reverse_home[...].astype(f32)
    grad_mine[core] = nt(after[core].astype(bf16), scaled_mine[core]) + inner
    grad_mine[other] = nt(after[other].astype(bf16), scaled_got[...])
    grad_over = to_partner(grad_mine, grad_got, 4)
    grad_over.start()
    after_over = to_partner(after.at[other], grad_after.at[core], 5)
    grad_over.wait_recv()
    grad_half = (grad_mine[...] + grad_got[...]).astype(bf16)
    grad_half = jnp.concatenate([grad_half[0], grad_half[1]], axis=1)
    for k in range(held):
        g = lax.rem(own + k, held)
        low = lax.rem(g, dp_count) * side + g // dp_count * wide
        term = dot(grad_half, inputs[:, span(low, wide)]).astype(bf16)
        for n in range(parts):
            part[n, g] = term[n * rows : (n + 1) * rows]

        @pl.when(g != own_held)
        def _():
            scatter(g, own, 0).start()

    for n in range(1, parts):
        to_holders(lambda g: scatter(g, own, n).start())
    after_over.start()
    grad_after[core] = after[core]
    def meet(i, running):
        meet_out[i] = jnp.sum(kept[i] * running, axis=0, keepdims=True)

        @pl.when(i != chip)
        def _():
            meeting(i, owners.me).start()

    forward.combine(meet)

    @pl.when(owners.is_me)
    def _():
        meet_home[owners.me] = meet_out[chip]

    read_turned = read_rows[...].astype(f32).T.astype(bf16)
    write_read = jnp.where(row_index < col_index, nt(write_rows, read_turned), 0.0)
    for h in range(heads):
        pairing = kernel_mat[h] * write_read
        row_sums[:, h : h + 1] = jnp.sum(pairing, axis=1, keepdims=True)
        col_sums[h : h + 1, :] = jnp.sum(pairing, axis=0, keepdims=True)
    after_over.wait_recv()
    second = []
    for h in range(2):
        grad_write = dot(repeat(write_rows, 1), stack_split(grad_after[h], 0))
        second.append(per_head(scan_rows[:, h * half : (h + 1) * half].astype(f32) * grad_write))
    overall_rows = run_rows[:, length - 1 :]
    before = repeat((col_index < row_index).astype(f32).astype(bf16), 1, 3)
    onward = repeat(causal.astype(f32).astype(bf16), 1, 3)
    second = (jnp.exp(overall_rows - run_rows) * jnp.concatenate(second, axis=0)
              + row_sums[...].T - col_sums[...])

    @pl.when(keep.is_me)
    def _():
        for n in range(parts):
            def collect(k, running):
                g = lax.rem(own + group - k, group)
                scatter(0, g, n).wait_recv()
                return running + pieces[n, g].astype(f32)

            total[n * rows : (n + 1) * rows, columns(core, keep.me)] = lax.fori_loop(
                1, group, collect, part[n, own_held].astype(f32),
                unroll=True).astype(bf16)
            reverse.others(lambda j: share(j, keep.me, n).start())
            hand(keep.me, core, n).start()

    forward.arrive()
    reverse.to_owners(lambda o: meeting(chip, o).wait_recv())
    met = jnp.concatenate([meet_home[o] for o in range(owners.count)], axis=1)
    came = forward_home[...].astype(f32)
    both = (last_decay * met + jnp.sum(pair[1, :state_size] * came, axis=0, keepdims=True),
            first_decay * met + jnp.sum(after[1] * front[0], axis=0, keepdims=True))
    prior[0, :state_size] = came
    prior[1, :state_size] = front[0] + first_decay * came
    for t in range(2):
        prior[t, state_size:] = jnp.broadcast_to(both[t], (8, half))
    prior_over = to_partner(prior.at[other], state_before.at[core], 6)
    prior_over.start()
    state_before[core] = prior[core]
    prior_over.wait_recv()
    third, first = [], []
    for h in range(2):
        at = slice(h * half, (h + 1) * half)
        state_read = dot(repeat(read_turned, 1), stack_split(state_before[h, :state_size], 0))
        third.append(per_head(back_rows[:, at].astype(f32) * state_read))
        first.append(per_head(state_before[h, state_size:])[:, :1])
    decay_grad[...] = (
        jnp.exp(overall_rows) * jnp.concatenate(first, axis=0)
        + nt(stack_split(second, 1, 3), before)
        + nt(stack_split(jnp.exp(run_rows) * jnp.concatenate(third, axis=0), 1, 3), onward)
    )

    for copy in passed:
        copy.wait()
    loop(1, dp_count, lambda k: across(lax.rem(dp_me + k, dp_count), 0).wait_send())
    for d in range(dp_count):
        lend(d, my_rows).wait_send()
    for copy in (states_over, scaled_over, write_over, front_over, grad_over, after_over, prior_over):
        copy.wait_send()
    reverse.drain()
    forward.drain()

    @pl.when(owners.is_me)
    def _():
        reverse.others(lambda j: meeting(j, 0).wait_send())

    reverse.to_owners(lambda o: tell(o, 0).wait_send())
    for n in range(parts):
        to_holders(lambda g: scatter(g, 0, n).wait_send())
    for n in range(parts):
        def pass_on(o):
            share(chip, o, n).wait_recv()
            hand(o, core, n).start()

        to_keepers(pass_on)
    for n in range(parts):
        loop(0, keep.count, lambda o: hand(o, other, n).wait_recv())

    for n in range(parts):
        @pl.when(keep.is_me)
        def _():
            reverse.others(lambda j: share(j, 0, n).wait_send())

        loop(0, keep.count, lambda o: hand(o, core, n).wait_send())


def dma(*sizes):
    shapes = [size if isinstance(size, tuple) else (size,) for size in sizes]
    return [pltpu.SemaphoreType.DMA(shape) for shape in shapes for _ in range(2)]


def adam_update(grad_rows, weight_rows, first_rows, second_rows):
    new_first = beta_one * first_rows + (1.0 - beta_one) * grad_rows
    new_second = beta_two * second_rows + (1.0 - beta_two) * grad_rows * grad_rows
    first_hat = new_first / (1.0 - beta_one**adam_count)
    second_hat = new_second / (1.0 - beta_two**adam_count)
    new_weight = weight_rows - learn_rate * (
        first_hat / (jnp.sqrt(second_hat) + epsilon) + weight_decay * weight_rows
    )
    return (new_weight, new_first, new_second)


def update_kernel(steps, decay, grad, weight, first, second, decay_out, weight_out, first_out,
                  second_out, new_weight, new_first, new_second, out_sem, decay_sem):
    decay_copy = pltpu.make_async_copy(decay, decay_out, decay_sem)
    decay_copy.start()
    size = grad.shape[1] // steps
    copies = []
    for step in range(steps):
        at = slice(step * size, (step + 1) * size)
        results = adam_update(grad[:, at].astype(f32), weight[:, at], first[:, at], second[:, at])
        for i, (value, held, out) in enumerate(zip(
                results, (new_weight, new_first, new_second),
                (weight_out, first_out, second_out))):
            held[:, at] = value
            copies.append(pltpu.make_async_copy(held.at[:, at], out.at[:, at], out_sem.at[i, step]))
            copies[-1].start()
    decay_copy.wait()
    for copy in copies:
        copy.wait()


def on_device(
    layer_input,
    scan_input,
    readout,
    log_decay,
    output_cotangent,
    write_weight,
    first_moment,
    second_moment,
):
    seq_count, dp_count = lax.axis_size("seq"), lax.axis_size("dp")
    input_rows = layer_input[0]
    scan_rows = scan_input[0]
    read_rows = readout[0]
    decay_rows = log_decay[0]
    back_rows = output_cotangent[0]
    length, model = input_rows.shape
    heads = decay_rows.shape[1]
    channels = scan_rows.shape[1]
    state_size = read_rows.shape[1]
    own_rows = write_weight.shape[0]
    width = channels // seq_count

    chips = seq_count // 2
    group = chips * dp_count
    fast = own_rows % (128 * seq_count) == 0 and channels % (128 * seq_count) == 0
    if fast:
        half = channels // 2
        owners = Owners(chips, 0, False).count
        keep = Owners(chips, 0, True).count
        held = keep * dp_count
        lanes = half // owners
        parts = PARTS if state_size % (16 * PARTS) == 0 else 1
        piece = (state_size // parts, own_rows // 2 // keep)
        results = pl.pallas_call(
            functools.partial(one_kernel, seq_count, dp_count),
            out_shape=(
                pltpu.VMEM((heads, length), f32),
                pltpu.VMEM((state_size, own_rows), bf16),
            ) + (pltpu.VMEM((state_size, own_rows), f32),) * 3,
            in_specs=[pl.BlockSpec(memory_space=pltpu.HBM)] * 8,
            out_specs=[VMEM] * 5,
            scratch_shapes=[
                pltpu.VMEM((heads, length), f32),
                pltpu.VMEM((length, channels), bf16),
                pltpu.VMEM((length, channels), bf16),
                pltpu.VMEM((state_size, length), bf16),
                pltpu.VMEM((state_size, own_rows // 2), f32),
                pltpu.VMEM((2 * length, model // 2), bf16),
                pltpu.VMEM((2, state_size + 8, half), f32),
                pltpu.VMEM((2, state_size + 8, half), f32),
                pltpu.VMEM((2, state_size, half), f32),
                pltpu.VMEM((2, state_size, half), f32),
                pltpu.VMEM((2, length, half), f32),
                pltpu.VMEM((2, length, half), bf16),
                pltpu.VMEM((length, half), bf16),
                pltpu.VMEM((heads, length, length), f32),
                pltpu.VMEM((length, heads), f32),
                pltpu.VMEM((heads, length), f32),
                pltpu.VMEM((dp_count, state_size, own_rows // 2), bf16),
                pltpu.VMEM((2, state_size, length), f32),
                pltpu.VMEM((state_size, length), f32),
                pltpu.VMEM((owners, 1, lanes), f32),
                pltpu.VMEM((chips, 1, lanes), f32),
            ]
            + [pltpu.VMEM(shape, kind)
               for out_kind, home_kind in ((REVERSE_OUT, REVERSE_HOME), (FORWARD_OUT, FORWARD_HOME))
               for shape, kind in (
                   ((owners, state_size, lanes), out_kind), ((chips, state_size, lanes), out_kind),
                   ((chips, state_size, lanes), home_kind), ((state_size, half), home_kind))]
            + [pltpu.VMEM((2, state_size, half), f32)] * 2
            + [pltpu.VMEM((2, state_size + 8, half), f32)] * 2
            + [pltpu.VMEM((2, state_size, length), f32)] * 2
            + [pltpu.VMEM((parts, held) + piece, bf16), pltpu.VMEM((parts, group) + piece, bf16),
               pltpu.VMEM((chips, state_size, lanes), f32), pltpu.VMEM((chips, 1, lanes), f32),
               pltpu.VMEM((owners, 1, lanes), f32)]
            + [pltpu.SemaphoreType.DMA((5,)), pltpu.SemaphoreType.DMA((dp_count,)),
               pltpu.SemaphoreType.DMA((3,))]
            + dma(dp_count, dp_count, chips, chips, chips, chips, chips, chips, 7, (parts, group), (parts, chips), (parts, keep)),
            compiler_params=pltpu.CompilerParams(collective_id=3, has_side_effects=True,
                                                 vmem_limit_bytes=60000000),
            name="whole_step",
        )(write_weight.T, decay_rows.T, scan_rows, back_rows, read_rows.T, input_rows,
          first_moment.T, second_moment.T)
        steps = 4
        decay_grad, new_weight, new_first, new_second = pl.pallas_call(
            functools.partial(update_kernel, steps),
            out_shape=(jax.ShapeDtypeStruct((heads, length), f32),)
            + (jax.ShapeDtypeStruct((state_size, own_rows), f32),) * 3,
            in_specs=[VMEM] * 5,
            out_specs=[pl.BlockSpec(memory_space=pltpu.HBM)] * 4,
            scratch_shapes=[pltpu.VMEM((state_size, own_rows), f32)] * 3
            + [pltpu.SemaphoreType.DMA((3, steps)), pltpu.SemaphoreType.DMA],
            compiler_params=pltpu.CompilerParams(vmem_limit_bytes=16 * 2**20),
            name="update",
        )(*results)
        return decay_grad.T[None], new_weight.T, new_first.T, new_second.T
    else:
        row_index = lax.broadcasted_iota(jnp.int32, (length, length), 0)
        col_index = lax.broadcasted_iota(jnp.int32, (length, length), 1)
        upto = (col_index <= row_index).astype(f32)
        before = (col_index < row_index).astype(f32)
        running = jnp.dot(upto, decay_rows, precision=highest)
        overall = running[-1]
        to_end = jnp.exp(overall[None, :] - running)
        from_start = jnp.exp(running)
        decay_total = jnp.exp(overall)

        def widen(a):
            return jnp.repeat(a, HEAD_DIM, axis=1)

        scaled_scan = scan_rows.astype(f32) * widen(to_end)
        scaled_back = back_rows.astype(f32) * widen(from_start)

        def state_of(vectors, rows):
            return lax.dot_general(
                vectors.astype(f32), rows, (((0,), (0,)), ((), ())), precision=highest
            ).astype(bf16)

        reverse_local = state_of(read_rows, scaled_back)
        decay_lanes = widen(decay_total[None]).reshape(seq_count, 1, width)
        weight_half = write_weight.T.astype(bf16).reshape(2, state_size // 2, own_rows)
        exchange = [
            pltpu.VMEM((seq_count, state_size, width), bf16),
            pltpu.VMEM((seq_count, state_size, width), bf16),
        ]
        piece = (state_size * own_rows // seq_count // 128, 128)
        scan_split = scan_rows.reshape(length, heads, HEAD_DIM)
        back_split = back_rows.reshape(length, heads, HEAD_DIM)
        crossed = jnp.einsum("thp,shp->hts", scan_split, back_split, preferred_element_type=f32)
        heads_running = running.T
        spread = heads_running[:, None, :] - heads_running[:, :, None]
        kernel_mat = (
            jnp.where((row_index <= col_index)[None], jnp.exp(jnp.minimum(spread, 0.0)), 0.0) * crossed
        )
        weights, decays, grad_after = pl.pallas_call(
            functools.partial(first_kernel, seq_count, dp_count),
            out_shape=(
                jax.ShapeDtypeStruct((dp_count,) + weight_half.shape, bf16),
                jax.ShapeDtypeStruct(decay_lanes.shape, f32),
                jax.ShapeDtypeStruct((state_size, channels), bf16),
            ),
            in_specs=[VMEM] * 3,
            out_specs=[VMEM] * 3,
            scratch_shapes=exchange + dma(dp_count, dp_count, seq_count, seq_count, seq_count),
            compiler_params=pltpu.CompilerParams(collective_id=0, has_side_effects=True),
            name="gather_reverse",
        )(weight_half, reverse_local, decay_lanes)

        weight_all = weights.reshape(dp_count, state_size, own_rows).transpose(1, 0, 2)
        write_half = lax.dot_general(
            input_rows, weight_all.reshape(state_size, model), (((1,), (1,)), ((), ())),
            preferred_element_type=f32,
        ).astype(bf16)
        state_local = state_of(write_half, scaled_scan)
        state_before = pl.pallas_call(
            functools.partial(second_kernel, seq_count),
            out_shape=jax.ShapeDtypeStruct((state_size, channels), bf16),
            in_specs=[VMEM] * 2,
            out_specs=VMEM,
            scratch_shapes=exchange + dma(seq_count, seq_count),
            compiler_params=pltpu.CompilerParams(collective_id=1, has_side_effects=True),
            name="forward_states",
        )(state_local, decays)

        kernel_sum = jnp.sum(kernel_mat, axis=0)
        write_grad = jnp.dot(kernel_sum, read_rows.astype(f32), precision=highest)
        write_grad = write_grad + lax.dot_general(
            scaled_scan.astype(bf16), grad_after, (((1,), (1,)), ((), ())), preferred_element_type=f32
        )
        grad_half = write_grad.astype(bf16)
        partial = lax.dot_general(
            grad_half, input_rows, (((0,), (0,)), ((), ())), preferred_element_type=f32
        ).astype(bf16)
        part = partial.reshape(state_size, dp_count, chips, 2, own_rows // seq_count)
        part = part.transpose(3, 2, 1, 0, 4).reshape((2, chips * dp_count) + piece)
        grad_sum = pl.pallas_call(
            functools.partial(third_kernel, seq_count, dp_count),
            out_shape=jax.ShapeDtypeStruct((seq_count,) + piece, bf16),
            in_specs=[VMEM],
            out_specs=VMEM,
            scratch_shapes=[pltpu.VMEM((chips * dp_count,) + piece, bf16)] * 3
            + dma(chips * dp_count, chips * dp_count, seq_count),
            compiler_params=pltpu.CompilerParams(collective_id=2, has_side_effects=True),
            name="reduce_gradient",
        )(part)
        def per_head(a):
            return jnp.sum(a.reshape(a.shape[0], heads, HEAD_DIM), axis=2)

        term_one = decay_total * jnp.sum(
            per_head(grad_after.astype(f32) * state_before.astype(f32)), axis=0)
        grad_write = jnp.dot(write_half, grad_after, preferred_element_type=f32)
        second_rows = to_end * per_head(scan_rows.astype(f32) * grad_write)
        term_two = jnp.dot(before, second_rows, precision=highest)
        state_read = jnp.dot(read_rows, state_before, preferred_element_type=f32)
        third_rows = from_start * per_head(back_rows.astype(f32) * state_read)
        term_three = jnp.dot(upto.T, third_rows, precision=highest)
        write_read = jnp.dot(write_half, read_rows.T, preferred_element_type=f32)
        pairing = jnp.where((row_index < col_index)[None], kernel_mat * write_read[None], 0.0)
        balance = (jnp.sum(pairing, axis=2) - jnp.sum(pairing, axis=1)).T
        term_four = jnp.dot(before, balance, precision=highest)
        decay_grad = term_one[None, :] + term_two + term_three + term_four
        grad_rows = grad_sum.reshape(seq_count, state_size, own_rows // seq_count)
        grad_rows = grad_rows.transpose(1, 0, 2).reshape(state_size, own_rows).astype(f32).T
    new_weight, new_first, new_second = adam_update(
        grad_rows, write_weight, first_moment, second_moment
    )

    return (decay_grad[None], new_weight, new_first, new_second)


def solution(mesh):
    in_specs = (
        P("dp", "seq", None),
        P("dp", "seq", None),
        P("dp", "seq", None),
        P("dp", "seq", None),
        P("dp", "seq", None),
        P("dp", None),
        P("dp", None),
        P("dp", None),
    )
    out_specs = (P("dp", "seq", None), P("dp", None), P("dp", None), P("dp", None))
    return jax.shard_map(
        on_device, mesh=mesh, in_specs=in_specs, out_specs=out_specs, check_vma=False
    )
```
